512 devices in a mesh: blk: 32 (over y, x, core), int: 16 (over z).
Axes of the slice: x: 4, y: 4, z: 16, core: 2. Of those that a mesh axis runs over, the one named last changes fastest.
Arguments:
- amplitudes: float32 [4, 608, 64, 608], P(None, 'blk', 'int'), may hold values from -6 to 6
- integrals: float32 [64, 608, 4, 608], P('int', None, None, 'blk'), may hold values from -0.078125 to 0.078125
- occ_irrep: int32 [64], replicated, may hold values from 0 to 7
- virt_irrep: int32 [608], replicated, may hold values from 0 to 7, as said below
- i_batch: int32 [4], replicated, may hold values from 0 to 63
- j_batch: int32 [4], replicated, may hold values from 0 to 63
Outputs:
- residual: float32 [4, 608, 4, 608], P(None, 'blk', None, 'int')
The draws below stay inside these ranges and needn't reach their ends.
Inputs may be any that keep to these rules, and one draw needn't show every extreme that they name: `occ_irrep`: labels of the eight D2h irreps; the product of two irreps is the bitwise exclusive or of their labels. `virt_irrep`: labels of the eight D2h irreps, combined as above; no irrep labels more than 96 virtual orbitals, and one labels exactly 96. `i_batch`: positions among the 64 occupied orbitals. `j_batch`: positions among the 64 occupied orbitals.
All inputs are finite; a program needn't handle non-finite values.
Results may differ from the reference program's by a relative error of at most 0.00007.
Values sent between devices are 32-bit elements; how exact they have to be, the bound alone decides.
A program may use at most 128 MiB of HBM per device.

```python
import jax
import jax.numpy as jnp
from jax import lax

I = 4
J = 4
O = 64
V = 608
VCAP = 96


def draw_virt_irrep(key, part):
    first_key, order_key = jax.random.split(jax.random.fold_in(key, 7))
    first = jax.random.randint(first_key, (), 0, 8).astype(jnp.int32)
    positions = jnp.arange(V, dtype=jnp.int32)
    rest = jnp.mod(positions - VCAP, 7).astype(jnp.int32)
    other = rest + (rest >= first).astype(jnp.int32)
    labels = jnp.where(positions < VCAP, first, other).astype(jnp.int32)
    order = jax.random.permutation(order_key, V)
    return labels[order].astype(jnp.int32)


def place_ends(array, rng, low, largest):
    place = [jax.random.randint(jax.random.fold_in(rng, axis), (), 0, length) for axis, length in enumerate(array.shape)]
    main_axis = array.shape.index(max(array.shape))
    neighbour = place[:main_axis] + [(place[main_axis] + 1) % array.shape[main_axis]] + place[main_axis + 1:]
    return array.at[tuple(place)].set(low).at[tuple(neighbour)].set(largest)


def block_scale(stream_key, extent, cuts, smallest, high):
    level = 1.0
    for dim, blocks in cuts:
        draws = jax.random.uniform(jax.random.fold_in(jax.random.fold_in(stream_key, 6), dim), (blocks,), jnp.float32, smallest / len(cuts), high / len(cuts))
        level = level * jnp.repeat(jnp.exp(draws), extent[dim] // blocks).reshape((-1,) + (1,) * (len(extent) - 1 - dim))
    return level


def normal_values(rng, dims, width, bound, cuts=(), held_as=jnp.bfloat16):
    entries = width * jax.random.normal(rng, dims, jnp.float32)
    if cuts:
        entries = entries * block_scale(rng, dims, cuts, -0.22, 0.18)
    return jnp.clip(entries, -bound, bound).astype(held_as)


def setup_inputs(seed: int = 0) -> dict:
    key_list = jax.random.split(jax.random.key(seed), 7)
    amplitudes = normal_values(key_list[0], (I, V, O, V), 1.0, 6.0, ((1, 32), (2, 16)), jnp.float32)
    integrals = normal_values(key_list[1], (O, V, J, V), (O * V // 8) ** -0.5, 0.078125, ((0, 16), (3, 32)), jnp.float32)
    occ_irrep = place_ends(jax.random.randint(key_list[2], (O,), 0, 8), jax.random.fold_in(key_list[2], 1), 0, 7).astype(jnp.int32)
    virt_irrep = draw_virt_irrep(jax.random.fold_in(key_list[6], 71), 0)
    i_batch = place_ends(jax.random.randint(key_list[4], (I,), 0, O), jax.random.fold_in(key_list[4], 1), 0, O - 1).astype(jnp.int32)
    j_batch = place_ends(jax.random.randint(key_list[5], (J,), 0, O), jax.random.fold_in(key_list[5], 1), 0, O - 1).astype(jnp.int32)
    return {"amplitudes": amplitudes, "integrals": integrals, "occ_irrep": occ_irrep, "virt_irrep": virt_irrep, "i_batch": i_batch, "j_batch": j_batch}


def reference(amplitudes, integrals, occ_irrep, virt_irrep, i_batch, j_batch):
    irr_i = occ_irrep[i_batch]
    irr_j = occ_irrep[j_batch]
    amp_keep = jnp.bitwise_xor(irr_i[:, None, None, None], occ_irrep[None, None, :, None]) == jnp.bitwise_xor(virt_irrep[None, :, None, None], virt_irrep[None, None, None, :])
    sym_amp = jnp.where(amp_keep, amplitudes, jnp.zeros_like(amplitudes))
    int_keep = jnp.bitwise_xor(occ_irrep[:, None, None, None], virt_irrep[None, :, None, None]) == jnp.bitwise_xor(irr_j[None, None, :, None], virt_irrep[None, None, None, :])
    sym_int = jnp.where(int_keep, integrals, jnp.zeros_like(integrals))
    cycle = jnp.einsum("iakc,kcjb->iajb", sym_amp, sym_int, precision=lax.Precision.HIGHEST)
    exchange = jnp.einsum("icka,kcjb->iajb", sym_amp, sym_int, precision=lax.Precision.HIGHEST)
    return 2.0 * cycle - exchange
```

```python
import jax
import jax.numpy as jnp
from jax import lax
from jax.experimental import pallas as pl
from jax.experimental.pallas import tpu as pltpu
from jax.sharding import PartitionSpec as P

MESH = pl.DeviceIdType.MESH
F32 = jnp.float32
BF16 = jnp.bfloat16
CAP = 96
NI = 4
NJ = 4
NA = 19
NK = 4
NB = 38
NV = 608
BLK = 32
INT = 16
ROWS = 80
CPAD = 24


def lookup(labels, where_at):
    positions = jnp.arange(labels.shape[0], dtype=jnp.int32)
    onehot = (where_at[:, None] == positions[None, :]).astype(jnp.int32)
    return jnp.sum(onehot * labels[None, :], axis=1)


def halves(x):
    high = x.astype(BF16)
    return high, (x - high.astype(F32)).astype(BF16)


def nn(a, b):
    return jnp.dot(a, b, preferred_element_type=F32)


def kernel(
    g_ref, at_ref, d_ref, pt_ref, irrc_ref, skia_ref, sbj_ref, sia_ref, code_ref, codez_ref, sjb_ref, siac_ref,
    out_ref,
    gbuf, dbuf, rbuf, ebuf, zsend, zrecv, ysum, ygath,
    g_send, g_recv, f_send, f_recv, d_send, d_recv, z_send, z_recv, y_send, y_recv,
):
    me = lax.axis_index("blk")
    mz = lax.axis_index("int")
    core = me % 2
    chip = me // 2
    cy = chip // 4
    cx = chip % 4
    sibling = me + 1 - 2 * core

    barrier = pltpu.get_barrier_semaphore()

    def greet_blk(n, c):
        pl.semaphore_signal(barrier, inc=1, device_id=((me + n) % BLK, mz), device_id_type=MESH)
        return c

    def greet_int(n, c):
        pl.semaphore_signal(barrier, inc=1, device_id=(me, (mz + n) % INT), device_id_type=MESH)
        return c

    lax.fori_loop(1, BLK, greet_blk, 0)
    lax.fori_loop(1, INT, greet_int, 0)
    pl.semaphore_wait(barrier, BLK - 1 + INT - 1)

    def at_offset(o, sign):
        return (((cy + sign * (o // 4) + 4) % 4) * 4 + (cx + sign * (o % 4) + 4) % 4) * 2 + core

    def g_copy(o):
        return pltpu.make_async_remote_copy(
            src_ref=g_ref, dst_ref=gbuf.at[me], send_sem=g_send.at[o], recv_sem=g_recv.at[o],
            device_id=(at_offset(o, 1), mz), device_id_type=MESH,
        )

    def f_copy(o):
        slot = at_offset(o, -1)
        return pltpu.make_async_remote_copy(
            src_ref=gbuf.at[slot], dst_ref=gbuf.at[slot], send_sem=f_send.at[o], recv_sem=f_recv.at[o],
            device_id=(sibling, mz), device_id_type=MESH,
        )

    own_forward = pltpu.make_async_remote_copy(
        src_ref=g_ref, dst_ref=gbuf.at[me], send_sem=f_send.at[0], recv_sem=f_recv.at[0],
        device_id=(sibling, mz), device_id_type=MESH,
    )

    def d_copy(n):
        target = (me + n) % BLK
        return pltpu.make_async_remote_copy(
            src_ref=d_ref.at[target], dst_ref=dbuf.at[me], send_sem=d_send.at[n], recv_sem=d_recv.at[n],
            device_id=(target, mz), device_id_type=MESH,
        )

    def z_copy(n):
        target = (mz + n) % INT
        return pltpu.make_async_remote_copy(
            src_ref=zsend.at[target], dst_ref=zrecv.at[mz], send_sem=z_send.at[n], recv_sem=z_recv.at[n],
            device_id=(me, target), device_id_type=MESH,
        )

    def y_copy(n):
        target = (mz + n) % INT
        return pltpu.make_async_remote_copy(
            src_ref=ysum, dst_ref=ygath.at[mz], send_sem=y_send.at[n], recv_sem=y_recv.at[n],
            device_id=(me, target), device_id_type=MESH,
        )

    def each(first, last, do):
        def body(n, c):
            do(n)
            return c

        lax.fori_loop(first, last, body, 0)

    each(1, 16, lambda o: g_copy(o).start())
    own_forward.start()
    each(1, BLK, lambda n: d_copy(n).start())

    gbuf[me] = g_ref[...]
    dbuf[me] = d_ref[me]

    @pl.loop(0, 10)
    def _(n):
        at = pl.ds(pl.multiple_of(n * 256, 256), 256)
        row = lax.broadcasted_iota(jnp.int32, (NJ * CAP, 256), 0)
        ebuf[:, at] = jnp.where(row == code_ref[:, at], 1.0, 0.0).astype(BF16)

    def pass_on(o):
        g_copy(o).wait_recv()
        f_copy(o).start()

    each(1, 16, pass_on)
    each(1, BLK, lambda n: d_copy(n).wait_recv())

    swapped = jnp.where(irrc_ref[...] == skia_ref[...], dbuf[...].reshape(BLK * CPAD, 384), 0.0)
    s_high, s_low = halves(swapped)
    s_t = nn(pt_ref[...], s_high) + nn(pt_ref[...], s_low)
    t_t = 2.0 * at_ref[...] - s_t
    w = jnp.concatenate([t_t[:, k * ROWS:(k + 1) * ROWS] for k in range(NK)], axis=0)
    w = jnp.concatenate([w, jnp.zeros((NK * CAP, 128 - ROWS), F32)], axis=1)
    w_high, w_low = halves(w)

    own_forward.wait_recv()
    each(1, 16, lambda o: f_copy(o).wait_recv())

    @pl.loop(0, 8)
    def _(n):
        g_high, g_low = halves(gbuf[pl.ds(n * 4, 4)].reshape(4 * ROWS, NK * CAP))
        r = nn(g_high, w_high) + (nn(g_high, w_low) + nn(g_low, w_high))
        at = pl.ds(pl.multiple_of(n * 4 * ROWS, 4 * ROWS), 4 * ROWS)
        rbuf[at] = jnp.where(sbj_ref[at] == sia_ref[...], r, 0.0)

    r_high, r_low = halves(rbuf[...])
    packed = nn(ebuf[...], r_high) + nn(ebuf[...], r_low)
    turned = packed.T[:ROWS]
    for block in range(3):
        for group in range(5):
            zsend[block * 5 + group] = turned[group * 16:(group + 1) * 16, block * 128:(block + 1) * 128]
    zsend[15] = jnp.zeros((16, 128), F32)

    each(1, INT, lambda n: z_copy(n).start())
    zrecv[mz] = zsend[mz]
    each(1, INT, lambda n: z_copy(n).wait_recv())
    total = zrecv[0]
    for n in range(1, INT):
        total = total + zrecv[n]
    ysum[...] = total
    each(1, INT, lambda n: y_copy(n).start())
    ygath[mz] = total
    row = lax.broadcasted_iota(jnp.int32, (NJ * CAP, 256), 0)
    spread = jnp.where(row == codez_ref[...], 1.0, 0.0).astype(BF16)
    each(1, INT, lambda n: y_copy(n).wait_recv())
    whole = jnp.concatenate(
        [jnp.concatenate([ygath[block * 5 + group] for group in range(5)], axis=0) for block in range(3)], axis=1
    )
    y_high, y_low = halves(whole)
    out = nn(y_high, spread) + nn(y_low, spread)
    out_ref[...] = jnp.where(siac_ref[...] == sjb_ref[...], out, 0.0)

    each(1, 16, lambda o: g_copy(o).wait_send())
    own_forward.wait_send()
    each(1, 16, lambda o: f_copy(o).wait_send())
    each(1, BLK, lambda n: d_copy(n).wait_send())
    each(1, INT, lambda n: z_copy(n).wait_send())
    each(1, INT, lambda n: y_copy(n).wait_send())


def pad_to(x, shape, value=0):
    return jnp.pad(x, [(0, n - m) for n, m in zip(shape, x.shape)], constant_values=value)


def per_device(amplitudes, integrals, occ_irrep, virt_irrep, i_batch, j_batch):
    blk = lax.axis_index("blk")
    z = lax.axis_index("int")
    occ_k = lax.dynamic_slice_in_dim(occ_irrep, z * NK, NK)
    virt_a = lax.dynamic_slice_in_dim(virt_irrep, blk * NA, NA)
    irr_i = lookup(occ_irrep, i_batch)
    irr_j = lookup(occ_irrep, j_batch)
    orbital = jnp.arange(NV, dtype=jnp.int32)
    alike = (virt_irrep[:, None] == virt_irrep[None, :]) & (orbital[None, :] < orbital[:, None])
    place = jnp.sum(alike.astype(jnp.int32), axis=1)
    onehot = (place[:, None] == jnp.arange(CAP, dtype=jnp.int32)[None, :]).astype(F32)

    s_ika = jnp.bitwise_xor(
        jnp.bitwise_xor(irr_i[:, None, None], occ_k[None, None, :]), virt_a[None, :, None]
    )
    sym_amp = jnp.where(s_ika[..., None] == virt_irrep, amplitudes, 0.0)
    amp_t = jnp.einsum("iakc,cp->pkia", sym_amp, onehot, precision=lax.Precision.HIGHEST)
    amp_t = pad_to(amp_t.reshape(CAP, NK, NI * NA), (CAP, NK, ROWS)).reshape(CAP, NK * ROWS)
    amp_t = pad_to(amp_t, (CAP, 384))

    g = jnp.transpose(integrals, (0, 3, 2, 1))
    s_kbj = jnp.bitwise_xor(
        jnp.bitwise_xor(occ_k[:, None, None], virt_a[None, :, None]), irr_j[None, None, :]
    )
    sym_g = jnp.where(s_kbj[..., None] == virt_irrep, g, 0.0)
    g_p = jnp.einsum("kbjc,cp->bjkp", sym_g, onehot, precision=lax.Precision.HIGHEST)
    g_p = pad_to(g_p.reshape(NA * NJ, NK * CAP), (ROWS, NK * CAP))

    moved = jnp.transpose(amplitudes.reshape(NI, NA, NK, BLK, NA), (3, 1, 2, 0, 4)).reshape(BLK, NA, NK, NI * NA)
    moved = pad_to(pad_to(moved, (BLK, CPAD, NK, ROWS)).reshape(BLK, CPAD, NK * ROWS), (BLK, CPAD, 384))

    p_t = pad_to(onehot.reshape(BLK, NA, CAP), (BLK, CPAD, CAP)).reshape(BLK * CPAD, CAP).T.astype(BF16)
    irr_c = pad_to(virt_irrep.reshape(BLK, NA), (BLK, CPAD), -1).reshape(BLK * CPAD, 1)
    s_kia = jnp.transpose(s_ika, (2, 0, 1)).reshape(NK, NI * NA)
    s_kia = pad_to(pad_to(s_kia, (NK, ROWS), -2).reshape(1, NK * ROWS), (1, 384), -2)

    s_bj = jnp.bitwise_xor(virt_irrep[:, None], irr_j[None, :]).reshape(BLK, NA * NJ)
    s_bj = pad_to(s_bj, (BLK, ROWS), -1).reshape(BLK * ROWS, 1)
    s_ia = jnp.bitwise_xor(irr_i[:, None], virt_a[None, :]).reshape(1, NI * NA)
    code = (place[:, None] + CAP * jnp.arange(NJ, dtype=jnp.int32)[None, :]).reshape(BLK, NA * NJ)
    code = pad_to(code, (BLK, ROWS), -1).reshape(1, BLK * ROWS)

    virt_b = lax.dynamic_slice_in_dim(virt_irrep, z * NB, NB)
    place_b = lax.dynamic_slice_in_dim(place, z * NB, NB)
    codez = (place_b[None, :] + CAP * jnp.arange(NJ, dtype=jnp.int32)[:, None]).reshape(1, NJ * NB)
    s_jb = jnp.bitwise_xor(irr_j[:, None], virt_b[None, :]).reshape(1, NJ * NB)

    vmem = pl.BlockSpec(memory_space=pltpu.VMEM)
    dma = pltpu.SemaphoreType.DMA
    out = pl.pallas_call(
        kernel,
        out_shape=jax.ShapeDtypeStruct((ROWS, 256), F32),
        in_specs=[vmem] * 12,
        out_specs=vmem,
        scratch_shapes=[
            pltpu.VMEM((BLK, ROWS, NK * CAP), F32),
            pltpu.VMEM((BLK, CPAD, 384), F32),
            pltpu.VMEM((BLK * ROWS, 128), F32),
            pltpu.VMEM((NJ * CAP, BLK * ROWS), BF16),
            pltpu.VMEM((INT, 16, 128), F32),
            pltpu.VMEM((INT, 16, 128), F32),
            pltpu.VMEM((16, 128), F32),
            pltpu.VMEM((INT, 16, 128), F32),
            dma((16,)), dma((16,)), dma((16,)), dma((16,)), dma((BLK,)), dma((BLK,)),
            dma((INT,)), dma((INT,)), dma((INT,)), dma((INT,)),
        ],
        compiler_params=pltpu.CompilerParams(
            collective_id=0, has_side_effects=True, vmem_limit_bytes=48 * 1024 * 1024
        ),
    )(
        g_p, amp_t, moved, p_t, irr_c, s_kia, s_bj, pad_to(s_ia, (1, 128), -2), code,
        pad_to(codez, (1, 256), -1), pad_to(s_jb, (1, 256), -1), pad_to(s_ia, (1, ROWS), -2).reshape(ROWS, 1),
    )
    return out[:NI * NA, :NJ * NB].reshape(NI, NA, NJ, NB)


def solution(mesh):
    placed = (P(None, "blk", "int", None), P("int", None, None, "blk"), P(), P(), P(), P())
    return jax.shard_map(
        per_device,
        mesh=mesh,
        in_specs=placed,
        out_specs=P(None, "blk", None, "int"),
        check_vma=False,
    )
```

```python
import jax
import jax.numpy as jnp
from jax import lax
from jax.experimental import pallas as pl
from jax.experimental.pallas import tpu as pltpu
from jax.sharding import PartitionSpec as P

MESH = pl.DeviceIdType.MESH
F32 = jnp.float32
BF16 = jnp.bfloat16
CAP = 96
NI = 4
NJ = 4
NA = 19
NK = 4
NB = 38
NV = 608
BLK = 32
INT = 16
ROWS = 80
CPAD = 24
HALF = 40
GROUP = 320
PITCH = 21


def lookup(labels, where_at):
    positions = jnp.arange(labels.shape[0], dtype=jnp.int32)
    onehot = (where_at[:, None] == positions[None, :]).astype(jnp.int32)
    return jnp.sum(onehot * labels[None, :], axis=1)


def halves(x):
    high = x.astype(BF16)
    return high, (x - high.astype(F32)).astype(BF16)


def nn(a, b):
    return jnp.dot(a, b, preferred_element_type=F32)


def kernel(
    g_ref, at_ref, a_ref, pt_ref, irrc_ref, skia_ref, sbj_ref, sia_ref, code_ref, codez_ref, sjb_ref, siac_ref,
    out_ref,
    gh0, gh1, spaced, moved, dbuf, ebuf, acc, zsend, zrecv, ysum, ygath,
    own_sem, p0_send, p0_recv, p1_send, p1_recv, q0_send, q0_recv, q1_send, q1_recv,
    s0_send, s0_recv, s1_send, s1_recv, d_send, d_recv, z_send, z_recv, y_send, y_recv,
):
    me = lax.axis_index("blk")
    mz = lax.axis_index("int")
    core = me % 2
    cx = (me // 2) % 4
    cy = me // 8

    def plane(y, x, c):
        return ((((y + 4) % 4) * 4 + (x + 4) % 4) * 2 + c, mz)

    def each(first, last, do):
        def body(n, c):
            do(n)
            return c

        lax.fori_loop(first, last, body, 0)

    def remote(src, dst, send, recv, device):
        return pltpu.make_async_remote_copy(
            src_ref=src, dst_ref=dst, send_sem=send, recv_sem=recv, device_id=device, device_id_type=MESH
        )

    barrier = pltpu.get_barrier_semaphore()

    def greet(device):
        pl.semaphore_signal(barrier, inc=1, device_id=device, device_id_type=MESH)

    each(1, INT, lambda n: greet((me, (mz + n) % INT)))
    each(1, BLK, lambda n: greet(((me + n) % BLK, mz)))

    own0 = pltpu.make_async_copy(g_ref.at[pl.ds(0, HALF)], gh0.at[cy, core, cx], own_sem.at[0])
    own1 = pltpu.make_async_copy(g_ref.at[pl.ds(HALF, HALF)], gh1.at[cx, core, cy], own_sem.at[1])
    own0.start()
    own1.start()

    lane = lax.broadcasted_iota(jnp.int32, (NV, 1024), 1)
    source = jnp.where(lane % 32 < NA, NA * (lane // 32) + lane % 32, -1)
    respace = jnp.where(lax.broadcasted_iota(jnp.int32, (NV, 1024), 0) == source, 1.0, 0.0).astype(BF16)
    a_high, a_low = halves(a_ref[...])
    spaced[...] = nn(a_high, respace) + nn(a_low, respace)

    pl.semaphore_wait(barrier, BLK - 1 + INT - 1)

    def p0(o):
        return remote(g_ref.at[pl.ds(0, HALF)], gh0.at[cy, core, cx], p0_send.at[o], p0_recv.at[o], plane(cy, cx + o, core))

    def p1(o):
        return remote(g_ref.at[pl.ds(HALF, HALF)], gh1.at[cx, core, cy], p1_send.at[o], p1_recv.at[o], plane(cy + o, cx, core))

    each(1, 4, lambda o: p0(o).start())
    each(1, 4, lambda o: p1(o).start())

    def d_copy(d):
        return remote(moved.at[d], dbuf.at[me], d_send.at[d], d_recv.at[me], (d, mz))

    def d_start(d):
        @pl.when(d != me)
        def _():
            d_copy(d).start()

    def d_tile(step):
        return (me // 4 + step) % 8

    small = lax.broadcasted_iota(jnp.int32, (CPAD, 128), 1)

    def shuffle(step, c):
        tile = d_tile(step)
        at = pl.ds(pl.multiple_of(tile * 128, 128), 128)
        blocks = [spaced[m * CPAD:(m + 1) * CPAD, at] for m in range(NI * NK)]
        for part in range(4):
            for t in range(3):
                held = jnp.zeros((CPAD, 128), F32)
                here = blocks[6 * t:6 * t + 6]
                for n, block in enumerate(here):
                    shift = (PITCH * n - 32 * part) % 128
                    turned = pltpu.roll(block, shift, 1) if shift else block
                    held = jnp.where((small >= PITCH * n) & (small < PITCH * n + NA), turned, held)
                moved[4 * tile + part, :, t * 128:(t + 1) * 128] = held

        @pl.when(step > 0)
        def _():
            each(0, 4, lambda n: d_start(4 * d_tile(step + 7) + n))

        return c

    lax.fori_loop(0, 8, shuffle, 0)
    each(0, 4, lambda n: d_start(4 * d_tile(7) + n))
    dbuf[me] = moved[me]

    def q0(o):
        dev = plane(cy + 1 - 2 * o, cx, core)
        return remote(gh0.at[cy, core], gh0.at[cy, core], q0_send.at[o], q0_recv.at[o], dev)

    def q1(o):
        dev = plane(cy, cx + 1 - 2 * o, core)
        return remote(gh1.at[cx, core], gh1.at[cx, core], q1_send.at[o], q1_recv.at[o], dev)

    def r0(o):
        row = (cy + 3 + 2 * o) % 4
        part = pl.ds(2 * o, 2)
        ref = gh0.at[row, core, part]
        return remote(ref, ref, q0_send.at[2 + o], q0_recv.at[2 + o], plane(cy + 1 - 2 * o, cx, core))

    def r1(o):
        row = (cx + 3 + 2 * o) % 4
        part = pl.ds(2 * o, 2)
        ref = gh1.at[row, core, part]
        return remote(ref, ref, q1_send.at[2 + o], q1_recv.at[2 + o], plane(cy, cx + 1 - 2 * o, core))

    sibling = plane(cy, cx, 1 - core)
    order = (0, 3, 1, 2)

    def s0(n):
        ref = gh0.at[(cy + order[n]) % 4, core]
        return remote(ref, ref, s0_send.at[n], s0_recv.at[n], sibling)

    def s1(n):
        ref = gh1.at[(cx + order[n]) % 4, core]
        return remote(ref, ref, s1_send.at[n], s1_recv.at[n], sibling)

    own0.wait()
    each(1, 4, lambda o: p0(o).wait_recv())
    q0(0).start()
    q0(1).start()
    s0(0).start()
    own1.wait()
    each(1, 4, lambda o: p1(o).wait_recv())
    q1(0).start()
    q1(1).start()
    s1(0).start()

    @pl.loop(0, 8)
    def _(n):
        row = lax.broadcasted_iota(jnp.int32, (NJ * CAP, GROUP), 0)
        ebuf[n] = jnp.where(row == code_ref[n], 1.0, 0.0).astype(BF16)

    def d_wait(n):
        d = (me + n) % BLK
        remote(moved.at[d], dbuf.at[d], d_send.at[d], d_recv.at[d], (d, mz)).wait_recv()

    each(1, BLK, d_wait)
    swapped = jnp.where(irrc_ref[...] == skia_ref[...], dbuf[...].reshape(BLK * CPAD, 384), 0.0)
    s_high, s_low = halves(swapped)
    s_t = nn(pt_ref[...], s_high) + nn(pt_ref[...], s_low)
    t_t = 2.0 * at_ref[...] - s_t
    columns = []
    for k in range(NK):
        first = [128 * ((NI * k + i) // 6) + PITCH * ((NI * k + i) % 6) for i in range(NI)]
        columns.append(jnp.concatenate([t_t[:, f:f + NA] for f in first], axis=1))
    w = jnp.concatenate(columns, axis=0)
    w = jnp.concatenate([w, jnp.zeros((NK * CAP, 128 - NI * NA), F32)], axis=1)
    w_high, w_low = halves(w)

    acc[...] = jnp.zeros_like(acc)

    def product(piece, n):
        g_high, g_low = halves(piece.reshape(GROUP, NK * CAP))
        r = nn(g_high, w_high) + (nn(g_high, w_low) + nn(g_low, w_high))
        r_high, r_low = halves(jnp.where(sbj_ref[n] == sia_ref[...], r, 0.0))
        acc[...] += nn(ebuf[n], r_high) + nn(ebuf[n], r_low)

    def product0(n):
        s0(n).wait_recv()
        row = (cy + order[n]) % 4
        product(gh0[row], row)

    def product1(n):
        s1(n).wait_recv()
        row = (cx + order[n]) % 4
        product(gh1[row], 4 + row)

    q0(0).wait_recv()
    r0(0).start()
    s0(1).start()
    q1(0).wait_recv()
    r1(0).start()
    s1(1).start()
    q0(1).wait_recv()
    r0(1).start()
    s0(2).start()
    q1(1).wait_recv()
    r1(1).start()
    s1(2).start()
    for n in range(3):
        product0(n)
        product1(n)
    r0(0).wait_recv()
    r0(1).wait_recv()
    s0(3).start()
    r1(0).wait_recv()
    r1(1).wait_recv()
    s1(3).start()
    product0(3)
    product1(3)

    def z_copy(n):
        target = (mz + n) % INT
        return remote(zsend.at[target], zrecv.at[mz], z_send.at[n], z_recv.at[n], (me, target))

    def y_copy(n):
        target = (mz + n) % INT
        return remote(ysum, ygath.at[mz], y_send.at[n], y_recv.at[n], (me, target))

    turned = acc[...].T[:ROWS]
    for block in range(3):
        for group in range(5):
            zsend[block * 5 + group] = turned[group * 16:(group + 1) * 16, block * 128:(block + 1) * 128]
    zsend[15] = jnp.zeros((16, 128), F32)

    each(1, INT, lambda n: z_copy((n + 7) % 15 + 1).start())
    zrecv[mz] = zsend[mz]
    each(1, INT, lambda n: z_copy(n).wait_recv())
    total = zrecv[0]
    for n in range(1, INT):
        total = total + zrecv[n]
    ysum[...] = total
    each(1, INT, lambda n: y_copy((n + 7) % 15 + 1).start())
    ygath[mz] = total
    row = lax.broadcasted_iota(jnp.int32, (NJ * CAP, 256), 0)
    spread = jnp.where(row == codez_ref[...], 1.0, 0.0).astype(BF16)
    each(1, INT, lambda n: y_copy(n).wait_recv())
    whole = jnp.concatenate(
        [jnp.concatenate([ygath[block * 5 + group] for group in range(5)], axis=0) for block in range(3)], axis=1
    )
    y_high, y_low = halves(whole)
    out = nn(y_high, spread) + nn(y_low, spread)
    out_ref[...] = jnp.where(siac_ref[...] == sjb_ref[...], out, 0.0)

    each(1, 4, lambda o: p0(o).wait_send())
    each(1, 4, lambda o: p1(o).wait_send())
    for o in range(2):
        q0(o).wait_send()
        q1(o).wait_send()
        r0(o).wait_send()
        r1(o).wait_send()
    for n in range(4):
        s0(n).wait_send()
        s1(n).wait_send()
    each(1, BLK, lambda n: d_copy((me + n) % BLK).wait_send())
    each(1, INT, lambda n: z_copy(n).wait_send())
    each(1, INT, lambda n: y_copy(n).wait_send())


def pad_to(x, shape, value=0):
    return jnp.pad(x, [(0, n - m) for n, m in zip(shape, x.shape)], constant_values=value)


def blocks_of_six(x, value):
    x = pad_to(x, (x.shape[0], 18, PITCH), value).reshape(-1, 3, 6 * PITCH)
    return pad_to(x, (x.shape[0], 3, 128), value).reshape(-1, 384)


def by_group(x):
    x = x.reshape(4, 4, 2, 2, HALF)
    first = jnp.transpose(x[:, :, :, 0], (0, 2, 1, 3)).reshape(4, GROUP)
    second = jnp.transpose(x[:, :, :, 1], (1, 2, 0, 3)).reshape(4, GROUP)
    return jnp.concatenate([first, second], axis=0)


def per_device(amplitudes, integrals, occ_irrep, virt_irrep, i_batch, j_batch):
    blk = lax.axis_index("blk")
    z = lax.axis_index("int")
    occ_k = lax.dynamic_slice_in_dim(occ_irrep, z * NK, NK)
    virt_a = lax.dynamic_slice_in_dim(virt_irrep, blk * NA, NA)
    irr_i = lookup(occ_irrep, i_batch)
    irr_j = lookup(occ_irrep, j_batch)
    orbital = jnp.arange(NV, dtype=jnp.int32)
    alike = (virt_irrep[:, None] == virt_irrep[None, :]) & (orbital[None, :] < orbital[:, None])
    place = jnp.sum(alike.astype(jnp.int32), axis=1)
    onehot = (place[:, None] == jnp.arange(CAP, dtype=jnp.int32)[None, :]).astype(F32)

    s_ika = jnp.bitwise_xor(
        jnp.bitwise_xor(irr_i[:, None, None], occ_k[None, None, :]), virt_a[None, :, None]
    )
    sym_amp = jnp.where(s_ika[..., None] == virt_irrep, amplitudes, 0.0)
    amp_t = jnp.einsum("iakc,cp->pkia", sym_amp, onehot, precision=lax.Precision.HIGHEST)
    amp_t = blocks_of_six(amp_t.reshape(CAP, NK * NI, NA), 0)

    g = jnp.transpose(integrals, (0, 3, 2, 1))
    s_kbj = jnp.bitwise_xor(
        jnp.bitwise_xor(occ_k[:, None, None], virt_a[None, :, None]), irr_j[None, None, :]
    )
    sym_g = jnp.where(s_kbj[..., None] == virt_irrep, g, 0.0)
    g_p = jnp.einsum("kbjc,cp->bjkp", sym_g, onehot, precision=lax.Precision.HIGHEST)
    g_p = pad_to(g_p.reshape(NA * NJ, NK * CAP), (ROWS, NK * CAP))

    a_rows = pad_to(jnp.transpose(amplitudes, (2, 0, 1, 3)), (NK, NI, CPAD, NV)).reshape(NK * NI * CPAD, NV)

    p_t = pad_to(onehot.reshape(BLK, NA, CAP), (BLK, CPAD, CAP)).reshape(BLK * CPAD, CAP).T.astype(BF16)
    irr_c = pad_to(virt_irrep.reshape(BLK, NA), (BLK, CPAD), -1).reshape(BLK * CPAD, 1)
    s_kia = blocks_of_six(jnp.transpose(s_ika, (2, 0, 1)).reshape(1, NK * NI, NA), -2)

    s_bj = jnp.bitwise_xor(virt_irrep[:, None], irr_j[None, :]).reshape(BLK, NA * NJ)
    s_bj = by_group(pad_to(s_bj, (BLK, ROWS), -1)).reshape(8, GROUP, 1)
    s_ia = jnp.bitwise_xor(irr_i[:, None], virt_a[None, :]).reshape(1, NI * NA)
    code = (place[:, None] + CAP * jnp.arange(NJ, dtype=jnp.int32)[None, :]).reshape(BLK, NA * NJ)
    code = by_group(pad_to(code, (BLK, ROWS), -1)).reshape(8, 1, GROUP)

    virt_b = lax.dynamic_slice_in_dim(virt_irrep, z * NB, NB)
    place_b = lax.dynamic_slice_in_dim(place, z * NB, NB)
    codez = (place_b[None, :] + CAP * jnp.arange(NJ, dtype=jnp.int32)[:, None]).reshape(1, NJ * NB)
    s_jb = jnp.bitwise_xor(irr_j[:, None], virt_b[None, :]).reshape(1, NJ * NB)

    vmem = pl.BlockSpec(memory_space=pltpu.VMEM)
    dma = pltpu.SemaphoreType.DMA
    out = pl.pallas_call(
        kernel,
        out_shape=jax.ShapeDtypeStruct((ROWS, 256), F32),
        in_specs=[vmem] * 12,
        out_specs=vmem,
        scratch_shapes=[
            pltpu.VMEM((4, 2, 4, HALF, NK * CAP), F32),
            pltpu.VMEM((4, 2, 4, HALF, NK * CAP), F32),
            pltpu.VMEM((NI * NK * CPAD, 1024), F32),
            pltpu.VMEM((BLK, CPAD, 384), F32),
            pltpu.VMEM((BLK, CPAD, 384), F32),
            pltpu.VMEM((8, NJ * CAP, GROUP), BF16),
            pltpu.VMEM((NJ * CAP, 128), F32),
            pltpu.VMEM((INT, 16, 128), F32),
            pltpu.VMEM((INT, 16, 128), F32),
            pltpu.VMEM((16, 128), F32),
            pltpu.VMEM((INT, 16, 128), F32),
            dma((2,)), dma((4,)), dma((4,)), dma((4,)), dma((4,)), dma((4,)), dma((4,)), dma((4,)), dma((4,)),
            dma((4,)), dma((4,)), dma((4,)), dma((4,)), dma((BLK,)), dma((BLK,)),
            dma((INT,)), dma((INT,)), dma((INT,)), dma((INT,)),
        ],
        compiler_params=pltpu.CompilerParams(
            collective_id=0, has_side_effects=True, vmem_limit_bytes=48 * 1024 * 1024
        ),
    )(
        g_p, amp_t, a_rows, p_t, irr_c, s_kia, s_bj, pad_to(s_ia, (1, 128), -2), code,
        pad_to(codez, (1, 256), -1), pad_to(s_jb, (1, 256), -1), pad_to(s_ia, (1, ROWS), -2).reshape(ROWS, 1),
    )
    return out[:NI * NA, :NJ * NB].reshape(NI, NA, NJ, NB)


def solution(mesh):
    placed = (P(None, "blk", "int", None), P("int", None, None, "blk"), P(), P(), P(), P())
    return jax.shard_map(
        per_device,
        mesh=mesh,
        in_specs=placed,
        out_specs=P(None, "blk", None, "int"),
        check_vma=False,
    )
```

```python
import jax
import jax.numpy as jnp
from jax import lax
from jax.experimental import pallas as pl
from jax.experimental.pallas import tpu as pltpu
from jax.sharding import PartitionSpec as P

MESH = pl.DeviceIdType.MESH
F32 = jnp.float32
BF16 = jnp.bfloat16
CAP = 96
NI = 4
NJ = 4
NA = 19
NK = 4
NB = 38
NV = 608
BLK = 32
INT = 16
ROWS = 80
CPAD = 24
HALF = 40
GROUP = 320
FAR_FIRST = (8, 7, 9, 6, 10, 5, 11, 4, 12, 3, 13, 2, 14, 1, 15)
PITCH = 21


def lookup(labels, where_at):
    positions = jnp.arange(labels.shape[0], dtype=jnp.int32)
    onehot = (where_at[:, None] == positions[None, :]).astype(jnp.int32)
    return jnp.sum(onehot * labels[None, :], axis=1)


def halves(x):
    high = x.astype(BF16)
    return high, (x - high.astype(F32)).astype(BF16)


def nn(a, b):
    return jnp.dot(a, b, preferred_element_type=F32)


def nt(a, b):
    return lax.dot_general(a, b, (((1,), (1,)), ((), ())), preferred_element_type=F32)


def kernel(
    int_ref, skbj_ref, a_ref, skiac_ref, virt_ref, place_ref, placed_ref, irrc_ref, skia_ref, row_ref, column_ref, sia_ref,
    rowz_ref, siac_ref,
    out_ref,
    g_ref, g_rows, gh0, gh1, spaced, moved, dbuf, arrived, ebuf, acc, zsend, zrecv, ysum, ygath,
    own_sem, p0_send, p0_recv, p1_send, p1_recv, q0_send, q0_recv, q1_send, q1_recv,
    s0_send, s0_recv, s1_send, s1_recv, d_send, d_recv, z_send, z_recv, y_send, y_recv,
):
    me = lax.axis_index("blk")
    mz = lax.axis_index("int")
    core = me % 2
    cx = (me // 2) % 4
    cy = me // 8

    def plane(y, x, c):
        return ((((y + 4) % 4) * 4 + (x + 4) % 4) * 2 + c, mz)

    def each(first, last, do):
        def body(n, c):
            do(n)
            return c

        lax.fori_loop(first, last, body, 0)

    def remote(src, dst, send, recv, device):
        return pltpu.make_async_remote_copy(
            src_ref=src, dst_ref=dst, send_sem=send, recv_sem=recv, device_id=device, device_id_type=MESH
        )

    barrier = pltpu.get_barrier_semaphore()

    def greet(device):
        pl.semaphore_signal(barrier, inc=1, device_id=device, device_id_type=MESH)

    each(1, INT, lambda n: greet((me, (mz + n) % INT)))
    each(1, BLK, lambda n: greet(((me + n) % BLK, mz)))

    own0 = pltpu.make_async_copy(g_ref.at[pl.ds(0, HALF)], gh0.at[cy, core, cx], own_sem.at[0])
    own1 = pltpu.make_async_copy(g_ref.at[pl.ds(HALF, HALF)], gh1.at[cx, core, cy], own_sem.at[1])

    def onehot(places):
        row = lax.broadcasted_iota(jnp.int32, (CAP, places.shape[1]), 0)
        return jnp.where(row == places, 1.0, 0.0).astype(BF16)

    p_all = onehot(place_ref[...])
    for k in range(NK):
        for b in range(NA):
            g_rows[k, b * NJ:(b + 1) * NJ] = int_ref[k, b]
        g_rows[k, NA * NJ:] = jnp.zeros((ROWS - NA * NJ, NV), F32)
    packed = []
    for k in range(NK):
        high, low = halves(jnp.where(skbj_ref[k] == virt_ref[...], g_rows[k], 0.0))
        packed.append(nt(high, p_all) + nt(low, p_all))
    g_ref[...] = jnp.concatenate(packed, axis=1)
    high, low = halves(jnp.where(skiac_ref[...] == virt_ref[...], a_ref[...], 0.0))
    direct = nt(p_all, high) + nt(p_all, low)
    p_t = onehot(placed_ref[...])

    a_high, a_low = halves(a_ref[...])
    for n in range(4):
        lane = lax.broadcasted_iota(jnp.int32, (1, 256), 1)
        source = jnp.where(lane % 32 < NA, NA * (8 * n + lane // 32) + lane % 32, -1)
        respace = jnp.where(lax.broadcasted_iota(jnp.int32, (NV, 256), 0) == source, 1.0, 0.0).astype(BF16)
        spaced[:, n * 256:(n + 1) * 256] = nn(a_high, respace) + nn(a_low, respace)

    pl.semaphore_wait(barrier, BLK - 1 + INT - 1)

    own0.start()
    own1.start()

    def p0(o):
        return remote(g_ref.at[pl.ds(0, HALF)], gh0.at[cy, core, cx], p0_send.at[o], p0_recv.at[o], plane(cy, cx + o, core))

    def p1(o):
        return remote(g_ref.at[pl.ds(HALF, HALF)], gh1.at[cx, core, cy], p1_send.at[o], p1_recv.at[o], plane(cy + o, cx, core))

    each(1, 4, lambda o: p0(o).start())
    each(1, 4, lambda o: p1(o).start())

    def d_copy(d):
        return remote(moved.at[d], dbuf.at[me], d_send.at[d], d_recv.at[me], (d, mz))

    def d_start(d):
        @pl.when(d != me)
        def _():
            d_copy(d).start()

    def d_tile(step):
        return (me // 4 + step) % 8

    small = lax.broadcasted_iota(jnp.int32, (CPAD, 128), 1)

    def shuffle(step, c):
        tile = d_tile(step)
        at = pl.ds(pl.multiple_of(tile * 128, 128), 128)
        blocks = [spaced[m * CPAD:(m + 1) * CPAD, at] for m in range(NI * NK)]
        for part in range(4):
            for t in range(3):
                held = jnp.zeros((CPAD, 128), F32)
                here = blocks[6 * t:6 * t + 6]
                for n, block in enumerate(here):
                    shift = (PITCH * n - 32 * part) % 128
                    turned = pltpu.roll(block, shift, 1) if shift else block
                    held = jnp.where((small >= PITCH * n) & (small < PITCH * n + NA), turned, held)
                moved[4 * tile + part, :, t * 128:(t + 1) * 128] = held[:NA]

        @pl.when(step > 0)
        def _():
            each(0, 4, lambda n: d_start(4 * d_tile(step + 7) + n))

        return c

    lax.fori_loop(0, 8, shuffle, 0)
    each(0, 4, lambda n: d_start(4 * d_tile(7) + n))
    dbuf[me] = moved[me]

    def q0(o):
        dev = plane(cy + 1 - 2 * o, cx, core)
        return remote(gh0.at[cy, core], gh0.at[cy, core], q0_send.at[o], q0_recv.at[o], dev)

    def q1(o):
        dev = plane(cy, cx + 1 - 2 * o, core)
        return remote(gh1.at[cx, core], gh1.at[cx, core], q1_send.at[o], q1_recv.at[o], dev)

    def r0(o):
        row = (cy + 3 + 2 * o) % 4
        part = pl.ds(2 * o, 2)
        ref = gh0.at[row, core, part]
        return remote(ref, ref, q0_send.at[2 + o], q0_recv.at[2 + o], plane(cy + 1 - 2 * o, cx, core))

    def r1(o):
        row = (cx + 3 + 2 * o) % 4
        part = pl.ds(2 * o, 2)
        ref = gh1.at[row, core, part]
        return remote(ref, ref, q1_send.at[2 + o], q1_recv.at[2 + o], plane(cy, cx + 1 - 2 * o, core))

    sibling = plane(cy, cx, 1 - core)

    def order(n):
        return n + n // 2 - 2 * (n // 3)

    def s0(n):
        ref = gh0.at[(cy + order(n)) % 4, core]
        return remote(ref, ref, s0_send.at[n], s0_recv.at[n], sibling)

    def s1(n):
        ref = gh1.at[(cx + order(n)) % 4, core]
        return remote(ref, ref, s1_send.at[n], s1_recv.at[n], sibling)

    own0.wait()
    each(1, 4, lambda o: p0(o).wait_recv())
    q0(0).start()
    q0(1).start()
    s0(0).start()
    own1.wait()
    each(1, 4, lambda o: p1(o).wait_recv())
    q1(0).start()
    q1(1).start()
    s1(0).start()

    @pl.loop(0, 8)
    def _(n):
        row = lax.broadcasted_iota(jnp.int32, (NJ * CAP, GROUP), 0)
        ebuf[n] = jnp.where(row == row_ref[n] // 8, 1.0, 0.0).astype(BF16)

    def d_wait(n):
        d = (me + n) % BLK
        remote(moved.at[d], dbuf.at[d], d_send.at[d], d_recv.at[d], (d, mz)).wait_recv()

    each(1, BLK, d_wait)
    for d in range(BLK):
        arrived[d * CPAD:d * CPAD + NA] = dbuf[d]
    swapped = jnp.where(irrc_ref[...] == skia_ref[...], arrived[...], 0.0)
    s_high, s_low = halves(swapped)
    s_t = nn(p_t, s_high) + nn(p_t, s_low)
    columns = []
    for k in range(NK):
        pairs = []
        for m in range(NI * k, NI * k + NI):
            first = 128 * (m // 6) + PITCH * (m % 6)
            pairs.append(2.0 * direct[:, m * CPAD:m * CPAD + NA] - s_t[:, first:first + NA])
        columns.append(jnp.concatenate(pairs, axis=1))
    w = jnp.concatenate(columns, axis=0)
    w = jnp.concatenate([w, jnp.zeros((NK * CAP, 128 - NI * NA), F32)], axis=1)
    w_high, w_low = halves(w)

    acc[...] = jnp.zeros_like(acc)

    def product(piece, n):
        g_high, g_low = halves(piece.reshape(GROUP, NK * CAP))
        r = nn(g_high, w_high) + (nn(g_high, w_low) + nn(g_low, w_high))
        r_high, r_low = halves(jnp.where(column_ref[n] % 8 == sia_ref[...], r, 0.0))
        acc[...] += nn(ebuf[n], r_high) + nn(ebuf[n], r_low)

    def product0(n):
        s0(n).wait_recv()
        row = (cy + order(n)) % 4
        product(gh0[row], row)

    def product1(n):
        s1(n).wait_recv()
        row = (cx + order(n)) % 4
        product(gh1[row], 4 + row)

    q0(1).wait_recv()
    r0(1).start()
    s0(1).start()
    q1(1).wait_recv()
    r1(1).start()
    s1(1).start()
    q0(0).wait_recv()
    r0(0).start()
    s0(2).start()
    q1(0).wait_recv()
    r1(0).start()
    s1(2).start()

    def products(n, c):
        @pl.when(n == 3)
        def _():
            r0(0).wait_recv()
            r0(1).wait_recv()
            s0(3).start()
            r1(0).wait_recv()
            r1(1).wait_recv()
            s1(3).start()

        product0(n)
        product1(n)
        return c

    lax.fori_loop(0, 4, products, 0)

    def z_copy(n):
        target = (mz + n) % INT
        return remote(zsend.at[target], zrecv.at[mz], z_send.at[n], z_recv.at[n], (me, target))

    def y_copy(n):
        target = (mz + n) % INT
        return remote(ysum, ygath.at[mz], y_send.at[n], y_recv.at[n], (me, target))

    turned = acc[...].T[:ROWS]
    for block in range(3):
        for group in range(5):
            zsend[block * 5 + group] = turned[group * 16:(group + 1) * 16, block * 128:(block + 1) * 128]
    zsend[15] = jnp.zeros((16, 128), F32)

    for n in FAR_FIRST:
        z_copy(n).start()
    zrecv[mz] = zsend[mz]
    each(1, INT, lambda n: z_copy(n).wait_recv())
    total = zrecv[0]
    for n in range(1, INT):
        total = total + zrecv[n]
    ysum[...] = total
    for n in FAR_FIRST:
        y_copy(n).start()
    ygath[mz] = total
    row = lax.broadcasted_iota(jnp.int32, (NJ * CAP, 256), 0)
    spread = jnp.where(row == rowz_ref[...] // 8, 1.0, 0.0).astype(BF16)
    each(1, INT, lambda n: y_copy(n).wait_recv())
    whole = jnp.concatenate(
        [jnp.concatenate([ygath[block * 5 + group] for group in range(5)], axis=0) for block in range(3)], axis=1
    )
    y_high, y_low = halves(whole)
    out = nn(y_high, spread) + nn(y_low, spread)
    out_ref[...] = jnp.where(siac_ref[...] == rowz_ref[...] % 8, out, 0.0)

    each(1, 4, lambda o: p0(o).wait_send())
    each(1, 4, lambda o: p1(o).wait_send())
    for o in range(2):
        q0(o).wait_send()
        q1(o).wait_send()
        r0(o).wait_send()
        r1(o).wait_send()
    for n in range(4):
        s0(n).wait_send()
        s1(n).wait_send()
    each(1, BLK, lambda n: d_copy((me + n) % BLK).wait_send())
    each(1, INT, lambda n: z_copy(n).wait_send())
    each(1, INT, lambda n: y_copy(n).wait_send())


def pad_to(x, shape, value=0):
    return jnp.pad(x, [(0, n - m) for n, m in zip(shape, x.shape)], constant_values=value)


def blocks_of_six(x, value):
    x = pad_to(x, (x.shape[0], 18, PITCH), value).reshape(-1, 3, 6 * PITCH)
    return pad_to(x, (x.shape[0], 3, 128), value).reshape(-1, 384)


def by_group(x):
    x = x.reshape(4, 4, 2, 2, HALF)
    first = jnp.transpose(x[:, :, :, 0], (0, 2, 1, 3)).reshape(4, GROUP)
    second = jnp.transpose(x[:, :, :, 1], (1, 2, 0, 3)).reshape(4, GROUP)
    return jnp.concatenate([first, second], axis=0)


def per_device(amplitudes, integrals, occ_irrep, virt_irrep, i_batch, j_batch):
    blk = lax.axis_index("blk")
    z = lax.axis_index("int")
    occ_k = lax.dynamic_slice_in_dim(occ_irrep, z * NK, NK)
    virt_a = lax.dynamic_slice_in_dim(virt_irrep, blk * NA, NA)
    irr_i = lookup(occ_irrep, i_batch)
    irr_j = lookup(occ_irrep, j_batch)
    orbital = jnp.arange(NV, dtype=jnp.int32)
    alike = (virt_irrep[:, None] == virt_irrep[None, :]) & (orbital[None, :] < orbital[:, None])
    place = jnp.sum(alike.astype(jnp.int32), axis=1)
    s_ika = jnp.bitwise_xor(
        jnp.bitwise_xor(irr_i[:, None, None], occ_k[None, None, :]), virt_a[None, :, None]
    )
    a_rows = pad_to(jnp.transpose(amplitudes, (2, 0, 1, 3)), (NK, NI, CPAD, NV)).reshape(NK * NI * CPAD, NV)
    s_kia = jnp.transpose(s_ika, (2, 0, 1)).reshape(1, NK * NI, NA)
    s_kia_column = pad_to(s_kia, (1, NK * NI, CPAD), -2).reshape(NK * NI * CPAD, 1)
    s_kia = blocks_of_six(s_kia, -2)

    ints = jnp.transpose(integrals, (0, 3, 2, 1))
    s_kbj = jnp.bitwise_xor(
        jnp.bitwise_xor(occ_k[:, None, None], virt_a[None, :, None]), irr_j[None, None, :]
    )
    s_kbj = pad_to(s_kbj.reshape(NK, NA * NJ), (NK, ROWS), -2).reshape(NK, ROWS, 1)

    placed = pad_to(place.reshape(BLK, NA), (BLK, CPAD), -1).reshape(1, BLK * CPAD)
    irr_c = pad_to(virt_irrep.reshape(BLK, NA), (BLK, CPAD), -1).reshape(BLK * CPAD, 1)
    s_ia = jnp.bitwise_xor(irr_i[:, None], virt_a[None, :]).reshape(1, NI * NA)

    offset = 8 * CAP * jnp.arange(NJ, dtype=jnp.int32)
    pairs = 8 * place[:, None] + offset[None, :] + jnp.bitwise_xor(virt_irrep[:, None], irr_j[None, :])
    pairs = by_group(pad_to(pairs.reshape(BLK, NA * NJ), (BLK, ROWS), -1))
    virt_b = lax.dynamic_slice_in_dim(virt_irrep, z * NB, NB)
    place_b = lax.dynamic_slice_in_dim(place, z * NB, NB)
    row_z = 8 * place_b[None, :] + offset[:, None] + jnp.bitwise_xor(irr_j[:, None], virt_b[None, :])
    row_z = pad_to(row_z.reshape(1, NJ * NB), (1, 256), -1)

    vmem = pl.BlockSpec(memory_space=pltpu.VMEM)
    dma = pltpu.SemaphoreType.DMA
    out = pl.pallas_call(
        kernel,
        out_shape=jax.ShapeDtypeStruct((ROWS, 256), F32),
        in_specs=[vmem] * 14,
        out_specs=vmem,
        scratch_shapes=[
            pltpu.VMEM((ROWS, NK * CAP), F32),
            pltpu.VMEM((NK, ROWS, NV), F32),
            pltpu.VMEM((4, 2, 4, HALF, NK * CAP), F32),
            pltpu.VMEM((4, 2, 4, HALF, NK * CAP), F32),
            pltpu.VMEM((NI * NK * CPAD, 1024), F32),
            pltpu.VMEM((BLK, NA, 384), F32),
            pltpu.VMEM((BLK, NA, 384), F32),
            pltpu.VMEM((BLK * CPAD, 384), F32),
            pltpu.VMEM((8, NJ * CAP, GROUP), BF16),
            pltpu.VMEM((NJ * CAP, 128), F32),
            pltpu.VMEM((INT, 16, 128), F32),
            pltpu.VMEM((INT, 16, 128), F32),
            pltpu.VMEM((16, 128), F32),
            pltpu.VMEM((INT, 16, 128), F32),
            dma((2,)), dma((4,)), dma((4,)), dma((4,)), dma((4,)), dma((4,)), dma((4,)), dma((4,)), dma((4,)),
            dma((4,)), dma((4,)), dma((4,)), dma((4,)), dma((BLK,)), dma((BLK,)),
            dma((INT,)), dma((INT,)), dma((INT,)), dma((INT,)),
        ],
        compiler_params=pltpu.CompilerParams(
            collective_id=0, has_side_effects=True, vmem_limit_bytes=48 * 1024 * 1024
        ),
    )(
        ints, s_kbj, a_rows, s_kia_column, virt_irrep.reshape(1, NV), place.reshape(1, NV), placed, irr_c, s_kia,
        pairs.reshape(8, 1, GROUP), pairs.reshape(8, GROUP, 1), pad_to(s_ia, (1, 128), -2), row_z,
        pad_to(s_ia, (1, ROWS), -2).reshape(ROWS, 1),
    )
    return out[:NI * NA, :NJ * NB].reshape(NI, NA, NJ, NB)


def solution(mesh):
    placed = (P(None, "blk", "int", None), P("int", None, None, "blk"), P(), P(), P(), P())
    return jax.shard_map(
        per_device,
        mesh=mesh,
        in_specs=placed,
        out_specs=P(None, "blk", None, "int"),
        check_vma=False,
    )
```

```python
import jax
import jax.numpy as jnp
from jax import lax
from jax.experimental import pallas as pl
from jax.experimental.pallas import tpu as pltpu
from jax.sharding import PartitionSpec as P

MESH = pl.DeviceIdType.MESH
F32 = jnp.float32
BF16 = jnp.bfloat16
CAP = 96
NI = 4
NJ = 4
NA = 19
NK = 4
NB = 38
NV = 608
BLK = 32
INT = 16
ROWS = 80
CPAD = 24
HALF = 40
GROUP = 320
FAR_FIRST = (8, 7, 9, 6, 10, 5, 11, 4, 12, 3, 13, 2, 14, 1, 15)
PITCH = 21


def lookup(labels, where_at):
    positions = jnp.arange(labels.shape[0], dtype=jnp.int32)
    onehot = (where_at[:, None] == positions[None, :]).astype(jnp.int32)
    return jnp.sum(onehot * labels[None, :], axis=1)


def halves(x):
    high = x.astype(BF16)
    return high, (x - high.astype(F32)).astype(BF16)


def nn(a, b):
    return jnp.dot(a, b, preferred_element_type=F32)


def nt(a, b):
    return lax.dot_general(a, b, (((1,), (1,)), ((), ())), preferred_element_type=F32)


def kernel(
    int_ref, skbj_ref, a_ref, skiac_ref, virt_ref, place_ref, placed_ref, irrc_ref, skia_ref, row_ref, column_ref, sia_ref,
    rowz_ref, siac_ref,
    out_ref,
    g_ref, g_rows, gh0, gh1, spaced, moved, dbuf, arrived, ebuf, acc, zsend, zrecv, ysum, ygath,
    own_sem, p0_send, p0_recv, p1_send, p1_recv, q0_send, q0_recv, q1_send, q1_recv,
    s0_send, s0_recv, s1_send, s1_recv, d_send, d_recv, z_send, z_recv, y_send, y_recv,
):
    me = lax.axis_index("blk")
    mz = lax.axis_index("int")
    core = me % 2
    cx = (me // 2) % 4
    cy = me // 8

    def plane(y, x, c):
        return ((((y + 4) % 4) * 4 + (x + 4) % 4) * 2 + c, mz)

    def each(first, last, do):
        def body(n, c):
            do(n)
            return c

        lax.fori_loop(first, last, body, 0)

    def remote(src, dst, send, recv, device):
        return pltpu.make_async_remote_copy(
            src_ref=src, dst_ref=dst, send_sem=send, recv_sem=recv, device_id=device, device_id_type=MESH
        )

    barrier = pltpu.get_barrier_semaphore()

    def greet(device):
        pl.semaphore_signal(barrier, inc=1, device_id=device, device_id_type=MESH)

    each(1, INT, lambda n: greet((me, (mz + n) % INT)))
    each(1, BLK, lambda n: greet(((me + n) % BLK, mz)))

    own0 = pltpu.make_async_copy(g_ref.at[pl.ds(0, HALF)], gh0.at[cy, core, cx], own_sem.at[0])
    own1 = pltpu.make_async_copy(g_ref.at[pl.ds(HALF, HALF)], gh1.at[cx, core, cy], own_sem.at[1])

    def onehot(places):
        row = lax.broadcasted_iota(jnp.int32, (CAP, places.shape[1]), 0)
        return jnp.where(row == places, 1.0, 0.0).astype(BF16)

    p_all = onehot(place_ref[...])
    for k in range(NK):
        for b in range(NA):
            g_rows[k, b * NJ:(b + 1) * NJ] = int_ref[k, b]
        g_rows[k, NA * NJ:] = jnp.zeros((ROWS - NA * NJ, NV), F32)
    packed = []
    for k in range(NK):
        high, low = halves(jnp.where(skbj_ref[k] == virt_ref[...], g_rows[k], 0.0))
        packed.append(nt(high, p_all) + nt(low, p_all))
    g_ref[...] = jnp.concatenate(packed, axis=1)
    pl.semaphore_wait(barrier, BLK - 1 + INT - 1)

    own0.start()
    own1.start()

    def p0(o):
        return remote(g_ref.at[pl.ds(0, HALF)], gh0.at[cy, core, cx], p0_send.at[o], p0_recv.at[o], plane(cy, cx + o, core))

    def p1(o):
        return remote(g_ref.at[pl.ds(HALF, HALF)], gh1.at[cx, core, cy], p1_send.at[o], p1_recv.at[o], plane(cy + o, cx, core))

    each(1, 4, lambda o: p0(o).start())
    each(1, 4, lambda o: p1(o).start())

    a_high, a_low = halves(a_ref[...])
    for n in range(4):
        lane = lax.broadcasted_iota(jnp.int32, (1, 256), 1)
        source = jnp.where(lane % 32 < NA, NA * (8 * n + lane // 32) + lane % 32, -1)
        respace = jnp.where(lax.broadcasted_iota(jnp.int32, (NV, 256), 0) == source, 1.0, 0.0).astype(BF16)
        spaced[:, n * 256:(n + 1) * 256] = nn(a_high, respace) + nn(a_low, respace)

    def d_copy(d):
        return remote(moved.at[d], dbuf.at[me], d_send.at[d], d_recv.at[me], (d, mz))

    def d_start(d):
        @pl.when(d != me)
        def _():
            d_copy(d).start()

    def d_tile(step):
        return (me // 4 + step) % 8

    small = lax.broadcasted_iota(jnp.int32, (CPAD, 128), 1)

    def shuffle(step, c):
        tile = d_tile(step)
        at = pl.ds(pl.multiple_of(tile * 128, 128), 128)
        blocks = [spaced[m * CPAD:(m + 1) * CPAD, at] for m in range(NI * NK)]
        for part in range(4):
            for t in range(3):
                held = jnp.zeros((CPAD, 128), F32)
                here = blocks[6 * t:6 * t + 6]
                for n, block in enumerate(here):
                    shift = (PITCH * n - 32 * part) % 128
                    turned = pltpu.roll(block, shift, 1) if shift else block
                    held = jnp.where((small >= PITCH * n) & (small < PITCH * n + NA), turned, held)
                moved[4 * tile + part, :, t * 128:(t + 1) * 128] = held[:NA]

        @pl.when(step > 0)
        def _():
            each(0, 4, lambda n: d_start(4 * d_tile(step + 7) + n))

        return c

    lax.fori_loop(0, 8, shuffle, 0)
    each(0, 4, lambda n: d_start(4 * d_tile(7) + n))
    dbuf[me] = moved[me]

    def q0(o, late):
        ref = gh0.at[cy, core, pl.ds(2 * abs(o - late), 2)]
        return remote(ref, ref, q0_send.at[2 * late + o], q0_recv.at[2 * late + o], plane(cy + 1 - 2 * o, cx, core))

    def q1(o, late):
        ref = gh1.at[cx, core, pl.ds(2 * abs(o - late), 2)]
        return remote(ref, ref, q1_send.at[2 * late + o], q1_recv.at[2 * late + o], plane(cy, cx + 1 - 2 * o, core))

    def r0(o):
        row = (cy + 3 + 2 * o) % 4
        part = pl.ds(2 * o, 2)
        ref = gh0.at[row, core, part]
        return remote(ref, ref, q0_send.at[4 + o], q0_recv.at[4 + o], plane(cy + 1 - 2 * o, cx, core))

    def r1(o):
        row = (cx + 3 + 2 * o) % 4
        part = pl.ds(2 * o, 2)
        ref = gh1.at[row, core, part]
        return remote(ref, ref, q1_send.at[4 + o], q1_recv.at[4 + o], plane(cy, cx + 1 - 2 * o, core))

    sibling = plane(cy, cx, 1 - core)

    def order(n):
        return n + n // 2 - 2 * (n // 3)

    def s0(n):
        ref = gh0.at[(cy + order(n)) % 4, core]
        return remote(ref, ref, s0_send.at[n], s0_recv.at[n], sibling)

    def s1(n):
        ref = gh1.at[(cx + order(n)) % 4, core]
        return remote(ref, ref, s1_send.at[n], s1_recv.at[n], sibling)

    own0.wait()
    each(1, 4, lambda o: p0(o).wait_recv())
    q0(0, 0).start()
    q0(1, 0).start()
    q0(0, 1).start()
    q0(1, 1).start()
    s0(0).start()
    own1.wait()
    each(1, 4, lambda o: p1(o).wait_recv())
    q1(0, 0).start()
    q1(1, 0).start()
    q1(0, 1).start()
    q1(1, 1).start()
    s1(0).start()

    @pl.loop(0, 8)
    def _(n):
        row = lax.broadcasted_iota(jnp.int32, (NJ * CAP, GROUP), 0)
        ebuf[n] = jnp.where(row == row_ref[n] // 8, 1.0, 0.0).astype(BF16)

    high, low = halves(jnp.where(skiac_ref[...] == virt_ref[...], a_ref[...], 0.0))
    direct = nt(p_all, high) + nt(p_all, low)
    p_t = onehot(placed_ref[...])

    def d_wait(n):
        d = (me + n) % BLK
        remote(moved.at[d], dbuf.at[d], d_send.at[d], d_recv.at[d], (d, mz)).wait_recv()

    each(1, BLK, d_wait)
    for d in range(BLK):
        arrived[d * CPAD:d * CPAD + NA] = dbuf[d]
    swapped = jnp.where(irrc_ref[...] == skia_ref[...], arrived[...], 0.0)
    s_high, s_low = halves(swapped)
    s_t = nn(p_t, s_high) + nn(p_t, s_low)
    columns = []
    for k in range(NK):
        pairs = []
        for m in range(NI * k, NI * k + NI):
            first = 128 * (m // 6) + PITCH * (m % 6)
            pairs.append(2.0 * direct[:, m * CPAD:m * CPAD + NA] - s_t[:, first:first + NA])
        columns.append(jnp.concatenate(pairs, axis=1))
    w = jnp.concatenate(columns, axis=0)
    w = jnp.concatenate([w, jnp.zeros((NK * CAP, 128 - NI * NA), F32)], axis=1)
    w_high, w_low = halves(w)

    acc[...] = jnp.zeros_like(acc)

    def product(piece, n):
        g_high, g_low = halves(piece.reshape(GROUP, NK * CAP))
        r = nn(g_high, w_high) + (nn(g_high, w_low) + nn(g_low, w_high))
        r_high, r_low = halves(jnp.where(column_ref[n] % 8 == sia_ref[...], r, 0.0))
        acc[...] += nn(ebuf[n], r_high) + nn(ebuf[n], r_low)

    def product0(n):
        s0(n).wait_recv()
        row = (cy + order(n)) % 4
        product(gh0[row], row)

    def product1(n):
        s1(n).wait_recv()
        row = (cx + order(n)) % 4
        product(gh1[row], 4 + row)

    for o in (1, 0):
        q0(o, 0).wait_recv()
        r0(o).start()
        q1(o, 0).wait_recv()
        r1(o).start()
    for o in (1, 0):
        q0(o, 1).wait_recv()
        s0(2 - o).start()
        q1(o, 1).wait_recv()
        s1(2 - o).start()

    def products(n, c):
        @pl.when(n == 3)
        def _():
            r0(0).wait_recv()
            r0(1).wait_recv()
            s0(3).start()
            r1(0).wait_recv()
            r1(1).wait_recv()
            s1(3).start()

        product0(n)
        product1(n)
        return c

    lax.fori_loop(0, 4, products, 0)

    def z_copy(n):
        target = (mz + n) % INT
        return remote(zsend.at[target], zrecv.at[mz], z_send.at[n], z_recv.at[n], (me, target))

    def y_copy(n):
        target = (mz + n) % INT
        return remote(ysum, ygath.at[mz], y_send.at[n], y_recv.at[n], (me, target))

    turned = acc[...].T[:ROWS]
    for block in range(3):
        for group in range(5):
            zsend[block * 5 + group] = turned[group * 16:(group + 1) * 16, block * 128:(block + 1) * 128]
    zsend[15] = jnp.zeros((16, 128), F32)

    for n in FAR_FIRST:
        z_copy(n).start()
    zrecv[mz] = zsend[mz]
    each(1, INT, lambda n: z_copy(n).wait_recv())
    total = zrecv[0]
    for n in range(1, INT):
        total = total + zrecv[n]
    ysum[...] = total
    for n in FAR_FIRST:
        y_copy(n).start()
    ygath[mz] = total
    row = lax.broadcasted_iota(jnp.int32, (NJ * CAP, 256), 0)
    spread = jnp.where(row == rowz_ref[...] // 8, 1.0, 0.0).astype(BF16)
    each(1, INT, lambda n: y_copy(n).wait_recv())
    whole = jnp.concatenate(
        [jnp.concatenate([ygath[block * 5 + group] for group in range(5)], axis=0) for block in range(3)], axis=1
    )
    y_high, y_low = halves(whole)
    out = nn(y_high, spread) + nn(y_low, spread)
    out_ref[...] = jnp.where(siac_ref[...] == rowz_ref[...] % 8, out, 0.0)

    each(1, 4, lambda o: p0(o).wait_send())
    each(1, 4, lambda o: p1(o).wait_send())
    for o in range(2):
        q0(o, 0).wait_send()
        q0(o, 1).wait_send()
        q1(o, 0).wait_send()
        q1(o, 1).wait_send()
        r0(o).wait_send()
        r1(o).wait_send()
    for n in range(4):
        s0(n).wait_send()
        s1(n).wait_send()
    each(1, BLK, lambda n: d_copy((me + n) % BLK).wait_send())
    each(1, INT, lambda n: z_copy(n).wait_send())
    each(1, INT, lambda n: y_copy(n).wait_send())


def pad_to(x, shape, value=0):
    return jnp.pad(x, [(0, n - m) for n, m in zip(shape, x.shape)], constant_values=value)


def blocks_of_six(x, value):
    x = pad_to(x, (x.shape[0], 18, PITCH), value).reshape(-1, 3, 6 * PITCH)
    return pad_to(x, (x.shape[0], 3, 128), value).reshape(-1, 384)


def by_group(x):
    x = x.reshape(4, 4, 2, 2, HALF)
    first = jnp.transpose(x[:, :, :, 0], (0, 2, 1, 3)).reshape(4, GROUP)
    second = jnp.transpose(x[:, :, :, 1], (1, 2, 0, 3)).reshape(4, GROUP)
    return jnp.concatenate([first, second], axis=0)


def per_device(amplitudes, integrals, occ_irrep, virt_irrep, i_batch, j_batch):
    blk = lax.axis_index("blk")
    z = lax.axis_index("int")
    occ_k = lookup(occ_irrep, z * NK + jnp.arange(NK, dtype=jnp.int32))
    virt_irrep = lax.optimization_barrier(jnp.bitwise_and(virt_irrep, 7))
    virt_a = lax.dynamic_slice_in_dim(virt_irrep, blk * NA, NA)
    irr_i = lookup(occ_irrep, i_batch)
    irr_j = lookup(occ_irrep, j_batch)
    orbital = jnp.arange(NV, dtype=jnp.int32)
    alike = (virt_irrep[:, None] == virt_irrep[None, :]) & (orbital[None, :] < orbital[:, None])
    place = jnp.sum(alike.astype(jnp.int32), axis=1)
    s_ika = jnp.bitwise_xor(
        jnp.bitwise_xor(irr_i[:, None, None], occ_k[None, None, :]), virt_a[None, :, None]
    )
    a_rows = pad_to(jnp.transpose(amplitudes, (2, 0, 1, 3)), (NK, NI, CPAD, NV)).reshape(NK * NI * CPAD, NV)
    s_kia = jnp.transpose(s_ika, (2, 0, 1)).reshape(1, NK * NI, NA)
    s_kia_column = pad_to(s_kia, (1, NK * NI, CPAD), -2).reshape(NK * NI * CPAD, 1)
    s_kia = blocks_of_six(s_kia, -2)

    ints = jnp.transpose(integrals, (0, 3, 2, 1))
    s_kbj = jnp.bitwise_xor(
        jnp.bitwise_xor(occ_k[:, None, None], virt_a[None, :, None]), irr_j[None, None, :]
    )
    s_kbj = pad_to(s_kbj.reshape(NK, NA * NJ), (NK, ROWS), -2).reshape(NK, ROWS, 1)

    placed = pad_to(place.reshape(BLK, NA), (BLK, CPAD), -1).reshape(1, BLK * CPAD)
    irr_c = pad_to(virt_irrep.reshape(BLK, NA), (BLK, CPAD), -1).reshape(BLK * CPAD, 1)
    s_ia = jnp.bitwise_xor(irr_i[:, None], virt_a[None, :]).reshape(1, NI * NA)

    offset = 8 * CAP * jnp.arange(NJ, dtype=jnp.int32)
    pairs = 8 * place[:, None] + offset[None, :] + jnp.bitwise_xor(virt_irrep[:, None], irr_j[None, :])
    pairs = by_group(pad_to(pairs.reshape(BLK, NA * NJ), (BLK, ROWS), -1))
    virt_b = lax.dynamic_slice_in_dim(virt_irrep, z * NB, NB)
    place_b = lax.dynamic_slice_in_dim(place, z * NB, NB)
    row_z = 8 * place_b[None, :] + offset[:, None] + jnp.bitwise_xor(irr_j[:, None], virt_b[None, :])
    row_z = pad_to(row_z.reshape(1, NJ * NB), (1, 256), -1)

    vmem = pl.BlockSpec(memory_space=pltpu.VMEM)
    dma = pltpu.SemaphoreType.DMA
    out = pl.pallas_call(
        kernel,
        out_shape=jax.ShapeDtypeStruct((ROWS, 256), F32),
        in_specs=[vmem] * 14,
        out_specs=vmem,
        scratch_shapes=[
            pltpu.VMEM((ROWS, NK * CAP), F32),
            pltpu.VMEM((NK, ROWS, NV), F32),
            pltpu.VMEM((4, 2, 4, HALF, NK * CAP), F32),
            pltpu.VMEM((4, 2, 4, HALF, NK * CAP), F32),
            pltpu.VMEM((NI * NK * CPAD, 1024), F32),
            pltpu.VMEM((BLK, NA, 384), F32),
            pltpu.VMEM((BLK, NA, 384), F32),
            pltpu.VMEM((BLK * CPAD, 384), F32),
            pltpu.VMEM((8, NJ * CAP, GROUP), BF16),
            pltpu.VMEM((NJ * CAP, 128), F32),
            pltpu.VMEM((INT, 16, 128), F32),
            pltpu.VMEM((INT, 16, 128), F32),
            pltpu.VMEM((16, 128), F32),
            pltpu.VMEM((INT, 16, 128), F32),
            dma((2,)), dma((4,)), dma((4,)), dma((4,)), dma((4,)), dma((6,)), dma((6,)), dma((6,)), dma((6,)),
            dma((4,)), dma((4,)), dma((4,)), dma((4,)), dma((BLK,)), dma((BLK,)),
            dma((INT,)), dma((INT,)), dma((INT,)), dma((INT,)),
        ],
        compiler_params=pltpu.CompilerParams(
            collective_id=0, has_side_effects=True, vmem_limit_bytes=48 * 1024 * 1024
        ),
    )(
        ints, s_kbj, a_rows, s_kia_column, virt_irrep.reshape(1, NV), place.reshape(1, NV), placed, irr_c, s_kia,
        pairs.reshape(8, 1, GROUP), pairs.reshape(8, GROUP, 1), pad_to(s_ia, (1, 128), -2), row_z,
        pad_to(s_ia, (1, ROWS), -2).reshape(ROWS, 1),
    )
    return out[:NI * NA, :NJ * NB].reshape(NI, NA, NJ, NB)


def solution(mesh):
    placed = (P(None, "blk", "int", None), P("int", None, None, "blk"), P(), P(), P(), P())
    return jax.shard_map(
        per_device,
        mesh=mesh,
        in_specs=placed,
        out_specs=P(None, "blk", None, "int"),
        check_vma=False,
    )
```

```python
import jax
import jax.numpy as jnp
import numpy as np
from jax import lax
from jax.experimental import pallas as pl
from jax.experimental.pallas import tpu as pltpu
from jax.sharding import PartitionSpec as P

MESH = pl.DeviceIdType.MESH
F32 = jnp.float32
BF16 = jnp.bfloat16
CAP = 96
NI = 4
NJ = 4
NA = 19
NK = 4
NB = 38
NV = 608
BLK = 32
INT = 16
ROWS = 80
CPAD = 24
HALF = 40
GROUP = 320
FAR_FIRST = (8, 7, 9, 6, 10, 5, 11, 4, 12, 3, 13, 2, 14, 1, 15)
PITCH = 21


def halves(x):
    high = x.astype(BF16)
    return high, (x - high.astype(F32)).astype(BF16)


def nn(a, b):
    return jnp.dot(a, b, preferred_element_type=F32)


def nt(a, b):
    return lax.dot_general(a, b, (((1,), (1,)), ((), ())), preferred_element_type=F32)


def kernel(
    int_ref, a_ref, virt_ref, index_ref, pair_ref, occ_ref, i_ref, j_ref,
    out_ref,
    g_ref, g_rows, column_buf, gh0, gh1, spaced, moved, dbuf, arrived, ebuf, acc, zsend, zrecv, ysum, ygath,
    own_sem, p0_send, p0_recv, p1_send, p1_recv, q0_send, q0_recv, q1_send, q1_recv,
    s0_send, s0_recv, s1_send, s1_recv, d_send, d_recv, z_send, z_recv, y_send, y_recv,
):
    me = lax.axis_index("blk")
    mz = lax.axis_index("int")
    core = me % 2
    cx = (me // 2) % 4
    cy = me // 8

    def plane(y, x, c):
        return ((((y + 4) % 4) * 4 + (x + 4) % 4) * 2 + c, mz)

    def each(first, last, do):
        def body(n, c):
            do(n)
            return c

        lax.fori_loop(first, last, body, 0)

    def remote(src, dst, send, recv, device):
        return pltpu.make_async_remote_copy(
            src_ref=src, dst_ref=dst, send_sem=send, recv_sem=recv, device_id=device, device_id_type=MESH
        )

    barrier = pltpu.get_barrier_semaphore()

    def greet(device):
        pl.semaphore_signal(barrier, inc=1, device_id=device, device_id_type=MESH)

    each(1, INT, lambda n: greet((me, (mz + n) % INT)))
    each(1, BLK, lambda n: greet(((me + n) % BLK, mz)))

    own0 = pltpu.make_async_copy(g_ref.at[pl.ds(0, HALF)], gh0.at[cy, core, cx], own_sem.at[0])
    own1 = pltpu.make_async_copy(g_ref.at[pl.ds(HALF, HALF)], gh1.at[cx, core, cy], own_sem.at[1])

    irr_i = [occ_ref[i_ref[i]] for i in range(NI)]
    irr_j = [occ_ref[j_ref[j]] for j in range(NJ)]
    occ_k = [occ_ref[mz * NK + k] for k in range(NK)]
    virt = virt_ref[...]

    label = lax.broadcasted_iota(jnp.int32, (16, NV), 0)
    mine = jnp.where(label == virt, 1.0, 0.0)
    earlier = lax.broadcasted_iota(jnp.int32, (NV, NV), 0) < lax.broadcasted_iota(jnp.int32, (NV, NV), 1)
    counts = nn(mine.astype(BF16), jnp.where(earlier, 1.0, 0.0).astype(BF16))
    place = jnp.sum(mine * counts, axis=0, keepdims=True)
    both = jnp.where(label == 0, virt.astype(F32), jnp.where(label == 1, place, 0.0)).astype(BF16)

    def look(index):
        chosen = lax.broadcasted_iota(jnp.int32, (NV, index.shape[1]), 0) == index
        found = nn(both, jnp.where(chosen, 1.0, 0.0).astype(BF16))
        return found[0:1].astype(jnp.int32), found[1:2].astype(jnp.int32)

    def pick(values, which):
        out = jnp.zeros_like(which)
        for n, value in enumerate(values):
            out = jnp.where(which == n, value, out)
        return out

    def turn(row):
        return jnp.broadcast_to(row.astype(F32), (8, row.shape[1])).T[:, 0:1].astype(jnp.int32)

    def constant(n, lanes):
        return index_ref[n:n + 1, 0:lanes]

    def own_label(n, lanes):
        offset = constant(n, lanes)
        return offset >= 0, look(me * NA + offset)[0]

    def onehot(places):
        row = lax.broadcasted_iota(jnp.int32, (CAP, places.shape[1]), 0)
        return jnp.where(row == places, 1.0, 0.0).astype(BF16)

    p_all = onehot(place.astype(jnp.int32))
    valid, s_bj = own_label(5, 128)
    s_bj = jnp.bitwise_xor(s_bj, pick(irr_j, constant(6, 128)))
    for k in range(NK):
        for b in range(NA):
            g_rows[k, b * NJ:(b + 1) * NJ] = int_ref[k, b]
        g_rows[k, NA * NJ:] = jnp.zeros((ROWS - NA * NJ, NV), F32)
    packed = []
    for k in range(NK):
        high, low = halves(jnp.where(turn(jnp.where(valid, jnp.bitwise_xor(s_bj, occ_k[k]), -2))[:ROWS] == virt, g_rows[k], 0.0))
        packed.append(nt(high, p_all) + nt(low, p_all))
    g_ref[...] = jnp.concatenate(packed, axis=1)
    pl.semaphore_wait(barrier, BLK - 1 + INT - 1)

    own0.start()
    own1.start()

    def p0(o):
        return remote(g_ref.at[pl.ds(0, HALF)], gh0.at[cy, core, cx], p0_send.at[o], p0_recv.at[o], plane(cy, cx + o, core))

    def p1(o):
        return remote(g_ref.at[pl.ds(HALF, HALF)], gh1.at[cx, core, cy], p1_send.at[o], p1_recv.at[o], plane(cy + o, cx, core))

    each(1, 4, lambda o: p0(o).start())
    each(1, 4, lambda o: p1(o).start())

    a_high, a_low = halves(a_ref[...])
    for n in range(4):
        lane = lax.broadcasted_iota(jnp.int32, (1, 256), 1)
        source = jnp.where(lane % 32 < NA, NA * (8 * n + lane // 32) + lane % 32, -1)
        respace = jnp.where(lax.broadcasted_iota(jnp.int32, (NV, 256), 0) == source, 1.0, 0.0).astype(BF16)
        spaced[:, n * 256:(n + 1) * 256] = nn(a_high, respace) + nn(a_low, respace)

    def d_copy(d):
        return remote(moved.at[d], dbuf.at[me], d_send.at[d], d_recv.at[me], (d, mz))

    def d_start(d):
        @pl.when(d != me)
        def _():
            d_copy(d).start()

    def d_tile(step):
        return (me // 4 + step) % 8

    small = lax.broadcasted_iota(jnp.int32, (CPAD, 128), 1)

    def shuffle(step, c):
        tile = d_tile(step)
        at = pl.ds(pl.multiple_of(tile * 128, 128), 128)
        blocks = [spaced[m * CPAD:(m + 1) * CPAD, at] for m in range(NI * NK)]
        for part in range(4):
            for t in range(3):
                held = jnp.zeros((CPAD, 128), F32)
                here = blocks[6 * t:6 * t + 6]
                for n, block in enumerate(here):
                    shift = (PITCH * n - 32 * part) % 128
                    turned = pltpu.roll(block, shift, 1) if shift else block
                    held = jnp.where((small >= PITCH * n) & (small < PITCH * n + NA), turned, held)
                moved[4 * tile + part, :, t * 128:(t + 1) * 128] = held[:NA]

        @pl.when(step > 0)
        def _():
            each(0, 4, lambda n: d_start(4 * d_tile(step + 7) + n))

        return c

    lax.fori_loop(0, 8, shuffle, 0)
    each(0, 4, lambda n: d_start(4 * d_tile(7) + n))
    dbuf[me] = moved[me]

    def q0(o, late):
        ref = gh0.at[cy, core, pl.ds(2 * abs(o - late), 2)]
        return remote(ref, ref, q0_send.at[2 * late + o], q0_recv.at[2 * late + o], plane(cy + 1 - 2 * o, cx, core))

    def q1(o, late):
        ref = gh1.at[cx, core, pl.ds(2 * abs(o - late), 2)]
        return remote(ref, ref, q1_send.at[2 * late + o], q1_recv.at[2 * late + o], plane(cy, cx + 1 - 2 * o, core))

    def r0(o):
        row = (cy + 3 + 2 * o) % 4
        part = pl.ds(2 * o, 2)
        ref = gh0.at[row, core, part]
        return remote(ref, ref, q0_send.at[4 + o], q0_recv.at[4 + o], plane(cy + 1 - 2 * o, cx, core))

    def r1(o):
        row = (cx + 3 + 2 * o) % 4
        part = pl.ds(2 * o, 2)
        ref = gh1.at[row, core, part]
        return remote(ref, ref, q1_send.at[4 + o], q1_recv.at[4 + o], plane(cy, cx + 1 - 2 * o, core))

    sibling = plane(cy, cx, 1 - core)

    def order(n):
        return n + n // 2 - 2 * (n // 3)

    def s0(n):
        ref = gh0.at[(cy + order(n)) % 4, core]
        return remote(ref, ref, s0_send.at[n], s0_recv.at[n], sibling)

    def s1(n):
        ref = gh1.at[(cx + order(n)) % 4, core]
        return remote(ref, ref, s1_send.at[n], s1_recv.at[n], sibling)

    own0.wait()
    each(1, 4, lambda o: p0(o).wait_recv())
    q0(0, 0).start()
    q0(1, 0).start()
    q0(0, 1).start()
    q0(1, 1).start()
    s0(0).start()
    own1.wait()
    each(1, 4, lambda o: p1(o).wait_recv())
    q1(0, 0).start()
    q1(1, 0).start()
    q1(0, 1).start()
    q1(1, 1).start()
    s1(0).start()

    @pl.loop(0, 8)
    def _(n):
        row = lax.broadcasted_iota(jnp.int32, (NJ * CAP, GROUP), 0)
        orbital = pair_ref[n, 0:1]
        which = pair_ref[n, 1:2]
        irrep, at = look(orbital)
        at = jnp.where(orbital >= 0, at + CAP * which, -1)
        ebuf[n] = jnp.where(row == at[:, :GROUP], 1.0, 0.0).astype(BF16)
        column_buf[n] = turn(jnp.bitwise_xor(irrep, pick(irr_j, which)))[:GROUP]

    def s_kia(n):
        good, irrep = own_label(n, 384)
        m = constant(n + 1, 384)
        irrep = jnp.bitwise_xor(irrep, pick([irr_i[i] for k in range(NK) for i in range(NI)], m))
        irrep = jnp.bitwise_xor(irrep, pick([occ_k[k] for k in range(NK) for i in range(NI)], m))
        return jnp.where(good, irrep, -2)

    high, low = halves(jnp.where(turn(s_kia(1)) == virt, a_ref[...], 0.0))
    direct = nt(p_all, high) + nt(p_all, low)
    orbital = constant(0, BLK * CPAD)
    irrep, at = look(orbital)
    p_t = onehot(jnp.where(orbital >= 0, at, -1))
    irrep_c = turn(jnp.where(orbital >= 0, irrep, -1))
    s_row = s_kia(3)
    good, s_ia = own_label(7, 128)
    s_ia = jnp.where(good, jnp.bitwise_xor(s_ia, pick(irr_i, constant(8, 128))), -2)
    s_ia_column = turn(s_ia)[:ROWS]
    offset = constant(9, 256)
    which = constant(10, 256)
    s_jb, at_z = look(mz * NB + offset)
    s_jb = jnp.where(offset >= 0, jnp.bitwise_xor(s_jb, pick(irr_j, which)), -1)
    at_z = jnp.where(offset >= 0, at_z + CAP * which, -1)

    def d_wait(n):
        d = (me + n) % BLK
        remote(moved.at[d], dbuf.at[d], d_send.at[d], d_recv.at[d], (d, mz)).wait_recv()

    each(1, BLK, d_wait)
    for d in range(BLK):
        arrived[d * CPAD:d * CPAD + NA] = dbuf[d]
    swapped = jnp.where(irrep_c == s_row, arrived[...], 0.0)
    s_high, s_low = halves(swapped)
    s_t = nn(p_t, s_high) + nn(p_t, s_low)
    columns = []
    for k in range(NK):
        pairs = []
        for m in range(NI * k, NI * k + NI):
            first = 128 * (m // 6) + PITCH * (m % 6)
            pairs.append(2.0 * direct[:, m * CPAD:m * CPAD + NA] - s_t[:, first:first + NA])
        columns.append(jnp.concatenate(pairs, axis=1))
    w = jnp.concatenate(columns, axis=0)
    w = jnp.concatenate([w, jnp.zeros((NK * CAP, 128 - NI * NA), F32)], axis=1)
    w_high, w_low = halves(w)

    acc[...] = jnp.zeros_like(acc)

    def product(piece, n):
        g_high, g_low = halves(piece.reshape(GROUP, NK * CAP))
        r = nn(g_high, w_high) + (nn(g_high, w_low) + nn(g_low, w_high))
        r_high, r_low = halves(jnp.where(column_buf[n] == s_ia, r, 0.0))
        acc[...] += nn(ebuf[n], r_high) + nn(ebuf[n], r_low)

    def product0(n):
        s0(n).wait_recv()
        row = (cy + order(n)) % 4
        product(gh0[row], row)

    def product1(n):
        s1(n).wait_recv()
        row = (cx + order(n)) % 4
        product(gh1[row], 4 + row)

    for o in (1, 0):
        q0(o, 0).wait_recv()
        r0(o).start()
        q1(o, 0).wait_recv()
        r1(o).start()
    for o in (1, 0):
        q0(o, 1).wait_recv()
        s0(2 - o).start()
        q1(o, 1).wait_recv()
        s1(2 - o).start()

    def products(n, c):
        @pl.when(n == 3)
        def _():
            r0(0).wait_recv()
            r0(1).wait_recv()
            s0(3).start()
            r1(0).wait_recv()
            r1(1).wait_recv()
            s1(3).start()

        product0(n)
        product1(n)
        return c

    lax.fori_loop(0, 4, products, 0)

    def z_copy(n):
        target = (mz + n) % INT
        return remote(zsend.at[target], zrecv.at[mz], z_send.at[n], z_recv.at[n], (me, target))

    def y_copy(n):
        target = (mz + n) % INT
        return remote(ysum, ygath.at[mz], y_send.at[n], y_recv.at[n], (me, target))

    turned = acc[...].T[:ROWS]
    for block in range(3):
        for group in range(5):
            zsend[block * 5 + group] = turned[group * 16:(group + 1) * 16, block * 128:(block + 1) * 128]
    zsend[15] = jnp.zeros((16, 128), F32)

    for n in FAR_FIRST:
        z_copy(n).start()
    zrecv[mz] = zsend[mz]
    each(1, INT, lambda n: z_copy(n).wait_recv())
    total = zrecv[0]
    for n in range(1, INT):
        total = total + zrecv[n]
    ysum[...] = total
    for n in FAR_FIRST:
        y_copy(n).start()
    ygath[mz] = total
    row = lax.broadcasted_iota(jnp.int32, (NJ * CAP, 256), 0)
    spread = jnp.where(row == at_z, 1.0, 0.0).astype(BF16)
    each(1, INT, lambda n: y_copy(n).wait_recv())
    whole = jnp.concatenate(
        [jnp.concatenate([ygath[block * 5 + group] for group in range(5)], axis=0) for block in range(3)], axis=1
    )
    y_high, y_low = halves(whole)
    out = nn(y_high, spread) + nn(y_low, spread)
    out_ref[...] = jnp.where(s_ia_column == s_jb, out, 0.0)

    each(1, 4, lambda o: p0(o).wait_send())
    each(1, 4, lambda o: p1(o).wait_send())
    for o in range(2):
        q0(o, 0).wait_send()
        q0(o, 1).wait_send()
        q1(o, 0).wait_send()
        q1(o, 1).wait_send()
        r0(o).wait_send()
        r1(o).wait_send()
    for n in range(4):
        s0(n).wait_send()
        s1(n).wait_send()
    each(1, BLK, lambda n: d_copy((me + n) % BLK).wait_send())
    each(1, INT, lambda n: z_copy(n).wait_send())
    each(1, INT, lambda n: y_copy(n).wait_send())


def pad_to(x, shape, value=0):
    return jnp.pad(x, [(0, n - m) for n, m in zip(shape, x.shape)], constant_values=value)


def index_tables():
    far = -100000
    table = np.full((16, BLK * CPAD), far, np.int32)
    lane = np.arange(BLK * CPAD)
    table[0] = np.where(lane % CPAD < NA, NA * (lane // CPAD) + lane % CPAD, -1)
    lane = np.arange(384)
    table[1, :384] = np.where(lane % CPAD < NA, lane % CPAD, far)
    table[2, :384] = lane // CPAD
    m = 6 * (lane // 128) + lane % 128 // PITCH
    a = lane % 128 % PITCH
    table[3, :384] = np.where((a < NA) & (lane % 128 < 6 * PITCH) & (m < NI * NK), a, far)
    table[4, :384] = m
    lane = np.arange(NA * NJ)
    table[5, :NA * NJ] = lane // NJ
    table[6, :NA * NJ] = lane % NJ
    table[7, :NI * NA] = lane % NA
    table[8, :NI * NA] = lane // NA
    lane = np.arange(NJ * NB)
    table[9, :NJ * NB] = lane % NB
    table[10, :NJ * NB] = lane // NB
    pairs = np.full((8, 2, 384), -1, np.int32)
    lane = np.arange(GROUP)
    core, other, row = lane // (4 * HALF), lane // HALF % 4, lane % HALF
    for n in range(8):
        y, x = (n, other) if n < 4 else (other, n - 4)
        n_row = row + HALF * (n // 4)
        good = n_row < NA * NJ
        pairs[n, 0, :GROUP] = np.where(good, ((y * 4 + x) * 2 + core) * NA + n_row // NJ, -1)
        pairs[n, 1, :GROUP] = n_row % NJ
    return table, pairs


def per_device(amplitudes, integrals, occ_irrep, virt_irrep, i_batch, j_batch):
    a_rows = pad_to(jnp.transpose(amplitudes, (2, 0, 1, 3)), (NK, NI, CPAD, NV)).reshape(NK * NI * CPAD, NV)
    ints = jnp.transpose(integrals, (0, 3, 2, 1))
    table, pairs = index_tables()

    vmem = pl.BlockSpec(memory_space=pltpu.VMEM)
    dma = pltpu.SemaphoreType.DMA
    out = pl.pallas_call(
        kernel,
        out_shape=jax.ShapeDtypeStruct((ROWS, 256), F32),
        in_specs=[vmem] * 5 + [pl.BlockSpec(memory_space=pltpu.SMEM)] * 3,
        out_specs=vmem,
        scratch_shapes=[
            pltpu.VMEM((ROWS, NK * CAP), F32),
            pltpu.VMEM((NK, ROWS, NV), F32),
            pltpu.VMEM((8, GROUP, 1), jnp.int32),
            pltpu.VMEM((4, 2, 4, HALF, NK * CAP), F32),
            pltpu.VMEM((4, 2, 4, HALF, NK * CAP), F32),
            pltpu.VMEM((NI * NK * CPAD, 1024), F32),
            pltpu.VMEM((BLK, NA, 384), F32),
            pltpu.VMEM((BLK, NA, 384), F32),
            pltpu.VMEM((BLK * CPAD, 384), F32),
            pltpu.VMEM((8, NJ * CAP, GROUP), BF16),
            pltpu.VMEM((NJ * CAP, 128), F32),
            pltpu.VMEM((INT, 16, 128), F32),
            pltpu.VMEM((INT, 16, 128), F32),
            pltpu.VMEM((16, 128), F32),
            pltpu.VMEM((INT, 16, 128), F32),
            dma((2,)), dma((4,)), dma((4,)), dma((4,)), dma((4,)), dma((6,)), dma((6,)), dma((6,)), dma((6,)),
            dma((4,)), dma((4,)), dma((4,)), dma((4,)), dma((BLK,)), dma((BLK,)),
            dma((INT,)), dma((INT,)), dma((INT,)), dma((INT,)),
        ],
        compiler_params=pltpu.CompilerParams(
            collective_id=0, has_side_effects=True, vmem_limit_bytes=48 * 1024 * 1024
        ),
    )(
        ints, a_rows, virt_irrep.reshape(1, NV), jnp.asarray(table), jnp.asarray(pairs), occ_irrep, i_batch, j_batch
    )
    return out[:NI * NA, :NJ * NB].reshape(NI, NA, NJ, NB)


def solution(mesh):
    placed = (P(None, "blk", "int", None), P("int", None, None, "blk"), P(), P(), P(), P())
    return jax.shard_map(
        per_device,
        mesh=mesh,
        in_specs=placed,
        out_specs=P(None, "blk", None, "int"),
        check_vma=False,
    )
```

```python
import jax
import jax.numpy as jnp
import numpy as np
from jax import lax
from jax.experimental import pallas as pl
from jax.experimental.pallas import tpu as pltpu
from jax.sharding import PartitionSpec as P

MESH = pl.DeviceIdType.MESH
F32 = jnp.float32
BF16 = jnp.bfloat16
CAP = 96
NI = 4
NJ = 4
NA = 19
NK = 4
NB = 38
NV = 608
BLK = 32
INT = 16
ROWS = 80
CPAD = 24
HALF = 40
GROUP = 320
FAR_FIRST = (8, 7, 9, 6, 10, 5, 11, 4, 12, 3, 13, 2, 14, 1, 15)
PITCH = 21


def halves(x):
    high = x.astype(BF16)
    return high, (x - high.astype(F32)).astype(BF16)


def nn(a, b):
    return jnp.dot(a, b, preferred_element_type=F32)


def nt(a, b):
    return lax.dot_general(a, b, (((1,), (1,)), ((), ())), preferred_element_type=F32)


def kernel(
    int_ref, a_ref, virt_ref, index_ref, pair_ref, occ_ref, i_ref, j_ref,
    out_ref,
    g_ref, g_rows, column_buf, gh0, gh1, spaced, moved, dbuf, arrived, ebuf, acc, zsend, zrecv, ysum, ygath,
    own_sem, p0_send, p0_recv, p1_send, p1_recv, q0_send, q0_recv, q1_send, q1_recv,
    s0_send, s0_recv, s1_send, s1_recv, d_send, d_recv, z_send, z_recv, y_send, y_recv,
):
    me = lax.axis_index("blk")
    mz = lax.axis_index("int")
    core = me % 2
    cx = (me // 2) % 4
    cy = me // 8

    def plane(y, x, c):
        return ((((y + 4) % 4) * 4 + (x + 4) % 4) * 2 + c, mz)

    def each(first, last, do):
        def body(n, c):
            do(n)
            return c

        lax.fori_loop(first, last, body, 0)

    def remote(src, dst, send, recv, device):
        return pltpu.make_async_remote_copy(
            src_ref=src, dst_ref=dst, send_sem=send, recv_sem=recv, device_id=device, device_id_type=MESH
        )

    barrier = pltpu.get_barrier_semaphore()

    def greet(device):
        pl.semaphore_signal(barrier, inc=1, device_id=device, device_id_type=MESH)

    each(1, INT, lambda n: greet((me, (mz + n) % INT)))
    each(1, BLK, lambda n: greet(((me + n) % BLK, mz)))

    own0 = pltpu.make_async_copy(g_ref.at[pl.ds(0, HALF)], gh0.at[cy, core, cx], own_sem.at[0])
    own1 = pltpu.make_async_copy(g_ref.at[pl.ds(HALF, HALF)], gh1.at[cx, core, cy], own_sem.at[1])

    irr_i = [occ_ref[i_ref[i]] for i in range(NI)]
    irr_j = [occ_ref[j_ref[j]] for j in range(NJ)]
    occ_k = [occ_ref[mz * NK + k] for k in range(NK)]
    virt = virt_ref[...]

    label = lax.broadcasted_iota(jnp.int32, (16, NV), 0)
    mine = jnp.where(label == virt, 1.0, 0.0)
    earlier = lax.broadcasted_iota(jnp.int32, (NV, NV), 0) < lax.broadcasted_iota(jnp.int32, (NV, NV), 1)
    counts = nn(mine.astype(BF16), jnp.where(earlier, 1.0, 0.0).astype(BF16))
    place = jnp.sum(mine * counts, axis=0, keepdims=True)
    both = jnp.where(label == 0, virt.astype(F32), jnp.where(label == 1, place, 0.0)).astype(BF16)

    def look(index):
        chosen = lax.broadcasted_iota(jnp.int32, (NV, index.shape[1]), 0) == index
        found = nn(both, jnp.where(chosen, 1.0, 0.0).astype(BF16))
        return found[0:1].astype(jnp.int32), found[1:2].astype(jnp.int32)

    def pick(values, which):
        out = jnp.zeros_like(which)
        for n, value in enumerate(values):
            out = jnp.where(which == n, value, out)
        return out

    def turn(row):
        return jnp.broadcast_to(row.astype(F32), (8, row.shape[1])).T[:, 0:1].astype(jnp.int32)

    def constant(n, lanes):
        return index_ref[n:n + 1, 0:lanes]

    def own_label(n, lanes):
        offset = constant(n, lanes)
        return offset >= 0, look(me * NA + offset)[0]

    def onehot(places):
        row = lax.broadcasted_iota(jnp.int32, (CAP, places.shape[1]), 0)
        return jnp.where(row == places, 1.0, 0.0).astype(BF16)

    p_all = onehot(place.astype(jnp.int32))
    valid, s_bj = own_label(5, 128)
    s_bj = jnp.bitwise_xor(s_bj, pick(irr_j, constant(6, 128)))
    for k in range(NK):
        for b in range(NA):
            g_rows[k, b * NJ:(b + 1) * NJ] = int_ref[k, b]
        g_rows[k, NA * NJ:] = jnp.zeros((ROWS - NA * NJ, NV), F32)
    packed = []
    for k in range(NK):
        high, low = halves(jnp.where(turn(jnp.where(valid, jnp.bitwise_xor(s_bj, occ_k[k]), -2))[:ROWS] == virt, g_rows[k], 0.0))
        packed.append(nt(high, p_all) + nt(low, p_all))
    g_ref[...] = jnp.concatenate(packed, axis=1)
    pl.semaphore_wait(barrier, BLK - 1 + INT - 1)

    own0.start()
    own1.start()

    def p0(o):
        return remote(g_ref.at[pl.ds(0, HALF)], gh0.at[cy, core, cx], p0_send.at[o], p0_recv.at[o], plane(cy, cx + o, core))

    def p1(o):
        return remote(g_ref.at[pl.ds(HALF, HALF)], gh1.at[cx, core, cy], p1_send.at[o], p1_recv.at[o], plane(cy + o, cx, core))

    each(1, 4, lambda o: p0(o).start())
    each(1, 4, lambda o: p1(o).start())

    a_high, a_low = halves(a_ref[...])
    for n in range(4):
        lane = lax.broadcasted_iota(jnp.int32, (1, 256), 1)
        source = jnp.where(lane % 32 < NA, NA * (8 * n + lane // 32) + lane % 32, -1)
        respace = jnp.where(lax.broadcasted_iota(jnp.int32, (NV, 256), 0) == source, 1.0, 0.0).astype(BF16)
        spaced[:, n * 256:(n + 1) * 256] = nn(a_high, respace) + nn(a_low, respace)

    def d_copy(d):
        return remote(moved.at[d], dbuf.at[me], d_send.at[d], d_recv.at[me], (d, mz))

    def d_start(d):
        @pl.when(d != me)
        def _():
            d_copy(d).start()

    def d_tile(step):
        return (me // 4 + step) % 8

    small = lax.broadcasted_iota(jnp.int32, (CPAD, 128), 1)

    def shuffle(step, c):
        tile = d_tile(step)
        at = pl.ds(pl.multiple_of(tile * 128, 128), 128)
        blocks = [spaced[m * CPAD:(m + 1) * CPAD, at] for m in range(NI * NK)]
        for part in range(4):
            d = 4 * tile + part
            lasts = []
            for t in range(3):
                held = jnp.zeros((CPAD, 128), F32)
                here = blocks[6 * t:6 * t + 6]
                for n, block in enumerate(here):
                    shift = (PITCH * n - 32 * part) % 128
                    turned = pltpu.roll(block, shift, 1) if shift else block
                    held = jnp.where((small >= PITCH * n) & (small < PITCH * n + NA), turned, held)
                last = held[16:]
                if t == 2:
                    packed_rows = jnp.concatenate([pltpu.roll(last, 84, 1)[:3], pltpu.roll(last, 42, 1)[:5]], axis=0)
                    top = jnp.where(small[:8] >= 84, packed_rows, held[:8])
                    moved[d, 32:40] = top
                    moved[d, 40:48] = held[8:16]
                else:
                    moved[d, 16 * t:16 * t + 16] = held[:16]
                    lasts.append(last)
            moved[d, 48:56] = jnp.concatenate([lasts[0][:3], lasts[1][:5]], axis=0)

        @pl.when(step > 0)
        def _():
            each(0, 4, lambda n: d_start(4 * d_tile(step + 7) + n))

        return c

    lax.fori_loop(0, 8, shuffle, 0)
    each(0, 4, lambda n: d_start(4 * d_tile(7) + n))
    dbuf[me] = moved[me]

    def q0(o, late):
        ref = gh0.at[cy, core, pl.ds(2 * abs(o - late), 2)]
        return remote(ref, ref, q0_send.at[2 * late + o], q0_recv.at[2 * late + o], plane(cy + 1 - 2 * o, cx, core))

    def q1(o, late):
        ref = gh1.at[cx, core, pl.ds(2 * abs(o - late), 2)]
        return remote(ref, ref, q1_send.at[2 * late + o], q1_recv.at[2 * late + o], plane(cy, cx + 1 - 2 * o, core))

    def r0(o):
        row = (cy + 3 + 2 * o) % 4
        part = pl.ds(2 * o, 2)
        ref = gh0.at[row, core, part]
        return remote(ref, ref, q0_send.at[4 + o], q0_recv.at[4 + o], plane(cy + 1 - 2 * o, cx, core))

    def r1(o):
        row = (cx + 3 + 2 * o) % 4
        part = pl.ds(2 * o, 2)
        ref = gh1.at[row, core, part]
        return remote(ref, ref, q1_send.at[4 + o], q1_recv.at[4 + o], plane(cy, cx + 1 - 2 * o, core))

    sibling = plane(cy, cx, 1 - core)

    def order(n):
        return n + n // 2 - 2 * (n // 3)

    def s0(n):
        ref = gh0.at[(cy + order(n)) % 4, core]
        return remote(ref, ref, s0_send.at[n], s0_recv.at[n], sibling)

    def s1(n):
        ref = gh1.at[(cx + order(n)) % 4, core]
        return remote(ref, ref, s1_send.at[n], s1_recv.at[n], sibling)

    own0.wait()
    each(1, 4, lambda o: p0(o).wait_recv())
    q0(0, 0).start()
    q0(1, 0).start()
    q0(0, 1).start()
    q0(1, 1).start()
    s0(0).start()
    own1.wait()
    each(1, 4, lambda o: p1(o).wait_recv())
    q1(0, 0).start()
    q1(1, 0).start()
    q1(0, 1).start()
    q1(1, 1).start()
    s1(0).start()

    @pl.loop(0, 8)
    def _(n):
        row = lax.broadcasted_iota(jnp.int32, (NJ * CAP, GROUP), 0)
        orbital = pair_ref[n, 0:1]
        which = pair_ref[n, 1:2]
        irrep, at = look(orbital)
        at = jnp.where(orbital >= 0, at + CAP * which, -1)
        ebuf[n] = jnp.where(row == at[:, :GROUP], 1.0, 0.0).astype(BF16)
        column_buf[n] = turn(jnp.bitwise_xor(irrep, pick(irr_j, which)))[:GROUP]

    def s_kia(n):
        good, irrep = own_label(n, 384)
        m = constant(n + 1, 384)
        irrep = jnp.bitwise_xor(irrep, pick([irr_i[i] for k in range(NK) for i in range(NI)], m))
        irrep = jnp.bitwise_xor(irrep, pick([occ_k[k] for k in range(NK) for i in range(NI)], m))
        return jnp.where(good, irrep, -2)

    high, low = halves(jnp.where(turn(s_kia(1)) == virt, a_ref[...], 0.0))
    direct = nt(p_all, high) + nt(p_all, low)
    orbital = constant(0, BLK * CPAD)
    irrep, at = look(orbital)
    p_t = onehot(jnp.where(orbital >= 0, at, -1))
    irrep_c = turn(jnp.where(orbital >= 0, irrep, -1))
    s_row = s_kia(3)
    good, s_ia = own_label(7, 128)
    s_ia = jnp.where(good, jnp.bitwise_xor(s_ia, pick(irr_i, constant(8, 128))), -2)
    s_ia_column = turn(s_ia)[:ROWS]
    offset = constant(9, 256)
    which = constant(10, 256)
    s_jb, at_z = look(mz * NB + offset)
    s_jb = jnp.where(offset >= 0, jnp.bitwise_xor(s_jb, pick(irr_j, which)), -1)
    at_z = jnp.where(offset >= 0, at_z + CAP * which, -1)

    def d_wait(n):
        d = (me + n) % BLK
        remote(moved.at[d], dbuf.at[d], d_send.at[d], d_recv.at[d], (d, mz)).wait_recv()

    each(1, BLK, d_wait)
    @pl.loop(0, BLK)
    def _(d):
        first = pl.multiple_of(d * CPAD, 8)
        for t in range(3):
            arrived[pl.ds(first, 16), t * 128:(t + 1) * 128] = dbuf[d, 16 * t:16 * t + 16]
        rest = dbuf[d, 48:56]
        arrived[pl.ds(first + 16, 8), 0:128] = rest
        arrived[pl.ds(first + 16, 8), 128:256] = jnp.concatenate([rest[3:6], rest[:5]], axis=0)
        top = dbuf[d, 32:40]
        below = jnp.concatenate([pltpu.roll(top, 86, 1)[3:6], top[:5]], axis=0)
        arrived[pl.ds(first + 16, 8), 256:384] = jnp.where(small[:8] < 2 * PITCH, pltpu.roll(top, 44, 1), below)

    swapped = jnp.where(irrep_c == s_row, arrived[...], 0.0)
    s_high, s_low = halves(swapped)
    s_t = nn(p_t, s_high) + nn(p_t, s_low)
    columns = []
    for k in range(NK):
        pairs = []
        for m in range(NI * k, NI * k + NI):
            first = 128 * (m // 6) + PITCH * (m % 6)
            pairs.append(2.0 * direct[:, m * CPAD:m * CPAD + NA] - s_t[:, first:first + NA])
        columns.append(jnp.concatenate(pairs, axis=1))
    w = jnp.concatenate(columns, axis=0)
    w = jnp.concatenate([w, jnp.zeros((NK * CAP, 128 - NI * NA), F32)], axis=1)
    w_high, w_low = halves(w)

    acc[...] = jnp.zeros_like(acc)

    def product(piece, n):
        g_high, g_low = halves(piece.reshape(GROUP, NK * CAP))
        r = nn(g_high, w_high) + (nn(g_high, w_low) + nn(g_low, w_high))
        r_high, r_low = halves(jnp.where(column_buf[n] == s_ia, r, 0.0))
        acc[...] += nn(ebuf[n], r_high) + nn(ebuf[n], r_low)

    def product0(n):
        s0(n).wait_recv()
        row = (cy + order(n)) % 4
        product(gh0[row], row)

    def product1(n):
        s1(n).wait_recv()
        row = (cx + order(n)) % 4
        product(gh1[row], 4 + row)

    for o in (1, 0):
        q0(o, 0).wait_recv()
        r0(o).start()
        q1(o, 0).wait_recv()
        r1(o).start()
    for o in (1, 0):
        q0(o, 1).wait_recv()
        s0(2 - o).start()
        q1(o, 1).wait_recv()
        s1(2 - o).start()

    def products(n, c):
        @pl.when(n == 3)
        def _():
            r0(0).wait_recv()
            r0(1).wait_recv()
            s0(3).start()
            r1(0).wait_recv()
            r1(1).wait_recv()
            s1(3).start()

        product0(n)
        product1(n)
        return c

    lax.fori_loop(0, 4, products, 0)

    def z_copy(n, half):
        target = (mz + n) % INT
        rows = pl.ds(8 * half, 8)
        sem = INT * half + n
        return remote(zsend.at[target, rows], zrecv.at[mz, rows], z_send.at[sem], z_recv.at[sem], (me, target))

    def y_copy(n, half):
        target = (mz + n) % INT
        rows = pl.ds(8 * half, 8)
        sem = INT * half + n
        return remote(ysum.at[rows], ygath.at[mz, rows], y_send.at[sem], y_recv.at[sem], (me, target))

    turned = acc[...].T[:ROWS]
    for block in range(3):
        for group in range(5):
            zsend[block * 5 + group] = turned[group * 16:(group + 1) * 16, block * 128:(block + 1) * 128]
    zsend[15] = jnp.zeros((16, 128), F32)

    for half in range(2):
        for n in FAR_FIRST:
            z_copy(n, half).start()
    zrecv[mz] = zsend[mz]
    for half in range(2):
        each(1, INT, lambda n: z_copy(n, half).wait_recv())
        rows = pl.ds(8 * half, 8)
        total = zrecv[0, rows]
        for n in range(1, INT):
            total = total + zrecv[n, rows]
        ysum[rows] = total
        for n in FAR_FIRST:
            y_copy(n, half).start()
        ygath[mz, rows] = total
    row = lax.broadcasted_iota(jnp.int32, (NJ * CAP, 256), 0)
    spread = jnp.where(row == at_z, 1.0, 0.0).astype(BF16)
    for half in range(2):
        each(1, INT, lambda n: y_copy(n, half).wait_recv())
    whole = jnp.concatenate(
        [jnp.concatenate([ygath[block * 5 + group] for group in range(5)], axis=0) for block in range(3)], axis=1
    )
    y_high, y_low = halves(whole)
    out = nn(y_high, spread) + nn(y_low, spread)
    out_ref[...] = jnp.where(s_ia_column == s_jb, out, 0.0)

    each(1, 4, lambda o: p0(o).wait_send())
    each(1, 4, lambda o: p1(o).wait_send())
    for o in range(2):
        q0(o, 0).wait_send()
        q0(o, 1).wait_send()
        q1(o, 0).wait_send()
        q1(o, 1).wait_send()
        r0(o).wait_send()
        r1(o).wait_send()
    for n in range(4):
        s0(n).wait_send()
        s1(n).wait_send()
    each(1, BLK, lambda n: d_copy((me + n) % BLK).wait_send())
    for half in range(2):
        each(1, INT, lambda n: z_copy(n, half).wait_send())
        each(1, INT, lambda n: y_copy(n, half).wait_send())


def pad_to(x, shape, value=0):
    return jnp.pad(x, [(0, n - m) for n, m in zip(shape, x.shape)], constant_values=value)


def index_tables():
    far = -100000
    table = np.full((16, BLK * CPAD), far, np.int32)
    lane = np.arange(BLK * CPAD)
    table[0] = np.where(lane % CPAD < NA, NA * (lane // CPAD) + lane % CPAD, -1)
    lane = np.arange(384)
    table[1, :384] = np.where(lane % CPAD < NA, lane % CPAD, far)
    table[2, :384] = lane // CPAD
    m = 6 * (lane // 128) + lane % 128 // PITCH
    a = lane % 128 % PITCH
    table[3, :384] = np.where((a < NA) & (lane % 128 < 6 * PITCH) & (m < NI * NK), a, far)
    table[4, :384] = m
    lane = np.arange(NA * NJ)
    table[5, :NA * NJ] = lane // NJ
    table[6, :NA * NJ] = lane % NJ
    table[7, :NI * NA] = lane % NA
    table[8, :NI * NA] = lane // NA
    lane = np.arange(NJ * NB)
    table[9, :NJ * NB] = lane % NB
    table[10, :NJ * NB] = lane // NB
    pairs = np.full((8, 2, 384), -1, np.int32)
    lane = np.arange(GROUP)
    core, other, row = lane // (4 * HALF), lane // HALF % 4, lane % HALF
    for n in range(8):
        y, x = (n, other) if n < 4 else (other, n - 4)
        n_row = row + HALF * (n // 4)
        good = n_row < NA * NJ
        pairs[n, 0, :GROUP] = np.where(good, ((y * 4 + x) * 2 + core) * NA + n_row // NJ, -1)
        pairs[n, 1, :GROUP] = n_row % NJ
    return table, pairs


def per_device(amplitudes, integrals, occ_irrep, virt_irrep, i_batch, j_batch):
    a_rows = pad_to(jnp.transpose(amplitudes, (2, 0, 1, 3)), (NK, NI, CPAD, NV)).reshape(NK * NI * CPAD, NV)
    ints = jnp.transpose(integrals, (0, 3, 2, 1))
    table, pairs = index_tables()

    vmem = pl.BlockSpec(memory_space=pltpu.VMEM)
    dma = pltpu.SemaphoreType.DMA
    out = pl.pallas_call(
        kernel,
        out_shape=jax.ShapeDtypeStruct((ROWS, 256), F32),
        in_specs=[vmem] * 5 + [pl.BlockSpec(memory_space=pltpu.SMEM)] * 3,
        out_specs=vmem,
        scratch_shapes=[
            pltpu.VMEM((ROWS, NK * CAP), F32),
            pltpu.VMEM((NK, ROWS, NV), F32),
            pltpu.VMEM((8, GROUP, 1), jnp.int32),
            pltpu.VMEM((4, 2, 4, HALF, NK * CAP), F32),
            pltpu.VMEM((4, 2, 4, HALF, NK * CAP), F32),
            pltpu.VMEM((NI * NK * CPAD, 1024), F32),
            pltpu.VMEM((BLK, 56, 128), F32),
            pltpu.VMEM((BLK, 56, 128), F32),
            pltpu.VMEM((BLK * CPAD, 384), F32),
            pltpu.VMEM((8, NJ * CAP, GROUP), BF16),
            pltpu.VMEM((NJ * CAP, 128), F32),
            pltpu.VMEM((INT, 16, 128), F32),
            pltpu.VMEM((INT, 16, 128), F32),
            pltpu.VMEM((16, 128), F32),
            pltpu.VMEM((INT, 16, 128), F32),
            dma((2,)), dma((4,)), dma((4,)), dma((4,)), dma((4,)), dma((6,)), dma((6,)), dma((6,)), dma((6,)),
            dma((4,)), dma((4,)), dma((4,)), dma((4,)), dma((BLK,)), dma((BLK,)),
            dma((2 * INT,)), dma((2 * INT,)), dma((2 * INT,)), dma((2 * INT,)),
        ],
        compiler_params=pltpu.CompilerParams(
            collective_id=0, has_side_effects=True, vmem_limit_bytes=48 * 1024 * 1024
        ),
    )(
        ints, a_rows, virt_irrep.reshape(1, NV), jnp.asarray(table), jnp.asarray(pairs), occ_irrep, i_batch, j_batch
    )
    return out[:NI * NA, :NJ * NB].reshape(NI, NA, NJ, NB)


def solution(mesh):
    placed = (P(None, "blk", "int", None), P("int", None, None, "blk"), P(), P(), P(), P())
    return jax.shard_map(
        per_device,
        mesh=mesh,
        in_specs=placed,
        out_specs=P(None, "blk", None, "int"),
        check_vma=False,
    )
```

```python
import jax
import jax.numpy as jnp
import numpy as np
from jax import lax
from jax.experimental import pallas as pl
from jax.experimental.pallas import tpu as pltpu
from jax.sharding import PartitionSpec as P

MESH = pl.DeviceIdType.MESH
F32 = jnp.float32
BF16 = jnp.bfloat16
CAP = 96
NI = 4
NJ = 4
NA = 19
NK = 4
NB = 38
NV = 608
BLK = 32
INT = 16
ROWS = 80
CPAD = 24
HALF = 40
GROUP = 320
FAR_FIRST = (8, 7, 9, 6, 10, 5, 11, 4, 12, 3, 13, 2, 14, 1, 15)
PITCH = 21


def halves(x):
    high = x.astype(BF16)
    return high, (x - high.astype(F32)).astype(BF16)


def nn(a, b):
    return jnp.dot(a, b, preferred_element_type=F32)


def nt(a, b):
    return lax.dot_general(a, b, (((1,), (1,)), ((), ())), preferred_element_type=F32)


def kernel(
    int_hbm, amp_hbm, virt_ref, index_hbm, pair_hbm, occ_ref, i_ref, j_ref,
    out_ref,
    int_ref, amp_ref, index_ref, pair_ref, load_sem, g_ref, g_rows, a_ref, column_buf, gh0, gh1, spaced, moved, dbuf, arrived, ebuf, acc, zsend, zrecv, ysum, ygath,
    own_sem, p0_send, p0_recv, p1_send, p1_recv, q0_send, q0_recv, q1_send, q1_recv,
    s0_send, s0_recv, s1_send, s1_recv, d_send, d_recv, z_send, z_recv, y_send, y_recv,
):
    me = lax.axis_index("blk")
    mz = lax.axis_index("int")
    core = me % 2
    cx = (me // 2) % 4
    cy = me // 8

    def plane(y, x, c):
        return ((((y + 4) % 4) * 4 + (x + 4) % 4) * 2 + c, mz)

    def each(first, last, do):
        def body(n, c):
            do(n)
            return c

        lax.fori_loop(first, last, body, 0)

    def remote(src, dst, send, recv, device):
        return pltpu.make_async_remote_copy(
            src_ref=src, dst_ref=dst, send_sem=send, recv_sem=recv, device_id=device, device_id_type=MESH
        )

    load_index = pltpu.make_async_copy(index_hbm, index_ref, load_sem.at[0])
    load_int = pltpu.make_async_copy(int_hbm, int_ref, load_sem.at[1])
    load_amp = pltpu.make_async_copy(amp_hbm, amp_ref, load_sem.at[2])
    load_pair = pltpu.make_async_copy(pair_hbm, pair_ref, load_sem.at[3])
    load_index.start()
    load_int.start()
    load_amp.start()
    load_pair.start()

    barrier = pltpu.get_barrier_semaphore()

    def greet(device):
        pl.semaphore_signal(barrier, inc=1, device_id=device, device_id_type=MESH)

    each(1, INT, lambda n: greet((me, (mz + n) % INT)))
    each(1, BLK, lambda n: greet(((me + n) % BLK, mz)))

    own0 = pltpu.make_async_copy(g_ref.at[pl.ds(0, HALF)], gh0.at[cy, core, cx], own_sem.at[0])
    own1 = pltpu.make_async_copy(g_ref.at[pl.ds(HALF, HALF)], gh1.at[cx, core, cy], own_sem.at[1])

    irr_i = [occ_ref[i_ref[i]] for i in range(NI)]
    irr_j = [occ_ref[j_ref[j]] for j in range(NJ)]
    occ_k = [occ_ref[mz * NK + k] for k in range(NK)]
    virt = virt_ref[...]

    label = lax.broadcasted_iota(jnp.int32, (16, NV), 0)
    mine = jnp.where(label == virt, 1.0, 0.0)
    earlier = lax.broadcasted_iota(jnp.int32, (NV, NV), 0) < lax.broadcasted_iota(jnp.int32, (NV, NV), 1)
    counts = nn(mine.astype(BF16), jnp.where(earlier, 1.0, 0.0).astype(BF16))
    place = jnp.sum(mine * counts, axis=0, keepdims=True)
    both = jnp.where(label == 0, virt.astype(F32), jnp.where(label == 1, place, 0.0)).astype(BF16)

    def look(index):
        chosen = lax.broadcasted_iota(jnp.int32, (NV, index.shape[1]), 0) == index
        found = nn(both, jnp.where(chosen, 1.0, 0.0).astype(BF16))
        return found[0:1].astype(jnp.int32), found[1:2].astype(jnp.int32)

    def pick(values, which):
        out = jnp.zeros_like(which)
        for n, value in enumerate(values):
            out = jnp.where(which == n, value, out)
        return out

    def turn(row):
        return jnp.broadcast_to(row.astype(F32), (8, row.shape[1])).T[:, 0:1].astype(jnp.int32)

    def constant(n, lanes):
        return index_ref[n:n + 1, 0:lanes]

    def own_label(n, lanes):
        offset = constant(n, lanes)
        return offset >= 0, look(me * NA + offset)[0]

    def onehot(places):
        row = lax.broadcasted_iota(jnp.int32, (CAP, places.shape[1]), 0)
        return jnp.where(row == places, 1.0, 0.0).astype(BF16)

    p_all = onehot(place.astype(jnp.int32))
    load_index.wait()
    valid, s_bj = own_label(5, 128)
    s_bj = jnp.bitwise_xor(s_bj, pick(irr_j, constant(6, 128)))
    load_int.wait()
    for k in range(NK):
        for b in range(NA):
            g_rows[k, b * NJ:(b + 1) * NJ] = int_ref[k, b]
        g_rows[k, NA * NJ:] = jnp.zeros((ROWS - NA * NJ, NV), F32)
    packed = []
    for k in range(NK):
        high, low = halves(jnp.where(turn(jnp.where(valid, jnp.bitwise_xor(s_bj, occ_k[k]), -2))[:ROWS] == virt, g_rows[k], 0.0))
        packed.append(nt(high, p_all) + nt(low, p_all))
    g_ref[...] = jnp.concatenate(packed, axis=1)
    pl.semaphore_wait(barrier, BLK - 1 + INT - 1)

    own0.start()
    own1.start()

    def p0(o):
        return remote(g_ref.at[pl.ds(0, HALF)], gh0.at[cy, core, cx], p0_send.at[o], p0_recv.at[o], plane(cy, cx + o, core))

    def p1(o):
        return remote(g_ref.at[pl.ds(HALF, HALF)], gh1.at[cx, core, cy], p1_send.at[o], p1_recv.at[o], plane(cy + o, cx, core))

    each(1, 4, lambda o: p0(o).start())
    each(1, 4, lambda o: p1(o).start())

    load_amp.wait()
    for k in range(NK):
        for i in range(NI):
            first = (NI * k + i) * CPAD
            a_ref[first + 16:first + CPAD] = jnp.zeros((8, NV), F32)
            a_ref[first:first + NA] = amp_ref[i, :, k, :]

    a_high, a_low = halves(a_ref[...])
    for n in range(4):
        lane = lax.broadcasted_iota(jnp.int32, (1, 256), 1)
        source = jnp.where(lane % 32 < NA, NA * (8 * n + lane // 32) + lane % 32, -1)
        respace = jnp.where(lax.broadcasted_iota(jnp.int32, (NV, 256), 0) == source, 1.0, 0.0).astype(BF16)
        spaced[:, n * 256:(n + 1) * 256] = nn(a_high, respace) + nn(a_low, respace)

    def d_copy(d):
        return remote(moved.at[d], dbuf.at[me], d_send.at[d], d_recv.at[me], (d, mz))

    def d_start(d):
        @pl.when(d != me)
        def _():
            d_copy(d).start()

    def d_tile(step):
        return (me // 4 + step) % 8

    small = lax.broadcasted_iota(jnp.int32, (CPAD, 128), 1)

    def shuffle(step, c):
        tile = d_tile(step)
        at = pl.ds(pl.multiple_of(tile * 128, 128), 128)
        blocks = [spaced[m * CPAD:(m + 1) * CPAD, at] for m in range(NI * NK)]
        for part in range(4):
            d = 4 * tile + part
            lasts = []
            for t in range(3):
                held = jnp.zeros((CPAD, 128), F32)
                here = blocks[6 * t:6 * t + 6]
                for n, block in enumerate(here):
                    shift = (PITCH * n - 32 * part) % 128
                    turned = pltpu.roll(block, shift, 1) if shift else block
                    held = jnp.where((small >= PITCH * n) & (small < PITCH * n + NA), turned, held)
                last = held[16:]
                if t == 2:
                    packed_rows = jnp.concatenate([pltpu.roll(last, 84, 1)[:3], pltpu.roll(last, 42, 1)[:5]], axis=0)
                    top = jnp.where(small[:8] >= 84, packed_rows, held[:8])
                    moved[d, 32:40] = top
                    moved[d, 40:48] = held[8:16]
                else:
                    moved[d, 16 * t:16 * t + 16] = held[:16]
                    lasts.append(last)
            moved[d, 48:56] = jnp.concatenate([lasts[0][:3], lasts[1][:5]], axis=0)

        @pl.when(step > 0)
        def _():
            each(0, 4, lambda n: d_start(4 * d_tile(step + 7) + n))

        return c

    lax.fori_loop(0, 8, shuffle, 0)
    each(0, 4, lambda n: d_start(4 * d_tile(7) + n))
    dbuf[me] = moved[me]

    def q0(o, late):
        ref = gh0.at[cy, core, pl.ds(2 * abs(o - late), 2)]
        return remote(ref, ref, q0_send.at[2 * late + o], q0_recv.at[2 * late + o], plane(cy + 1 - 2 * o, cx, core))

    def q1(o, late):
        ref = gh1.at[cx, core, pl.ds(2 * abs(o - late), 2)]
        return remote(ref, ref, q1_send.at[2 * late + o], q1_recv.at[2 * late + o], plane(cy, cx + 1 - 2 * o, core))

    def r0(o):
        row = (cy + 3 + 2 * o) % 4
        part = pl.ds(2 * o, 2)
        ref = gh0.at[row, core, part]
        return remote(ref, ref, q0_send.at[4 + o], q0_recv.at[4 + o], plane(cy + 1 - 2 * o, cx, core))

    def r1(o):
        row = (cx + 3 + 2 * o) % 4
        part = pl.ds(2 * o, 2)
        ref = gh1.at[row, core, part]
        return remote(ref, ref, q1_send.at[4 + o], q1_recv.at[4 + o], plane(cy, cx + 1 - 2 * o, core))

    sibling = plane(cy, cx, 1 - core)

    def order(n):
        return n + n // 2 - 2 * (n // 3)

    def s0(n):
        ref = gh0.at[(cy + order(n)) % 4, core]
        return remote(ref, ref, s0_send.at[n], s0_recv.at[n], sibling)

    def s1(n):
        ref = gh1.at[(cx + order(n)) % 4, core]
        return remote(ref, ref, s1_send.at[n], s1_recv.at[n], sibling)

    own0.wait()
    each(1, 4, lambda o: p0(o).wait_recv())
    q0(0, 0).start()
    q0(1, 0).start()
    q0(0, 1).start()
    q0(1, 1).start()
    s0(0).start()
    own1.wait()
    each(1, 4, lambda o: p1(o).wait_recv())
    q1(0, 0).start()
    q1(1, 0).start()
    q1(0, 1).start()
    q1(1, 1).start()
    s1(0).start()

    load_pair.wait()

    @pl.loop(0, 8)
    def _(n):
        row = lax.broadcasted_iota(jnp.int32, (NJ * CAP, GROUP), 0)
        orbital = pair_ref[n, 0:1]
        which = pair_ref[n, 1:2]
        irrep, at = look(orbital)
        at = jnp.where(orbital >= 0, at + CAP * which, -1)
        ebuf[n] = jnp.where(row == at[:, :GROUP], 1.0, 0.0).astype(BF16)
        column_buf[n] = turn(jnp.bitwise_xor(irrep, pick(irr_j, which)))[:GROUP]

    def s_kia(n):
        good, irrep = own_label(n, 384)
        m = constant(n + 1, 384)
        irrep = jnp.bitwise_xor(irrep, pick([irr_i[i] for k in range(NK) for i in range(NI)], m))
        irrep = jnp.bitwise_xor(irrep, pick([occ_k[k] for k in range(NK) for i in range(NI)], m))
        return jnp.where(good, irrep, -2)

    high, low = halves(jnp.where(turn(s_kia(1)) == virt, a_ref[...], 0.0))
    direct = nt(p_all, high) + nt(p_all, low)
    orbital = constant(0, BLK * CPAD)
    irrep, at = look(orbital)
    p_t = onehot(jnp.where(orbital >= 0, at, -1))
    irrep_c = turn(jnp.where(orbital >= 0, irrep, -1))
    s_row = s_kia(3)
    good, s_ia = own_label(7, 128)
    s_ia = jnp.where(good, jnp.bitwise_xor(s_ia, pick(irr_i, constant(8, 128))), -2)
    s_ia_column = turn(s_ia)[:ROWS]
    offset = constant(9, 256)
    which = constant(10, 256)
    s_jb, at_z = look(mz * NB + offset)
    s_jb = jnp.where(offset >= 0, jnp.bitwise_xor(s_jb, pick(irr_j, which)), -1)
    at_z = jnp.where(offset >= 0, at_z + CAP * which, -1)

    def d_wait(n):
        d = (me + n) % BLK
        remote(moved.at[d], dbuf.at[d], d_send.at[d], d_recv.at[d], (d, mz)).wait_recv()

    for o in (1, 0):
        q0(o, 0).wait_recv()
        r0(o).start()
        q1(o, 0).wait_recv()
        r1(o).start()
    each(1, BLK, d_wait)
    @pl.loop(0, BLK)
    def _(d):
        first = pl.multiple_of(d * CPAD, 8)
        for t in range(3):
            arrived[pl.ds(first, 16), t * 128:(t + 1) * 128] = dbuf[d, 16 * t:16 * t + 16]
        rest = dbuf[d, 48:56]
        arrived[pl.ds(first + 16, 8), 0:128] = rest
        arrived[pl.ds(first + 16, 8), 128:256] = jnp.concatenate([rest[3:6], rest[:5]], axis=0)
        top = dbuf[d, 32:40]
        below = jnp.concatenate([pltpu.roll(top, 86, 1)[3:6], top[:5]], axis=0)
        arrived[pl.ds(first + 16, 8), 256:384] = jnp.where(small[:8] < 2 * PITCH, pltpu.roll(top, 44, 1), below)

    swapped = jnp.where(irrep_c == s_row, arrived[...], 0.0)
    s_high, s_low = halves(swapped)
    s_t = nn(p_t, s_high) + nn(p_t, s_low)
    columns = []
    for k in range(NK):
        pairs = []
        for m in range(NI * k, NI * k + NI):
            first = 128 * (m // 6) + PITCH * (m % 6)
            pairs.append(2.0 * direct[:, m * CPAD:m * CPAD + NA] - s_t[:, first:first + NA])
        columns.append(jnp.concatenate(pairs, axis=1))
    w = jnp.concatenate(columns, axis=0)
    w = jnp.concatenate([w, jnp.zeros((NK * CAP, 128 - NI * NA), F32)], axis=1)
    w_high, w_low = halves(w)

    acc[...] = jnp.zeros_like(acc)

    def product(piece, n):
        g_high, g_low = halves(piece.reshape(GROUP, NK * CAP))
        r = nn(g_high, w_high) + (nn(g_high, w_low) + nn(g_low, w_high))
        r_high, r_low = halves(jnp.where(column_buf[n] == s_ia, r, 0.0))
        acc[...] += nn(ebuf[n], r_high) + nn(ebuf[n], r_low)

    def product0(n):
        s0(n).wait_recv()
        row = (cy + order(n)) % 4
        product(gh0[row], row)

    def product1(n):
        s1(n).wait_recv()
        row = (cx + order(n)) % 4
        product(gh1[row], 4 + row)

    for o in (1, 0):
        q0(o, 1).wait_recv()
        s0(2 - o).start()
        q1(o, 1).wait_recv()
        s1(2 - o).start()

    def products(n, c):
        @pl.when(n == 3)
        def _():
            r0(0).wait_recv()
            r0(1).wait_recv()
            s0(3).start()
            r1(0).wait_recv()
            r1(1).wait_recv()
            s1(3).start()

        product0(n)
        product1(n)
        return c

    lax.fori_loop(0, 4, products, 0)

    def z_copy(n, half):
        target = (mz + n) % INT
        rows = pl.ds(8 * half, 8)
        sem = INT * half + n
        return remote(zsend.at[target, rows], zrecv.at[mz, rows], z_send.at[sem], z_recv.at[sem], (me, target))

    def y_copy(n, half):
        target = (mz + n) % INT
        rows = pl.ds(8 * half, 8)
        sem = INT * half + n
        return remote(ysum.at[rows], ygath.at[mz, rows], y_send.at[sem], y_recv.at[sem], (me, target))

    turned = acc[...].T[:ROWS]
    for block in range(3):
        for group in range(5):
            zsend[block * 5 + group] = turned[group * 16:(group + 1) * 16, block * 128:(block + 1) * 128]
    zsend[15] = jnp.zeros((16, 128), F32)

    for half in range(2):
        for n in FAR_FIRST:
            z_copy(n, half).start()
    zrecv[mz] = zsend[mz]
    for half in range(2):
        each(1, INT, lambda n: z_copy(n, half).wait_recv())
        rows = pl.ds(8 * half, 8)
        total = zrecv[0, rows]
        for n in range(1, INT):
            total = total + zrecv[n, rows]
        ysum[rows] = total
        for n in FAR_FIRST:
            y_copy(n, half).start()
        ygath[mz, rows] = total
    row = lax.broadcasted_iota(jnp.int32, (NJ * CAP, 256), 0)
    spread = jnp.where(row == at_z, 1.0, 0.0).astype(BF16)
    for half in range(2):
        each(1, INT, lambda n: y_copy(n, half).wait_recv())
    whole = jnp.concatenate(
        [jnp.concatenate([ygath[block * 5 + group] for group in range(5)], axis=0) for block in range(3)], axis=1
    )
    y_high, y_low = halves(whole)
    out = nn(y_high, spread) + nn(y_low, spread)
    out_ref[...] = jnp.where(s_ia_column == s_jb, out, 0.0)

    each(1, 4, lambda o: p0(o).wait_send())
    each(1, 4, lambda o: p1(o).wait_send())
    for o in range(2):
        q0(o, 0).wait_send()
        q0(o, 1).wait_send()
        q1(o, 0).wait_send()
        q1(o, 1).wait_send()
        r0(o).wait_send()
        r1(o).wait_send()
    for n in range(4):
        s0(n).wait_send()
        s1(n).wait_send()
    each(1, BLK, lambda n: d_copy((me + n) % BLK).wait_send())
    for half in range(2):
        each(1, INT, lambda n: z_copy(n, half).wait_send())
        each(1, INT, lambda n: y_copy(n, half).wait_send())


def index_tables():
    far = -100000
    table = np.full((16, BLK * CPAD), far, np.int32)
    lane = np.arange(BLK * CPAD)
    table[0] = np.where(lane % CPAD < NA, NA * (lane // CPAD) + lane % CPAD, -1)
    lane = np.arange(384)
    table[1, :384] = np.where(lane % CPAD < NA, lane % CPAD, far)
    table[2, :384] = lane // CPAD
    m = 6 * (lane // 128) + lane % 128 // PITCH
    a = lane % 128 % PITCH
    table[3, :384] = np.where((a < NA) & (lane % 128 < 6 * PITCH) & (m < NI * NK), a, far)
    table[4, :384] = m
    lane = np.arange(NA * NJ)
    table[5, :NA * NJ] = lane // NJ
    table[6, :NA * NJ] = lane % NJ
    table[7, :NI * NA] = lane % NA
    table[8, :NI * NA] = lane // NA
    lane = np.arange(NJ * NB)
    table[9, :NJ * NB] = lane % NB
    table[10, :NJ * NB] = lane // NB
    pairs = np.full((8, 2, 384), -1, np.int32)
    lane = np.arange(GROUP)
    core, other, row = lane // (4 * HALF), lane // HALF % 4, lane % HALF
    for n in range(8):
        y, x = (n, other) if n < 4 else (other, n - 4)
        n_row = row + HALF * (n // 4)
        good = n_row < NA * NJ
        pairs[n, 0, :GROUP] = np.where(good, ((y * 4 + x) * 2 + core) * NA + n_row // NJ, -1)
        pairs[n, 1, :GROUP] = n_row % NJ
    return table, pairs


def per_device(amplitudes, integrals, occ_irrep, virt_irrep, i_batch, j_batch):
    ints = jnp.transpose(integrals, (0, 3, 2, 1))
    table, pairs = index_tables()

    vmem = pl.BlockSpec(memory_space=pltpu.VMEM)
    hbm = pl.BlockSpec(memory_space=pltpu.HBM)
    dma = pltpu.SemaphoreType.DMA
    out = pl.pallas_call(
        kernel,
        out_shape=jax.ShapeDtypeStruct((ROWS, 256), F32),
        in_specs=[hbm, hbm, vmem, hbm, hbm] + [pl.BlockSpec(memory_space=pltpu.SMEM)] * 3,
        out_specs=vmem,
        scratch_shapes=[
            pltpu.VMEM((NK, NA, NJ, NV), F32),
            pltpu.VMEM((NI, NA, NK, NV), F32),
            pltpu.VMEM((16, BLK * CPAD), jnp.int32),
            pltpu.VMEM((8, 2, 384), jnp.int32),
            dma((4,)),
            pltpu.VMEM((ROWS, NK * CAP), F32),
            pltpu.VMEM((NK, ROWS, NV), F32),
            pltpu.VMEM((NI * NK * CPAD, NV), F32),
            pltpu.VMEM((8, GROUP, 1), jnp.int32),
            pltpu.VMEM((4, 2, 4, HALF, NK * CAP), F32),
            pltpu.VMEM((4, 2, 4, HALF, NK * CAP), F32),
            pltpu.VMEM((NI * NK * CPAD, 1024), F32),
            pltpu.VMEM((BLK, 56, 128), F32),
            pltpu.VMEM((BLK, 56, 128), F32),
            pltpu.VMEM((BLK * CPAD, 384), F32),
            pltpu.VMEM((8, NJ * CAP, GROUP), BF16),
            pltpu.VMEM((NJ * CAP, 128), F32),
            pltpu.VMEM((INT, 16, 128), F32),
            pltpu.VMEM((INT, 16, 128), F32),
            pltpu.VMEM((16, 128), F32),
            pltpu.VMEM((INT, 16, 128), F32),
            dma((2,)), dma((4,)), dma((4,)), dma((4,)), dma((4,)), dma((6,)), dma((6,)), dma((6,)), dma((6,)),
            dma((4,)), dma((4,)), dma((4,)), dma((4,)), dma((BLK,)), dma((BLK,)),
            dma((2 * INT,)), dma((2 * INT,)), dma((2 * INT,)), dma((2 * INT,)),
        ],
        compiler_params=pltpu.CompilerParams(
            collective_id=0, has_side_effects=True, vmem_limit_bytes=66850000
        ),
    )(
        ints, amplitudes, virt_irrep.reshape(1, NV), jnp.asarray(table), jnp.asarray(pairs), occ_irrep, i_batch, j_batch
    )
    return out[:NI * NA, :NJ * NB].reshape(NI, NA, NJ, NB)


def solution(mesh):
    placed = (P(None, "blk", "int", None), P("int", None, None, "blk"), P(), P(), P(), P())
    return jax.shard_map(
        per_device,
        mesh=mesh,
        in_specs=placed,
        out_specs=P(None, "blk", None, "int"),
        check_vma=False,
    )
```

```python
import jax
import jax.numpy as jnp
import numpy as np
from jax import lax
from jax.experimental import pallas as pl
from jax.experimental.pallas import tpu as pltpu
from jax.sharding import PartitionSpec as P

MESH = pl.DeviceIdType.MESH
F32 = jnp.float32
BF16 = jnp.bfloat16
CAP = 96
NI = 4
NJ = 4
NA = 19
NK = 4
NB = 38
NV = 608
BLK = 32
INT = 16
ROWS = 80
CPAD = 24
HALF = 40
GROUP = 320
FAR_FIRST = (8, 7, 9, 6, 10, 5, 11, 4, 12, 3, 13, 2, 14, 1, 15)
PITCH = 21


def halves(x):
    high = x.astype(BF16)
    return high, (x - high.astype(F32)).astype(BF16)


def nn(a, b):
    return jnp.dot(a, b, preferred_element_type=F32)


def nt(a, b):
    return lax.dot_general(a, b, (((1,), (1,)), ((), ())), preferred_element_type=F32)


def kernel(
    int_ref, a_ref, virt_ref, index_ref, pair_ref, occ_ref, i_ref, j_ref,
    out_ref,
    g_ref, g_rows, column_buf, gh0, gh1, spaced, moved, dbuf, arrived, ebuf, acc, zsend, zrecv, ysum, ygath,
    own_sem, p0_send, p0_recv, p1_send, p1_recv, q0_send, q0_recv, q1_send, q1_recv,
    s0_send, s0_recv, s1_send, s1_recv, d_send, d_recv, z_send, z_recv, y_send, y_recv,
):
    me = lax.axis_index("blk")
    mz = lax.axis_index("int")
    core = me % 2
    cx = (me // 2) % 4
    cy = me // 8

    def plane(y, x, c):
        return ((((y + 4) % 4) * 4 + (x + 4) % 4) * 2 + c, mz)

    def each(first, last, do):
        def body(n, c):
            do(n)
            return c

        lax.fori_loop(first, last, body, 0)

    def remote(src, dst, send, recv, device):
        return pltpu.make_async_remote_copy(
            src_ref=src, dst_ref=dst, send_sem=send, recv_sem=recv, device_id=device, device_id_type=MESH
        )

    barrier = pltpu.get_barrier_semaphore()

    def greet(device):
        pl.semaphore_signal(barrier, inc=1, device_id=device, device_id_type=MESH)

    each(1, INT, lambda n: greet((me, (mz + n) % INT)))
    each(1, BLK, lambda n: greet(((me + n) % BLK, mz)))

    own0 = pltpu.make_async_copy(g_ref.at[pl.ds(0, HALF)], gh0.at[cy, core, cx], own_sem.at[0])
    own1 = pltpu.make_async_copy(g_ref.at[pl.ds(HALF, HALF)], gh1.at[cx, core, cy], own_sem.at[1])

    irr_i = [occ_ref[i_ref[i]] for i in range(NI)]
    irr_j = [occ_ref[j_ref[j]] for j in range(NJ)]
    occ_k = [occ_ref[mz * NK + k] for k in range(NK)]
    virt = virt_ref[...]

    label = lax.broadcasted_iota(jnp.int32, (16, NV), 0)
    mine = jnp.where(label == virt, 1.0, 0.0)
    earlier = lax.broadcasted_iota(jnp.int32, (NV, NV), 0) < lax.broadcasted_iota(jnp.int32, (NV, NV), 1)
    counts = nn(mine.astype(BF16), jnp.where(earlier, 1.0, 0.0).astype(BF16))
    place = jnp.sum(mine * counts, axis=0, keepdims=True)
    both = jnp.where(label == 0, virt.astype(F32), jnp.where(label == 1, place, 0.0)).astype(BF16)

    def look(index):
        chosen = lax.broadcasted_iota(jnp.int32, (NV, index.shape[1]), 0) == index
        found = nn(both, jnp.where(chosen, 1.0, 0.0).astype(BF16))
        return found[0:1].astype(jnp.int32), found[1:2].astype(jnp.int32)

    def pick(values, which):
        out = jnp.zeros_like(which)
        for n, value in enumerate(values):
            out = jnp.where(which == n, value, out)
        return out

    def turn(row):
        return jnp.broadcast_to(row.astype(F32), (8, row.shape[1])).T[:, 0:1].astype(jnp.int32)

    def constant(n, lanes):
        return index_ref[n:n + 1, 0:lanes]

    def own_label(n, lanes):
        offset = constant(n, lanes)
        return offset >= 0, look(me * NA + offset)[0]

    def onehot(places):
        row = lax.broadcasted_iota(jnp.int32, (CAP, places.shape[1]), 0)
        return jnp.where(row == places, 1.0, 0.0).astype(BF16)

    p_all = onehot(place.astype(jnp.int32))
    valid, s_bj = own_label(5, 128)
    s_bj = jnp.bitwise_xor(s_bj, pick(irr_j, constant(6, 128)))
    for k in range(NK):
        for b in range(NA):
            g_rows[k, b * NJ:(b + 1) * NJ] = int_ref[k, b]
        g_rows[k, NA * NJ:] = jnp.zeros((ROWS - NA * NJ, NV), F32)
    packed = []
    for k in range(NK):
        high, low = halves(jnp.where(turn(jnp.where(valid, jnp.bitwise_xor(s_bj, occ_k[k]), -2))[:ROWS] == virt, g_rows[k], 0.0))
        packed.append(nt(high, p_all) + nt(low, p_all))
    g_ref[...] = jnp.concatenate(packed, axis=1)
    pl.semaphore_wait(barrier, BLK - 1 + INT - 1)

    own0.start()
    own1.start()

    def p0(o):
        return remote(g_ref.at[pl.ds(0, HALF)], gh0.at[cy, core, cx], p0_send.at[o], p0_recv.at[o], plane(cy, cx + o, core))

    def p1(o):
        return remote(g_ref.at[pl.ds(HALF, HALF)], gh1.at[cx, core, cy], p1_send.at[o], p1_recv.at[o], plane(cy + o, cx, core))

    for o in (2, 1, 3):
        p0(o).start()
        p1(o).start()

    a_high, a_low = halves(a_ref[...])
    for n in range(4):
        lane = lax.broadcasted_iota(jnp.int32, (1, 256), 1)
        source = jnp.where(lane % 32 < NA, NA * (8 * n + lane // 32) + lane % 32, -1)
        respace = jnp.where(lax.broadcasted_iota(jnp.int32, (NV, 256), 0) == source, 1.0, 0.0).astype(BF16)
        spaced[:, n * 256:(n + 1) * 256] = nn(a_high, respace) + nn(a_low, respace)

    def d_copy(d):
        return remote(moved.at[d], dbuf.at[me], d_send.at[d], d_recv.at[me], (d, mz))

    def d_start(d):
        @pl.when(d != me)
        def _():
            d_copy(d).start()

    def d_tile(step):
        return (me // 4 + step) % 8

    small = lax.broadcasted_iota(jnp.int32, (CPAD, 128), 1)

    def shuffle(step, c):
        tile = d_tile(step)
        at = pl.ds(pl.multiple_of(tile * 128, 128), 128)
        blocks = [spaced[m * CPAD:(m + 1) * CPAD, at] for m in range(NI * NK)]
        for part in range(4):
            d = 4 * tile + part
            lasts = []
            for t in range(3):
                held = jnp.zeros((CPAD, 128), F32)
                here = blocks[6 * t:6 * t + 6]
                for n, block in enumerate(here):
                    shift = (PITCH * n - 32 * part) % 128
                    turned = pltpu.roll(block, shift, 1) if shift else block
                    held = jnp.where((small >= PITCH * n) & (small < PITCH * n + NA), turned, held)
                last = held[16:]
                if t == 2:
                    packed_rows = jnp.concatenate([pltpu.roll(last, 84, 1)[:3], pltpu.roll(last, 42, 1)[:5]], axis=0)
                    top = jnp.where(small[:8] >= 84, packed_rows, held[:8])
                    moved[d, 32:40] = top
                    moved[d, 40:48] = held[8:16]
                else:
                    moved[d, 16 * t:16 * t + 16] = held[:16]
                    lasts.append(last)
            moved[d, 48:56] = jnp.concatenate([lasts[0][:3], lasts[1][:5]], axis=0)

        @pl.when(step > 0)
        def _():
            each(0, 4, lambda n: d_start(4 * d_tile(step + 7) + n))

        return c

    lax.fori_loop(0, 8, shuffle, 0)
    each(0, 4, lambda n: d_start(4 * d_tile(7) + n))
    dbuf[me] = moved[me]

    def q0(o, late):
        ref = gh0.at[cy, core, pl.ds(2 * abs(o - late), 2)]
        return remote(ref, ref, q0_send.at[2 * late + o], q0_recv.at[2 * late + o], plane(cy + 1 - 2 * o, cx, core))

    def q1(o, late):
        ref = gh1.at[cx, core, pl.ds(2 * abs(o - late), 2)]
        return remote(ref, ref, q1_send.at[2 * late + o], q1_recv.at[2 * late + o], plane(cy, cx + 1 - 2 * o, core))

    def r0(o):
        row = (cy + 3 + 2 * o) % 4
        part = pl.ds(2 * o, 2)
        ref = gh0.at[row, core, part]
        return remote(ref, ref, q0_send.at[4 + o], q0_recv.at[4 + o], plane(cy + 1 - 2 * o, cx, core))

    def r1(o):
        row = (cx + 3 + 2 * o) % 4
        part = pl.ds(2 * o, 2)
        ref = gh1.at[row, core, part]
        return remote(ref, ref, q1_send.at[4 + o], q1_recv.at[4 + o], plane(cy, cx + 1 - 2 * o, core))

    sibling = plane(cy, cx, 1 - core)

    def order(n):
        return n + n // 2 - 2 * (n // 3)

    def s0(n):
        ref = gh0.at[(cy + order(n)) % 4, core]
        return remote(ref, ref, s0_send.at[n], s0_recv.at[n], sibling)

    def s1(n):
        ref = gh1.at[(cx + order(n)) % 4, core]
        return remote(ref, ref, s1_send.at[n], s1_recv.at[n], sibling)

    own0.wait()
    each(1, 4, lambda o: p0(o).wait_recv())
    q0(0, 0).start()
    q0(1, 0).start()
    q0(0, 1).start()
    q0(1, 1).start()
    s0(0).start()
    own1.wait()
    each(1, 4, lambda o: p1(o).wait_recv())
    q1(0, 0).start()
    q1(1, 0).start()
    q1(0, 1).start()
    q1(1, 1).start()
    s1(0).start()

    @pl.loop(0, 8)
    def _(n):
        row = lax.broadcasted_iota(jnp.int32, (NJ * CAP, GROUP), 0)
        orbital = pair_ref[n, 0:1]
        which = pair_ref[n, 1:2]
        irrep, at = look(orbital)
        at = jnp.where(orbital >= 0, at + CAP * which, -1)
        ebuf[n] = jnp.where(row == at[:, :GROUP], 1.0, 0.0).astype(BF16)
        column_buf[n] = turn(jnp.bitwise_xor(irrep, pick(irr_j, which)))[:GROUP]

    def s_kia(n):
        good, irrep = own_label(n, 384)
        m = constant(n + 1, 384)
        irrep = jnp.bitwise_xor(irrep, pick([irr_i[i] for k in range(NK) for i in range(NI)], m))
        irrep = jnp.bitwise_xor(irrep, pick([occ_k[k] for k in range(NK) for i in range(NI)], m))
        return jnp.where(good, irrep, -2)

    high, low = halves(jnp.where(turn(s_kia(1)) == virt, a_ref[...], 0.0))
    direct = nt(p_all, high) + nt(p_all, low)
    orbital = constant(0, BLK * CPAD)
    irrep, at = look(orbital)
    p_t = onehot(jnp.where(orbital >= 0, at, -1))
    irrep_c = turn(jnp.where(orbital >= 0, irrep, -1))
    s_row = s_kia(3)
    good, s_ia = own_label(7, 128)
    s_ia = jnp.where(good, jnp.bitwise_xor(s_ia, pick(irr_i, constant(8, 128))), -2)
    s_ia_column = turn(s_ia)[:ROWS]
    offset = constant(9, 256)
    which = constant(10, 256)
    s_jb, at_z = look(mz * NB + offset)
    s_jb = jnp.where(offset >= 0, jnp.bitwise_xor(s_jb, pick(irr_j, which)), -1)
    at_z = jnp.where(offset >= 0, at_z + CAP * which, -1)

    def d_wait(n):
        d = (me + n) % BLK
        remote(moved.at[d], dbuf.at[d], d_send.at[d], d_recv.at[d], (d, mz)).wait_recv()

    for o in (1, 0):
        q0(o, 0).wait_recv()
        r0(o).start()
        q1(o, 0).wait_recv()
        r1(o).start()
    each(1, BLK, d_wait)
    @pl.loop(0, BLK)
    def _(d):
        first = pl.multiple_of(d * CPAD, 8)
        for t in range(3):
            arrived[pl.ds(first, 16), t * 128:(t + 1) * 128] = dbuf[d, 16 * t:16 * t + 16]
        rest = dbuf[d, 48:56]
        arrived[pl.ds(first + 16, 8), 0:128] = rest
        arrived[pl.ds(first + 16, 8), 128:256] = jnp.concatenate([rest[3:6], rest[:5]], axis=0)
        top = dbuf[d, 32:40]
        below = jnp.concatenate([pltpu.roll(top, 86, 1)[3:6], top[:5]], axis=0)
        arrived[pl.ds(first + 16, 8), 256:384] = jnp.where(small[:8] < 2 * PITCH, pltpu.roll(top, 44, 1), below)

    swapped = jnp.where(irrep_c == s_row, arrived[...], 0.0)
    s_high, s_low = halves(swapped)
    s_t = nn(p_t, s_high) + nn(p_t, s_low)
    columns = []
    for k in range(NK):
        pairs = []
        for m in range(NI * k, NI * k + NI):
            first = 128 * (m // 6) + PITCH * (m % 6)
            pairs.append(2.0 * direct[:, m * CPAD:m * CPAD + NA] - s_t[:, first:first + NA])
        columns.append(jnp.concatenate(pairs, axis=1))
    w = jnp.concatenate(columns, axis=0)
    w = jnp.concatenate([w, jnp.zeros((NK * CAP, 128 - NI * NA), F32)], axis=1)
    w_high, w_low = halves(w)

    acc[...] = jnp.zeros_like(acc)

    def product(piece, n):
        g_high, g_low = halves(piece.reshape(GROUP, NK * CAP))
        r = nn(g_high, w_high) + (nn(g_high, w_low) + nn(g_low, w_high))
        r_high, r_low = halves(jnp.where(column_buf[n] == s_ia, r, 0.0))
        acc[...] += nn(ebuf[n], r_high) + nn(ebuf[n], r_low)

    def product0(n):
        s0(n).wait_recv()
        row = (cy + order(n)) % 4
        product(gh0[row], row)

    def product1(n):
        s1(n).wait_recv()
        row = (cx + order(n)) % 4
        product(gh1[row], 4 + row)

    for o in (1, 0):
        q0(o, 1).wait_recv()
        s0(2 - o).start()
        q1(o, 1).wait_recv()
        s1(2 - o).start()

    def products(n, c):
        @pl.when(n == 3)
        def _():
            r0(0).wait_recv()
            r0(1).wait_recv()
            s0(3).start()
            r1(0).wait_recv()
            r1(1).wait_recv()
            s1(3).start()

        product0(n)
        product1(n)
        return c

    lax.fori_loop(0, 4, products, 0)

    def z_copy(n, half):
        target = (mz + n) % INT
        rows = pl.ds(8 * half, 8)
        sem = INT * half + n
        return remote(zsend.at[target, rows], zrecv.at[mz, rows], z_send.at[sem], z_recv.at[sem], (me, target))

    def y_copy(n, half):
        target = (mz + n) % INT
        rows = pl.ds(8 * half, 8)
        sem = INT * half + n
        return remote(ysum.at[rows], ygath.at[mz, rows], y_send.at[sem], y_recv.at[sem], (me, target))

    turned = acc[...].T[:ROWS]
    for block in range(3):
        for group in range(5):
            zsend[block * 5 + group] = turned[group * 16:(group + 1) * 16, block * 128:(block + 1) * 128]
    zsend[15] = jnp.zeros((16, 128), F32)

    for half in range(2):
        for n in FAR_FIRST:
            z_copy(n, half).start()
    zrecv[mz] = zsend[mz]
    for half in range(2):
        each(1, INT, lambda n: z_copy(n, half).wait_recv())
        rows = pl.ds(8 * half, 8)
        total = zrecv[0, rows]
        for n in range(1, INT):
            total = total + zrecv[n, rows]
        ysum[rows] = total
        for n in FAR_FIRST:
            y_copy(n, half).start()
        ygath[mz, rows] = total
    row = lax.broadcasted_iota(jnp.int32, (NJ * CAP, 256), 0)
    spread = jnp.where(row == at_z, 1.0, 0.0).astype(BF16)
    for half in range(2):
        each(1, INT, lambda n: y_copy(n, half).wait_recv())
    whole = jnp.concatenate(
        [jnp.concatenate([ygath[block * 5 + group] for group in range(5)], axis=0) for block in range(3)], axis=1
    )
    y_high, y_low = halves(whole)
    out = nn(y_high, spread) + nn(y_low, spread)
    out_ref[...] = jnp.where(s_ia_column == s_jb, out, 0.0)

    each(1, 4, lambda o: p0(o).wait_send())
    each(1, 4, lambda o: p1(o).wait_send())
    for o in range(2):
        q0(o, 0).wait_send()
        q0(o, 1).wait_send()
        q1(o, 0).wait_send()
        q1(o, 1).wait_send()
        r0(o).wait_send()
        r1(o).wait_send()
    for n in range(4):
        s0(n).wait_send()
        s1(n).wait_send()
    each(1, BLK, lambda n: d_copy((me + n) % BLK).wait_send())
    for half in range(2):
        each(1, INT, lambda n: z_copy(n, half).wait_send())
        each(1, INT, lambda n: y_copy(n, half).wait_send())


def pad_to(x, shape, value=0):
    return jnp.pad(x, [(0, n - m) for n, m in zip(shape, x.shape)], constant_values=value)


def index_tables():
    far = -100000
    table = np.full((16, BLK * CPAD), far, np.int32)
    lane = np.arange(BLK * CPAD)
    table[0] = np.where(lane % CPAD < NA, NA * (lane // CPAD) + lane % CPAD, -1)
    lane = np.arange(384)
    table[1, :384] = np.where(lane % CPAD < NA, lane % CPAD, far)
    table[2, :384] = lane // CPAD
    m = 6 * (lane // 128) + lane % 128 // PITCH
    a = lane % 128 % PITCH
    table[3, :384] = np.where((a < NA) & (lane % 128 < 6 * PITCH) & (m < NI * NK), a, far)
    table[4, :384] = m
    lane = np.arange(NA * NJ)
    table[5, :NA * NJ] = lane // NJ
    table[6, :NA * NJ] = lane % NJ
    table[7, :NI * NA] = lane % NA
    table[8, :NI * NA] = lane // NA
    lane = np.arange(NJ * NB)
    table[9, :NJ * NB] = lane % NB
    table[10, :NJ * NB] = lane // NB
    pairs = np.full((8, 2, 384), -1, np.int32)
    lane = np.arange(GROUP)
    core, other, row = lane // (4 * HALF), lane // HALF % 4, lane % HALF
    for n in range(8):
        y, x = (n, other) if n < 4 else (other, n - 4)
        n_row = row + HALF * (n // 4)
        good = n_row < NA * NJ
        pairs[n, 0, :GROUP] = np.where(good, ((y * 4 + x) * 2 + core) * NA + n_row // NJ, -1)
        pairs[n, 1, :GROUP] = n_row % NJ
    return table, pairs


def per_device(amplitudes, integrals, occ_irrep, virt_irrep, i_batch, j_batch):
    a_rows = pad_to(jnp.transpose(amplitudes, (2, 0, 1, 3)), (NK, NI, CPAD, NV)).reshape(NK * NI * CPAD, NV)
    ints = jnp.transpose(integrals, (0, 3, 2, 1))
    table, pairs = index_tables()

    vmem = pl.BlockSpec(memory_space=pltpu.VMEM)
    dma = pltpu.SemaphoreType.DMA
    out = pl.pallas_call(
        kernel,
        out_shape=jax.ShapeDtypeStruct((ROWS, 256), F32),
        in_specs=[vmem] * 5 + [pl.BlockSpec(memory_space=pltpu.SMEM)] * 3,
        out_specs=vmem,
        scratch_shapes=[
            pltpu.VMEM((ROWS, NK * CAP), F32),
            pltpu.VMEM((NK, ROWS, NV), F32),
            pltpu.VMEM((8, GROUP, 1), jnp.int32),
            pltpu.VMEM((4, 2, 4, HALF, NK * CAP), F32),
            pltpu.VMEM((4, 2, 4, HALF, NK * CAP), F32),
            pltpu.VMEM((NI * NK * CPAD, 1024), F32),
            pltpu.VMEM((BLK, 56, 128), F32),
            pltpu.VMEM((BLK, 56, 128), F32),
            pltpu.VMEM((BLK * CPAD, 384), F32),
            pltpu.VMEM((8, NJ * CAP, GROUP), BF16),
            pltpu.VMEM((NJ * CAP, 128), F32),
            pltpu.VMEM((INT, 16, 128), F32),
            pltpu.VMEM((INT, 16, 128), F32),
            pltpu.VMEM((16, 128), F32),
            pltpu.VMEM((INT, 16, 128), F32),
            dma((2,)), dma((4,)), dma((4,)), dma((4,)), dma((4,)), dma((6,)), dma((6,)), dma((6,)), dma((6,)),
            dma((4,)), dma((4,)), dma((4,)), dma((4,)), dma((BLK,)), dma((BLK,)),
            dma((2 * INT,)), dma((2 * INT,)), dma((2 * INT,)), dma((2 * INT,)),
        ],
        compiler_params=pltpu.CompilerParams(
            collective_id=0, has_side_effects=True, vmem_limit_bytes=48 * 1024 * 1024
        ),
    )(
        ints, a_rows, virt_irrep.reshape(1, NV), jnp.asarray(table), jnp.asarray(pairs), occ_irrep, i_batch, j_batch
    )
    return out[:NI * NA, :NJ * NB].reshape(NI, NA, NJ, NB)


def solution(mesh):
    placed = (P(None, "blk", "int", None), P("int", None, None, "blk"), P(), P(), P(), P())
    return jax.shard_map(
        per_device,
        mesh=mesh,
        in_specs=placed,
        out_specs=P(None, "blk", None, "int"),
        check_vma=False,
    )
```

```python
import jax
import jax.numpy as jnp
import numpy as np
from jax import lax
from jax.experimental import pallas as pl
from jax.experimental.pallas import tpu as pltpu
from jax.sharding import PartitionSpec as P

MESH = pl.DeviceIdType.MESH
F32 = jnp.float32
BF16 = jnp.bfloat16
CAP = 96
NI = 4
NJ = 4
NA = 19
NK = 4
NB = 38
NV = 608
BLK = 32
INT = 16
ROWS = 80
CPAD = 24
HALF = 40
GROUP = 320
FAR_FIRST = (8, 7, 9, 6, 10, 5, 11, 4, 12, 3, 13, 2, 14, 1, 15)
PITCH = 21


def halves(x):
    high = x.astype(BF16)
    return high, (x - high.astype(F32)).astype(BF16)


def nn(a, b):
    return jnp.dot(a, b, preferred_element_type=F32)


def nt(a, b):
    return lax.dot_general(a, b, (((1,), (1,)), ((), ())), preferred_element_type=F32)


def kernel(
    int_ref, a_ref, virt_ref, index_ref, pair_ref, occ_ref, i_ref, j_ref,
    out_ref,
    g_ref, g_rows, column_buf, gh0, gh1, spaced, moved, dbuf, arrived, ebuf, acc, zsend, zrecv, ysum, ygath,
    own_sem, p0_send, p0_recv, p1_send, p1_recv, q0_send, q0_recv, q1_send, q1_recv,
    s0_send, s0_recv, s1_send, s1_recv, d_send, d_recv, z_send, z_recv, y_send, y_recv,
):
    me = lax.axis_index("blk")
    mz = lax.axis_index("int")
    core = me % 2
    cx = (me // 2) % 4
    cy = me // 8

    def plane(y, x, c):
        return ((((y + 4) % 4) * 4 + (x + 4) % 4) * 2 + c, mz)

    def each(first, last, do):
        def body(n, c):
            do(n)
            return c

        lax.fori_loop(first, last, body, 0)

    def remote(src, dst, send, recv, device):
        return pltpu.make_async_remote_copy(
            src_ref=src, dst_ref=dst, send_sem=send, recv_sem=recv, device_id=device, device_id_type=MESH
        )

    barrier = pltpu.get_barrier_semaphore()

    def greet(device):
        pl.semaphore_signal(barrier, inc=1, device_id=device, device_id_type=MESH)

    each(1, INT, lambda n: greet((me, (mz + n) % INT)))
    each(1, BLK, lambda n: greet(((me + n) % BLK, mz)))

    own0 = pltpu.make_async_copy(g_ref.at[pl.ds(0, HALF)], gh0.at[cy, core, cx], own_sem.at[0])
    own1 = pltpu.make_async_copy(g_ref.at[pl.ds(HALF, HALF)], gh1.at[cx, core, cy], own_sem.at[1])

    irr_i = [occ_ref[i_ref[i]] for i in range(NI)]
    irr_j = [occ_ref[j_ref[j]] for j in range(NJ)]
    occ_k = [occ_ref[mz * NK + k] for k in range(NK)]
    virt = virt_ref[...]

    label = lax.broadcasted_iota(jnp.int32, (16, NV), 0)
    mine = jnp.where(label == virt, 1.0, 0.0)
    earlier = lax.broadcasted_iota(jnp.int32, (NV, NV), 0) < lax.broadcasted_iota(jnp.int32, (NV, NV), 1)
    counts = nn(mine.astype(BF16), jnp.where(earlier, 1.0, 0.0).astype(BF16))
    place = jnp.sum(mine * counts, axis=0, keepdims=True)
    both = jnp.where(label == 0, virt.astype(F32), jnp.where(label == 1, place, 0.0)).astype(BF16)

    def look(index):
        chosen = lax.broadcasted_iota(jnp.int32, (NV, index.shape[1]), 0) == index
        found = nn(both, jnp.where(chosen, 1.0, 0.0).astype(BF16))
        return found[0:1].astype(jnp.int32), found[1:2].astype(jnp.int32)

    def pick(values, which):
        out = jnp.zeros_like(which)
        for n, value in enumerate(values):
            out = jnp.where(which == n, value, out)
        return out

    def turn(row):
        return jnp.broadcast_to(row.astype(F32), (8, row.shape[1])).T[:, 0:1].astype(jnp.int32)

    def constant(n, lanes):
        return index_ref[n:n + 1, 0:lanes]

    def own_label(n, lanes):
        offset = constant(n, lanes)
        return offset >= 0, look(me * NA + offset)[0]

    def onehot(places):
        row = lax.broadcasted_iota(jnp.int32, (CAP, places.shape[1]), 0)
        return jnp.where(row == places, 1.0, 0.0).astype(BF16)

    p_all = onehot(place.astype(jnp.int32))
    valid, s_bj = own_label(5, 128)
    s_bj = jnp.bitwise_xor(s_bj, pick(irr_j, constant(6, 128)))
    for k in range(NK):
        for b in range(NA):
            g_rows[k, b * NJ:(b + 1) * NJ] = int_ref[k, b]
        g_rows[k, NA * NJ:] = jnp.zeros((ROWS - NA * NJ, NV), F32)
    packed = []
    for k in range(NK):
        high, low = halves(jnp.where(turn(jnp.where(valid, jnp.bitwise_xor(s_bj, occ_k[k]), -2))[:ROWS] == virt, g_rows[k], 0.0))
        packed.append(nt(high, p_all) + nt(low, p_all))
    g_ref[...] = jnp.concatenate(packed, axis=1)
    pl.semaphore_wait(barrier, BLK - 1 + INT - 1)

    own0.start()
    own1.start()

    def p0(o):
        return remote(g_ref.at[pl.ds(0, HALF)], gh0.at[cy, core, cx], p0_send.at[o], p0_recv.at[o], plane(cy, cx + o, core))

    def p1(o):
        return remote(g_ref.at[pl.ds(HALF, HALF)], gh1.at[cx, core, cy], p1_send.at[o], p1_recv.at[o], plane(cy + o, cx, core))

    each(1, 4, lambda o: p0(o).start())
    each(1, 4, lambda o: p1(o).start())

    a_high, a_low = halves(a_ref[...])
    for n in range(4):
        lane = lax.broadcasted_iota(jnp.int32, (1, 256), 1)
        source = jnp.where(lane % 32 < NA, NA * (8 * n + lane // 32) + lane % 32, -1)
        respace = jnp.where(lax.broadcasted_iota(jnp.int32, (NV, 256), 0) == source, 1.0, 0.0).astype(BF16)
        spaced[:, n * 256:(n + 1) * 256] = nn(a_high, respace) + nn(a_low, respace)

    def d_copy(d):
        return remote(moved.at[d], dbuf.at[me], d_send.at[d], d_recv.at[me], (d, mz))

    def d_start(d):
        @pl.when(d != me)
        def _():
            d_copy(d).start()

    def d_tile(step):
        return (me // 4 + step) % 8

    small = lax.broadcasted_iota(jnp.int32, (CPAD, 128), 1)

    def shuffle(step, c):
        tile = d_tile(step)
        at = pl.ds(pl.multiple_of(tile * 128, 128), 128)
        blocks = [spaced[m * CPAD:(m + 1) * CPAD, at] for m in range(NI * NK)]
        for part in range(4):
            d = 4 * tile + part
            lasts = []
            for t in range(3):
                held = jnp.zeros((CPAD, 128), F32)
                here = blocks[6 * t:6 * t + 6]
                for n, block in enumerate(here):
                    shift = (PITCH * n - 32 * part) % 128
                    turned = pltpu.roll(block, shift, 1) if shift else block
                    held = jnp.where((small >= PITCH * n) & (small < PITCH * n + NA), turned, held)
                last = held[16:]
                if t == 2:
                    packed_rows = jnp.concatenate([pltpu.roll(last, 84, 1)[:3], pltpu.roll(last, 42, 1)[:5]], axis=0)
                    top = jnp.where(small[:8] >= 84, packed_rows, held[:8])
                    moved[d, 32:40] = top
                    moved[d, 40:48] = held[8:16]
                else:
                    moved[d, 16 * t:16 * t + 16] = held[:16]
                    lasts.append(last)
            moved[d, 48:56] = jnp.concatenate([lasts[0][:3], lasts[1][:5]], axis=0)

        @pl.when(step > 0)
        def _():
            each(0, 4, lambda n: d_start(4 * d_tile(step + 7) + n))

        return c

    lax.fori_loop(0, 8, shuffle, 0)
    each(0, 4, lambda n: d_start(4 * d_tile(7) + n))
    dbuf[me] = moved[me]

    def q0(o, late):
        ref = gh0.at[cy, core, pl.ds(2 * abs(o - late), 2)]
        return remote(ref, ref, q0_send.at[2 * late + o], q0_recv.at[2 * late + o], plane(cy + 1 - 2 * o, cx, core))

    def q1(o, late):
        ref = gh1.at[cx, core, pl.ds(2 * abs(o - late), 2)]
        return remote(ref, ref, q1_send.at[2 * late + o], q1_recv.at[2 * late + o], plane(cy, cx + 1 - 2 * o, core))

    def r0(o):
        row = (cy + 3 + 2 * o) % 4
        part = pl.ds(2 * o, 2)
        ref = gh0.at[row, core, part]
        return remote(ref, ref, q0_send.at[4 + o], q0_recv.at[4 + o], plane(cy + 1 - 2 * o, cx, core))

    def r1(o):
        row = (cx + 3 + 2 * o) % 4
        part = pl.ds(2 * o, 2)
        ref = gh1.at[row, core, part]
        return remote(ref, ref, q1_send.at[4 + o], q1_recv.at[4 + o], plane(cy, cx + 1 - 2 * o, core))

    sibling = plane(cy, cx, 1 - core)

    def order(n):
        return n + n // 2 - 2 * (n // 3)

    def s0(n):
        ref = gh0.at[(cy + order(n)) % 4, core]
        return remote(ref, ref, s0_send.at[n], s0_recv.at[n], sibling)

    def s1(n):
        ref = gh1.at[(cx + order(n)) % 4, core]
        return remote(ref, ref, s1_send.at[n], s1_recv.at[n], sibling)

    own0.wait()
    each(1, 4, lambda o: p0(o).wait_recv())
    q0(0, 0).start()
    q0(1, 0).start()
    q0(0, 1).start()
    q0(1, 1).start()
    s0(0).start()
    own1.wait()
    each(1, 4, lambda o: p1(o).wait_recv())
    q1(0, 0).start()
    q1(1, 0).start()
    q1(0, 1).start()
    q1(1, 1).start()
    s1(0).start()

    @pl.loop(0, 8)
    def _(n):
        row = lax.broadcasted_iota(jnp.int32, (NJ * CAP, GROUP), 0)
        orbital = pair_ref[n, 0:1]
        which = pair_ref[n, 1:2]
        irrep, at = look(orbital)
        at = jnp.where(orbital >= 0, at + CAP * which, -1)
        ebuf[n] = jnp.where(row == at[:, :GROUP], 1.0, 0.0).astype(BF16)
        column_buf[n] = turn(jnp.bitwise_xor(irrep, pick(irr_j, which)))[:GROUP]

    def s_kia(n):
        good, irrep = own_label(n, 384)
        m = constant(n + 1, 384)
        irrep = jnp.bitwise_xor(irrep, pick([irr_i[i] for k in range(NK) for i in range(NI)], m))
        irrep = jnp.bitwise_xor(irrep, pick([occ_k[k] for k in range(NK) for i in range(NI)], m))
        return jnp.where(good, irrep, -2)

    high, low = halves(jnp.where(turn(s_kia(1)) == virt, a_ref[...], 0.0))
    direct = nt(p_all, high) + nt(p_all, low)
    orbital = constant(0, BLK * CPAD)
    irrep, at = look(orbital)
    p_t = onehot(jnp.where(orbital >= 0, at, -1))
    irrep_c = turn(jnp.where(orbital >= 0, irrep, -1))
    s_row = s_kia(3)
    good, s_ia = own_label(7, 128)
    s_ia = jnp.where(good, jnp.bitwise_xor(s_ia, pick(irr_i, constant(8, 128))), -2)
    s_ia_column = turn(s_ia)[:ROWS]
    offset = constant(9, 256)
    which = constant(10, 256)
    s_jb, at_z = look(mz * NB + offset)
    s_jb = jnp.where(offset >= 0, jnp.bitwise_xor(s_jb, pick(irr_j, which)), -1)
    at_z = jnp.where(offset >= 0, at_z + CAP * which, -1)

    def d_wait(n):
        d = (me + n) % BLK
        remote(moved.at[d], dbuf.at[d], d_send.at[d], d_recv.at[d], (d, mz)).wait_recv()

    each(1, BLK, d_wait)
    @pl.loop(0, BLK)
    def _(d):
        first = pl.multiple_of(d * CPAD, 8)
        for t in range(3):
            arrived[pl.ds(first, 16), t * 128:(t + 1) * 128] = dbuf[d, 16 * t:16 * t + 16]
        rest = dbuf[d, 48:56]
        arrived[pl.ds(first + 16, 8), 0:128] = rest
        arrived[pl.ds(first + 16, 8), 128:256] = jnp.concatenate([rest[3:6], rest[:5]], axis=0)
        top = dbuf[d, 32:40]
        below = jnp.concatenate([pltpu.roll(top, 86, 1)[3:6], top[:5]], axis=0)
        arrived[pl.ds(first + 16, 8), 256:384] = jnp.where(small[:8] < 2 * PITCH, pltpu.roll(top, 44, 1), below)

    swapped = jnp.where(irrep_c == s_row, arrived[...], 0.0)
    s_high, s_low = halves(swapped)
    s_t = nn(p_t, s_high) + nn(p_t, s_low)
    columns = []
    for k in range(NK):
        pairs = []
        for m in range(NI * k, NI * k + NI):
            first = 128 * (m // 6) + PITCH * (m % 6)
            pairs.append(2.0 * direct[:, m * CPAD:m * CPAD + NA] - s_t[:, first:first + NA])
        columns.append(jnp.concatenate(pairs, axis=1))
    w = jnp.concatenate(columns, axis=0)
    w = jnp.concatenate([w, jnp.zeros((NK * CAP, 128 - NI * NA), F32)], axis=1)
    w_high, w_low = halves(w)

    acc[...] = jnp.zeros_like(acc)

    def product(piece, n):
        g_high, g_low = halves(piece.reshape(GROUP, NK * CAP))
        r = nn(g_high, w_high) + (nn(g_high, w_low) + nn(g_low, w_high))
        r_high, r_low = halves(jnp.where(column_buf[n] == s_ia, r, 0.0))
        acc[...] += nn(ebuf[n], r_high) + nn(ebuf[n], r_low)

    def product0(n):
        s0(n).wait_recv()
        row = (cy + order(n)) % 4
        product(gh0[row], row)

    def product1(n):
        s1(n).wait_recv()
        row = (cx + order(n)) % 4
        product(gh1[row], 4 + row)

    for o in (1, 0):
        q0(o, 0).wait_recv()
        r0(o).start()
        q1(o, 0).wait_recv()
        r1(o).start()
    def products(n, c):
        @pl.when(n == 1)
        def _():
            for o in (1, 0):
                q0(o, 1).wait_recv()
                s0(2 - o).start()
                q1(o, 1).wait_recv()
                s1(2 - o).start()

        @pl.when(n == 3)
        def _():
            r0(0).wait_recv()
            r0(1).wait_recv()
            s0(3).start()
            r1(0).wait_recv()
            r1(1).wait_recv()
            s1(3).start()

        product0(n)
        product1(n)
        return c

    lax.fori_loop(0, 4, products, 0)

    def z_copy(n, half):
        target = (mz + n) % INT
        rows = pl.ds(8 * half, 8)
        sem = INT * half + n
        return remote(zsend.at[target, rows], zrecv.at[mz, rows], z_send.at[sem], z_recv.at[sem], (me, target))

    def y_copy(n, half):
        target = (mz + n) % INT
        rows = pl.ds(8 * half, 8)
        sem = INT * half + n
        return remote(ysum.at[rows], ygath.at[mz, rows], y_send.at[sem], y_recv.at[sem], (me, target))

    turned = acc[...].T[:ROWS]
    for block in range(3):
        for group in range(5):
            zsend[block * 5 + group] = turned[group * 16:(group + 1) * 16, block * 128:(block + 1) * 128]
    zsend[15] = jnp.zeros((16, 128), F32)

    for half in range(2):
        for n in FAR_FIRST:
            z_copy(n, half).start()
    zrecv[mz] = zsend[mz]
    for half in range(2):
        each(1, INT, lambda n: z_copy(n, half).wait_recv())
        rows = pl.ds(8 * half, 8)
        total = zrecv[0, rows]
        for n in range(1, INT):
            total = total + zrecv[n, rows]
        ysum[rows] = total
        for n in FAR_FIRST:
            y_copy(n, half).start()
        ygath[mz, rows] = total
    row = lax.broadcasted_iota(jnp.int32, (NJ * CAP, 256), 0)
    spread = jnp.where(row == at_z, 1.0, 0.0).astype(BF16)
    for half in range(2):
        each(1, INT, lambda n: y_copy(n, half).wait_recv())
    whole = jnp.concatenate(
        [jnp.concatenate([ygath[block * 5 + group] for group in range(5)], axis=0) for block in range(3)], axis=1
    )
    y_high, y_low = halves(whole)
    out = nn(y_high, spread) + nn(y_low, spread)
    out_ref[...] = jnp.where(s_ia_column == s_jb, out, 0.0)

    each(1, 4, lambda o: p0(o).wait_send())
    each(1, 4, lambda o: p1(o).wait_send())
    for o in range(2):
        q0(o, 0).wait_send()
        q0(o, 1).wait_send()
        q1(o, 0).wait_send()
        q1(o, 1).wait_send()
        r0(o).wait_send()
        r1(o).wait_send()
    for n in range(4):
        s0(n).wait_send()
        s1(n).wait_send()
    each(1, BLK, lambda n: d_copy((me + n) % BLK).wait_send())
    for half in range(2):
        each(1, INT, lambda n: z_copy(n, half).wait_send())
        each(1, INT, lambda n: y_copy(n, half).wait_send())


def pad_to(x, shape, value=0):
    return jnp.pad(x, [(0, n - m) for n, m in zip(shape, x.shape)], constant_values=value)


def index_tables():
    far = -100000
    table = np.full((16, BLK * CPAD), far, np.int32)
    lane = np.arange(BLK * CPAD)
    table[0] = np.where(lane % CPAD < NA, NA * (lane // CPAD) + lane % CPAD, -1)
    lane = np.arange(384)
    table[1, :384] = np.where(lane % CPAD < NA, lane % CPAD, far)
    table[2, :384] = lane // CPAD
    m = 6 * (lane // 128) + lane % 128 // PITCH
    a = lane % 128 % PITCH
    table[3, :384] = np.where((a < NA) & (lane % 128 < 6 * PITCH) & (m < NI * NK), a, far)
    table[4, :384] = m
    lane = np.arange(NA * NJ)
    table[5, :NA * NJ] = lane // NJ
    table[6, :NA * NJ] = lane % NJ
    table[7, :NI * NA] = lane % NA
    table[8, :NI * NA] = lane // NA
    lane = np.arange(NJ * NB)
    table[9, :NJ * NB] = lane % NB
    table[10, :NJ * NB] = lane // NB
    pairs = np.full((8, 2, 384), -1, np.int32)
    lane = np.arange(GROUP)
    core, other, row = lane // (4 * HALF), lane // HALF % 4, lane % HALF
    for n in range(8):
        y, x = (n, other) if n < 4 else (other, n - 4)
        n_row = row + HALF * (n // 4)
        good = n_row < NA * NJ
        pairs[n, 0, :GROUP] = np.where(good, ((y * 4 + x) * 2 + core) * NA + n_row // NJ, -1)
        pairs[n, 1, :GROUP] = n_row % NJ
    return table, pairs


def per_device(amplitudes, integrals, occ_irrep, virt_irrep, i_batch, j_batch):
    a_rows = pad_to(jnp.transpose(amplitudes, (2, 0, 1, 3)), (NK, NI, CPAD, NV)).reshape(NK * NI * CPAD, NV)
    ints = jnp.transpose(integrals, (0, 3, 2, 1))
    table, pairs = index_tables()

    vmem = pl.BlockSpec(memory_space=pltpu.VMEM)
    dma = pltpu.SemaphoreType.DMA
    out = pl.pallas_call(
        kernel,
        out_shape=jax.ShapeDtypeStruct((ROWS, 256), F32),
        in_specs=[vmem] * 5 + [pl.BlockSpec(memory_space=pltpu.SMEM)] * 3,
        out_specs=vmem,
        scratch_shapes=[
            pltpu.VMEM((ROWS, NK * CAP), F32),
            pltpu.VMEM((NK, ROWS, NV), F32),
            pltpu.VMEM((8, GROUP, 1), jnp.int32),
            pltpu.VMEM((4, 2, 4, HALF, NK * CAP), F32),
            pltpu.VMEM((4, 2, 4, HALF, NK * CAP), F32),
            pltpu.VMEM((NI * NK * CPAD, 1024), F32),
            pltpu.VMEM((BLK, 56, 128), F32),
            pltpu.VMEM((BLK, 56, 128), F32),
            pltpu.VMEM((BLK * CPAD, 384), F32),
            pltpu.VMEM((8, NJ * CAP, GROUP), BF16),
            pltpu.VMEM((NJ * CAP, 128), F32),
            pltpu.VMEM((INT, 16, 128), F32),
            pltpu.VMEM((INT, 16, 128), F32),
            pltpu.VMEM((16, 128), F32),
            pltpu.VMEM((INT, 16, 128), F32),
            dma((2,)), dma((4,)), dma((4,)), dma((4,)), dma((4,)), dma((6,)), dma((6,)), dma((6,)), dma((6,)),
            dma((4,)), dma((4,)), dma((4,)), dma((4,)), dma((BLK,)), dma((BLK,)),
            dma((2 * INT,)), dma((2 * INT,)), dma((2 * INT,)), dma((2 * INT,)),
        ],
        compiler_params=pltpu.CompilerParams(
            collective_id=0, has_side_effects=True, vmem_limit_bytes=48 * 1024 * 1024
        ),
    )(
        ints, a_rows, virt_irrep.reshape(1, NV), jnp.asarray(table), jnp.asarray(pairs), occ_irrep, i_batch, j_batch
    )
    return out[:NI * NA, :NJ * NB].reshape(NI, NA, NJ, NB)


def solution(mesh):
    placed = (P(None, "blk", "int", None), P("int", None, None, "blk"), P(), P(), P(), P())
    return jax.shard_map(
        per_device,
        mesh=mesh,
        in_specs=placed,
        out_specs=P(None, "blk", None, "int"),
        check_vma=False,
    )
```

```python
import jax
import jax.numpy as jnp
import numpy as np
from jax import lax
from jax.experimental import pallas as pl
from jax.experimental.pallas import tpu as pltpu
from jax.sharding import PartitionSpec as P

MESH = pl.DeviceIdType.MESH
F32 = jnp.float32
BF16 = jnp.bfloat16
CAP = 96
NI = 4
NJ = 4
NA = 19
NK = 4
NB = 38
NV = 608
BLK = 32
INT = 16
ROWS = 80
CPAD = 24
HALF = 40
GROUP = 320
FAR_FIRST = (8, 7, 9, 6, 10, 5, 11, 4, 12, 3, 13, 2, 14, 1, 15)
PITCH = 21


def halves(x):
    high = x.astype(BF16)
    return high, (x - high.astype(F32)).astype(BF16)


def nn(a, b):
    return jnp.dot(a, b, preferred_element_type=F32)


def nt(a, b):
    return lax.dot_general(a, b, (((1,), (1,)), ((), ())), preferred_element_type=F32)


def kernel(
    int_ref, a_ref, virt_ref, index_ref, pair_ref, occ_ref, i_ref, j_ref,
    out_ref,
    g_ref, g_rows, column_buf, gh0, gh1, spaced, moved, dbuf, arrived, ebuf, acc, zsend, zrecv, ysum, ygath,
    own_sem, p0_send, p0_recv, p1_send, p1_recv, q0_send, q0_recv, q1_send, q1_recv,
    s0_send, s0_recv, s1_send, s1_recv, d_send, d_recv, z_send, z_recv, y_send, y_recv,
):
    me = lax.axis_index("blk")
    mz = lax.axis_index("int")
    core = me % 2
    cx = (me // 2) % 4
    cy = me // 8

    def plane(y, x, c):
        return ((((y + 4) % 4) * 4 + (x + 4) % 4) * 2 + c, mz)

    def each(first, last, do):
        def body(n, c):
            do(n)
            return c

        lax.fori_loop(first, last, body, 0)

    def remote(src, dst, send, recv, device):
        return pltpu.make_async_remote_copy(
            src_ref=src, dst_ref=dst, send_sem=send, recv_sem=recv, device_id=device, device_id_type=MESH
        )

    barrier = pltpu.get_barrier_semaphore()

    def greet(device):
        pl.semaphore_signal(barrier, inc=1, device_id=device, device_id_type=MESH)

    each(1, INT, lambda n: greet((me, (mz + n) % INT)))
    each(1, BLK, lambda n: greet(((me + n) % BLK, mz)))

    own0 = pltpu.make_async_copy(g_ref.at[pl.ds(0, HALF)], gh0.at[cy, core, cx], own_sem.at[0])
    own1 = pltpu.make_async_copy(g_ref.at[pl.ds(HALF, HALF)], gh1.at[cx, core, cy], own_sem.at[1])

    irr_i = [occ_ref[i_ref[i]] for i in range(NI)]
    irr_j = [occ_ref[j_ref[j]] for j in range(NJ)]
    occ_k = [occ_ref[mz * NK + k] for k in range(NK)]
    virt = virt_ref[...]

    label = lax.broadcasted_iota(jnp.int32, (16, NV), 0)
    mine = jnp.where(label == virt, 1.0, 0.0)
    earlier = lax.broadcasted_iota(jnp.int32, (NV, NV), 0) < lax.broadcasted_iota(jnp.int32, (NV, NV), 1)
    counts = nn(mine.astype(BF16), jnp.where(earlier, 1.0, 0.0).astype(BF16))
    place = jnp.sum(mine * counts, axis=0, keepdims=True)
    both = jnp.where(label == 0, virt.astype(F32), jnp.where(label == 1, place, 0.0)).astype(BF16)

    def look(index):
        chosen = lax.broadcasted_iota(jnp.int32, (NV, index.shape[1]), 0) == index
        found = nn(both, jnp.where(chosen, 1.0, 0.0).astype(BF16))
        return found[0:1].astype(jnp.int32), found[1:2].astype(jnp.int32)

    def pick(values, which):
        out = jnp.zeros_like(which)
        for n, value in enumerate(values):
            out = jnp.where(which == n, value, out)
        return out

    def turn(row):
        return jnp.broadcast_to(row.astype(F32), (8, row.shape[1])).T[:, 0:1].astype(jnp.int32)

    def constant(n, lanes):
        return index_ref[n:n + 1, 0:lanes]

    def own_label(n, lanes):
        offset = constant(n, lanes)
        return offset >= 0, look(me * NA + offset)[0]

    def onehot(places):
        row = lax.broadcasted_iota(jnp.int32, (CAP, places.shape[1]), 0)
        return jnp.where(row == places, 1.0, 0.0).astype(BF16)

    p_all = onehot(place.astype(jnp.int32))
    valid, s_bj = own_label(5, 128)
    s_bj = jnp.bitwise_xor(s_bj, pick(irr_j, constant(6, 128)))
    for k in range(NK):
        for b in range(NA):
            g_rows[k, b * NJ:(b + 1) * NJ] = int_ref[k, b]
        g_rows[k, NA * NJ:] = jnp.zeros((ROWS - NA * NJ, NV), F32)
    packed = []
    for k in range(NK):
        high, low = halves(jnp.where(turn(jnp.where(valid, jnp.bitwise_xor(s_bj, occ_k[k]), -2))[:ROWS] == virt, g_rows[k], 0.0))
        packed.append(nt(high, p_all) + nt(low, p_all))
    g_ref[...] = jnp.concatenate(packed, axis=1)
    pl.semaphore_wait(barrier, BLK - 1 + INT - 1)

    own0.start()
    own1.start()

    def p0(o):
        return remote(g_ref.at[pl.ds(0, HALF)], gh0.at[cy, core, cx], p0_send.at[o], p0_recv.at[o], plane(cy, cx + o, core))

    def p1(o):
        return remote(g_ref.at[pl.ds(HALF, HALF)], gh1.at[cx, core, cy], p1_send.at[o], p1_recv.at[o], plane(cy + o, cx, core))

    each(1, 4, lambda o: p0(o).start())
    each(1, 4, lambda o: p1(o).start())

    a_high, a_low = halves(a_ref[...])
    for n in range(4):
        lane = lax.broadcasted_iota(jnp.int32, (1, 256), 1)
        source = jnp.where(lane % 32 < NA, NA * (8 * n + lane // 32) + lane % 32, -1)
        respace = jnp.where(lax.broadcasted_iota(jnp.int32, (NV, 256), 0) == source, 1.0, 0.0).astype(BF16)
        spaced[:, n * 256:(n + 1) * 256] = nn(a_high, respace) + nn(a_low, respace)

    def d_copy(d):
        return remote(moved.at[d], dbuf.at[me], d_send.at[d], d_recv.at[me], (d, mz))

    def d_start(d):
        @pl.when(d != me)
        def _():
            d_copy(d).start()

    def d_tile(step):
        return (me // 4 + step) % 8

    small = lax.broadcasted_iota(jnp.int32, (CPAD, 128), 1)

    def shuffle(step, c):
        tile = d_tile(step)
        at = pl.ds(pl.multiple_of(tile * 128, 128), 128)
        blocks = [spaced[m * CPAD:(m + 1) * CPAD, at] for m in range(NI * NK)]
        for part in range(4):
            d = 4 * tile + part
            lasts = []
            for t in range(3):
                held = jnp.zeros((CPAD, 128), F32)
                here = blocks[6 * t:6 * t + 6]
                for n, block in enumerate(here):
                    shift = (PITCH * n - 32 * part) % 128
                    turned = pltpu.roll(block, shift, 1) if shift else block
                    held = jnp.where((small >= PITCH * n) & (small < PITCH * n + NA), turned, held)
                last = held[16:]
                if t == 2:
                    packed_rows = jnp.concatenate([pltpu.roll(last, 84, 1)[:3], pltpu.roll(last, 42, 1)[:5]], axis=0)
                    top = jnp.where(small[:8] >= 84, packed_rows, held[:8])
                    moved[d, 32:40] = top
                    moved[d, 40:48] = held[8:16]
                else:
                    moved[d, 16 * t:16 * t + 16] = held[:16]
                    lasts.append(last)
            moved[d, 48:56] = jnp.concatenate([lasts[0][:3], lasts[1][:5]], axis=0)

        @pl.when(step > 0)
        def _():
            each(0, 4, lambda n: d_start(4 * d_tile(step + 7) + n))

        return c

    lax.fori_loop(0, 8, shuffle, 0)
    each(0, 4, lambda n: d_start(4 * d_tile(7) + n))
    dbuf[me] = moved[me]

    def q0(o, late):
        ref = gh0.at[cy, core, pl.ds(2 * abs(o - late), 2)]
        return remote(ref, ref, q0_send.at[2 * late + o], q0_recv.at[2 * late + o], plane(cy + 1 - 2 * o, cx, core))

    def q1(o, late):
        ref = gh1.at[cx, core, pl.ds(2 * abs(o - late), 2)]
        return remote(ref, ref, q1_send.at[2 * late + o], q1_recv.at[2 * late + o], plane(cy, cx + 1 - 2 * o, core))

    def r0(o):
        row = (cy + 3 + 2 * o) % 4
        part = pl.ds(2 * o, 2)
        ref = gh0.at[row, core, part]
        return remote(ref, ref, q0_send.at[4 + o], q0_recv.at[4 + o], plane(cy + 1 - 2 * o, cx, core))

    def r1(o):
        row = (cx + 3 + 2 * o) % 4
        part = pl.ds(2 * o, 2)
        ref = gh1.at[row, core, part]
        return remote(ref, ref, q1_send.at[4 + o], q1_recv.at[4 + o], plane(cy, cx + 1 - 2 * o, core))

    sibling = plane(cy, cx, 1 - core)

    def order(n):
        return n + n // 2 - 2 * (n // 3)

    def s0(n):
        ref = gh0.at[(cy + order(n)) % 4, core]
        return remote(ref, ref, s0_send.at[n], s0_recv.at[n], sibling)

    def s1(n):
        ref = gh1.at[(cx + order(n)) % 4, core]
        return remote(ref, ref, s1_send.at[n], s1_recv.at[n], sibling)

    own0.wait()
    each(1, 4, lambda o: p0(o).wait_recv())
    q0(0, 0).start()
    q0(1, 0).start()
    q0(0, 1).start()
    q0(1, 1).start()
    s0(0).start()
    own1.wait()
    each(1, 4, lambda o: p1(o).wait_recv())
    q1(0, 0).start()
    q1(1, 0).start()
    q1(0, 1).start()
    q1(1, 1).start()
    s1(0).start()

    @pl.loop(0, 8)
    def _(n):
        row = lax.broadcasted_iota(jnp.int32, (NJ * CAP, GROUP), 0)
        orbital = pair_ref[n, 0:1]
        which = pair_ref[n, 1:2]
        irrep, at = look(orbital)
        at = jnp.where(orbital >= 0, at + CAP * which, -1)
        ebuf[n] = jnp.where(row == at[:, :GROUP], 1.0, 0.0).astype(BF16)
        column_buf[n] = turn(jnp.bitwise_xor(irrep, pick(irr_j, which)))[:GROUP]

    def s_kia(n):
        good, irrep = own_label(n, 384)
        m = constant(n + 1, 384)
        irrep = jnp.bitwise_xor(irrep, pick([irr_i[i] for k in range(NK) for i in range(NI)], m))
        irrep = jnp.bitwise_xor(irrep, pick([occ_k[k] for k in range(NK) for i in range(NI)], m))
        return jnp.where(good, irrep, -2)

    high, low = halves(jnp.where(turn(s_kia(1)) == virt, a_ref[...], 0.0))
    direct = nt(p_all, high) + nt(p_all, low)
    orbital = constant(0, BLK * CPAD)
    irrep, at = look(orbital)
    p_t = onehot(jnp.where(orbital >= 0, at, -1))
    irrep_c = turn(jnp.where(orbital >= 0, irrep, -1))
    s_row = s_kia(3)
    good, s_ia = own_label(7, 128)
    s_ia = jnp.where(good, jnp.bitwise_xor(s_ia, pick(irr_i, constant(8, 128))), -2)
    s_ia_column = turn(s_ia)[:ROWS]
    offset = constant(9, 256)
    which = constant(10, 256)
    s_jb, at_z = look(mz * NB + offset)
    s_jb = jnp.where(offset >= 0, jnp.bitwise_xor(s_jb, pick(irr_j, which)), -1)
    at_z = jnp.where(offset >= 0, at_z + CAP * which, -1)

    def d_wait(n):
        d = (me + n) % BLK
        remote(moved.at[d], dbuf.at[d], d_send.at[d], d_recv.at[d], (d, mz)).wait_recv()

    each(1, BLK, d_wait)
    @pl.loop(0, BLK)
    def _(d):
        first = pl.multiple_of(d * CPAD, 8)
        for t in range(3):
            arrived[pl.ds(first, 16), t * 128:(t + 1) * 128] = dbuf[d, 16 * t:16 * t + 16]
        rest = dbuf[d, 48:56]
        arrived[pl.ds(first + 16, 8), 0:128] = rest
        arrived[pl.ds(first + 16, 8), 128:256] = jnp.concatenate([rest[3:6], rest[:5]], axis=0)
        top = dbuf[d, 32:40]
        below = jnp.concatenate([pltpu.roll(top, 86, 1)[3:6], top[:5]], axis=0)
        arrived[pl.ds(first + 16, 8), 256:384] = jnp.where(small[:8] < 2 * PITCH, pltpu.roll(top, 44, 1), below)

    swapped = jnp.where(irrep_c == s_row, arrived[...], 0.0)
    s_high, s_low = halves(swapped)
    s_t = nn(p_t, s_high) + nn(p_t, s_low)
    columns = []
    for k in range(NK):
        pairs = []
        for m in range(NI * k, NI * k + NI):
            first = 128 * (m // 6) + PITCH * (m % 6)
            pairs.append(2.0 * direct[:, m * CPAD:m * CPAD + NA] - s_t[:, first:first + NA])
        columns.append(jnp.concatenate(pairs, axis=1))
    w = jnp.concatenate(columns, axis=0)
    w = jnp.concatenate([w, jnp.zeros((NK * CAP, 128 - NI * NA), F32)], axis=1)
    w_high, w_low = halves(w)

    acc[...] = jnp.zeros_like(acc)

    def product(piece, n):
        g_high, g_low = halves(piece.reshape(GROUP, NK * CAP))
        r = nn(g_high, w_high) + (nn(g_high, w_low) + nn(g_low, w_high))
        r_high, r_low = halves(jnp.where(column_buf[n] == s_ia, r, 0.0))
        acc[...] += nn(ebuf[n], r_high) + nn(ebuf[n], r_low)

    def product0(n):
        s0(n).wait_recv()
        row = (cy + order(n)) % 4
        product(gh0[row], row)

    def product1(n):
        s1(n).wait_recv()
        row = (cx + order(n)) % 4
        product(gh1[row], 4 + row)

    for o in (1, 0):
        q0(o, 0).wait_recv()
        r0(o).start()
        q1(o, 0).wait_recv()
        r1(o).start()
    def products(n, c):
        @pl.when(n == 1)
        def _():
            q0(1, 1).wait_recv()
            s0(1).start()
            q1(1, 1).wait_recv()
            s1(1).start()

        @pl.when(n == 2)
        def _():
            q0(0, 1).wait_recv()
            s0(2).start()
            q1(0, 1).wait_recv()
            s1(2).start()

        @pl.when(n == 3)
        def _():
            r0(0).wait_recv()
            r0(1).wait_recv()
            s0(3).start()
            r1(0).wait_recv()
            r1(1).wait_recv()
            s1(3).start()

        product0(n)
        product1(n)
        return c

    lax.fori_loop(0, 4, products, 0)

    def z_copy(n, half):
        target = (mz + n) % INT
        rows = pl.ds(8 * half, 8)
        sem = INT * half + n
        return remote(zsend.at[target, rows], zrecv.at[mz, rows], z_send.at[sem], z_recv.at[sem], (me, target))

    def y_copy(n, half):
        target = (mz + n) % INT
        rows = pl.ds(8 * half, 8)
        sem = INT * half + n
        return remote(ysum.at[rows], ygath.at[mz, rows], y_send.at[sem], y_recv.at[sem], (me, target))

    turned = acc[...].T[:ROWS]
    for block in range(3):
        for group in range(5):
            zsend[block * 5 + group] = turned[group * 16:(group + 1) * 16, block * 128:(block + 1) * 128]
    zsend[15] = jnp.zeros((16, 128), F32)

    for half in range(2):
        for n in FAR_FIRST:
            z_copy(n, half).start()
    zrecv[mz] = zsend[mz]
    for half in range(2):
        each(1, INT, lambda n: z_copy(n, half).wait_recv())
        rows = pl.ds(8 * half, 8)
        total = zrecv[0, rows]
        for n in range(1, INT):
            total = total + zrecv[n, rows]
        ysum[rows] = total
        for n in FAR_FIRST:
            y_copy(n, half).start()
        ygath[mz, rows] = total
    row = lax.broadcasted_iota(jnp.int32, (NJ * CAP, 256), 0)
    spread = jnp.where(row == at_z, 1.0, 0.0).astype(BF16)
    for half in range(2):
        each(1, INT, lambda n: y_copy(n, half).wait_recv())
    whole = jnp.concatenate(
        [jnp.concatenate([ygath[block * 5 + group] for group in range(5)], axis=0) for block in range(3)], axis=1
    )
    y_high, y_low = halves(whole)
    out = nn(y_high, spread) + nn(y_low, spread)
    out_ref[...] = jnp.where(s_ia_column == s_jb, out, 0.0)

    each(1, 4, lambda o: p0(o).wait_send())
    each(1, 4, lambda o: p1(o).wait_send())
    for o in range(2):
        q0(o, 0).wait_send()
        q0(o, 1).wait_send()
        q1(o, 0).wait_send()
        q1(o, 1).wait_send()
        r0(o).wait_send()
        r1(o).wait_send()
    for n in range(4):
        s0(n).wait_send()
        s1(n).wait_send()
    each(1, BLK, lambda n: d_copy((me + n) % BLK).wait_send())
    for half in range(2):
        each(1, INT, lambda n: z_copy(n, half).wait_send())
        each(1, INT, lambda n: y_copy(n, half).wait_send())


def pad_to(x, shape, value=0):
    return jnp.pad(x, [(0, n - m) for n, m in zip(shape, x.shape)], constant_values=value)


def index_tables():
    far = -100000
    table = np.full((16, BLK * CPAD), far, np.int32)
    lane = np.arange(BLK * CPAD)
    table[0] = np.where(lane % CPAD < NA, NA * (lane // CPAD) + lane % CPAD, -1)
    lane = np.arange(384)
    table[1, :384] = np.where(lane % CPAD < NA, lane % CPAD, far)
    table[2, :384] = lane // CPAD
    m = 6 * (lane // 128) + lane % 128 // PITCH
    a = lane % 128 % PITCH
    table[3, :384] = np.where((a < NA) & (lane % 128 < 6 * PITCH) & (m < NI * NK), a, far)
    table[4, :384] = m
    lane = np.arange(NA * NJ)
    table[5, :NA * NJ] = lane // NJ
    table[6, :NA * NJ] = lane % NJ
    table[7, :NI * NA] = lane % NA
    table[8, :NI * NA] = lane // NA
    lane = np.arange(NJ * NB)
    table[9, :NJ * NB] = lane % NB
    table[10, :NJ * NB] = lane // NB
    pairs = np.full((8, 2, 384), -1, np.int32)
    lane = np.arange(GROUP)
    core, other, row = lane // (4 * HALF), lane // HALF % 4, lane % HALF
    for n in range(8):
        y, x = (n, other) if n < 4 else (other, n - 4)
        n_row = row + HALF * (n // 4)
        good = n_row < NA * NJ
        pairs[n, 0, :GROUP] = np.where(good, ((y * 4 + x) * 2 + core) * NA + n_row // NJ, -1)
        pairs[n, 1, :GROUP] = n_row % NJ
    return table, pairs


def per_device(amplitudes, integrals, occ_irrep, virt_irrep, i_batch, j_batch):
    a_rows = pad_to(jnp.transpose(amplitudes, (2, 0, 1, 3)), (NK, NI, CPAD, NV)).reshape(NK * NI * CPAD, NV)
    ints = jnp.transpose(integrals, (0, 3, 2, 1))
    table, pairs = index_tables()

    vmem = pl.BlockSpec(memory_space=pltpu.VMEM)
    dma = pltpu.SemaphoreType.DMA
    out = pl.pallas_call(
        kernel,
        out_shape=jax.ShapeDtypeStruct((ROWS, 256), F32),
        in_specs=[vmem] * 5 + [pl.BlockSpec(memory_space=pltpu.SMEM)] * 3,
        out_specs=vmem,
        scratch_shapes=[
            pltpu.VMEM((ROWS, NK * CAP), F32),
            pltpu.VMEM((NK, ROWS, NV), F32),
            pltpu.VMEM((8, GROUP, 1), jnp.int32),
            pltpu.VMEM((4, 2, 4, HALF, NK * CAP), F32),
            pltpu.VMEM((4, 2, 4, HALF, NK * CAP), F32),
            pltpu.VMEM((NI * NK * CPAD, 1024), F32),
            pltpu.VMEM((BLK, 56, 128), F32),
            pltpu.VMEM((BLK, 56, 128), F32),
            pltpu.VMEM((BLK * CPAD, 384), F32),
            pltpu.VMEM((8, NJ * CAP, GROUP), BF16),
            pltpu.VMEM((NJ * CAP, 128), F32),
            pltpu.VMEM((INT, 16, 128), F32),
            pltpu.VMEM((INT, 16, 128), F32),
            pltpu.VMEM((16, 128), F32),
            pltpu.VMEM((INT, 16, 128), F32),
            dma((2,)), dma((4,)), dma((4,)), dma((4,)), dma((4,)), dma((6,)), dma((6,)), dma((6,)), dma((6,)),
            dma((4,)), dma((4,)), dma((4,)), dma((4,)), dma((BLK,)), dma((BLK,)),
            dma((2 * INT,)), dma((2 * INT,)), dma((2 * INT,)), dma((2 * INT,)),
        ],
        compiler_params=pltpu.CompilerParams(
            collective_id=0, has_side_effects=True, vmem_limit_bytes=48 * 1024 * 1024
        ),
    )(
        ints, a_rows, virt_irrep.reshape(1, NV), jnp.asarray(table), jnp.asarray(pairs), occ_irrep, i_batch, j_batch
    )
    return out[:NI * NA, :NJ * NB].reshape(NI, NA, NJ, NB)


def solution(mesh):
    placed = (P(None, "blk", "int", None), P("int", None, None, "blk"), P(), P(), P(), P())
    return jax.shard_map(
        per_device,
        mesh=mesh,
        in_specs=placed,
        out_specs=P(None, "blk", None, "int"),
        check_vma=False,
    )
```
